32 devices in a mesh: seq: 8 (over z, core), fsdp: 4 (over y, x).
Axes of the slice: x: 2, y: 2, z: 4, core: 2. Of those that a mesh axis runs over, the one named last changes fastest.
Arguments:
- signal: bfloat16 [4, 8192, 1024], P('fsdp', 'seq'), may hold values from -6 to 6
- cotangent: bfloat16 [4, 8192, 1024], P('fsdp', 'seq'), may hold values from -6 to 6
- w_in: bfloat16 [1024, 1024], P('fsdp'), may hold values from -0.1875 to 0.1875
- w_conv: bfloat16 [2, 1024, 128], P(None, 'seq'), may hold values from -0.5 to 0.5
- w_out: bfloat16 [1024, 1024], P('fsdp'), may hold values from -0.1875 to 0.1875
- dilation: int32 [16], P('seq'), may hold values from 512 to 4095
- lengths: int32 [4], P('fsdp'), may hold values from 2048 to 8192, as said below
Outputs:
- grad_signal: bfloat16 [4, 8192, 1024], P('fsdp', 'seq')
- grad_in: float32 [1024, 1024], P('fsdp')
- grad_out: float32 [1024, 1024], P('fsdp')
- grad_conv: float32 [2, 1024, 128], P(None, 'seq')
The draws below stay inside these ranges and needn't reach their ends.
Inputs may be any that keep to these rules, and one draw needn't show every extreme that they name: `lengths`: some record in every draw holds all 8192 samples.
All inputs are finite; a program needn't handle non-finite values.
Results may differ from the reference program's by a relative error of at most 0.0068.
Values may be sent and summed in bfloat16 or wider, within the bound.
No kernel may reach another device: no remote copies, remote signals or barrier semaphores. Data moves between devices by JAX's collectives and lax.ppermute only.
A program may use at most 128 MiB of HBM per device.

```python
import math
import jax
import jax.numpy as jnp
from jax import lax

C = 1024
G = 16
CG = 64
T_DEV = 1024
L = 8192
RECS = 4


def draw_lengths(key, part):
    key_count, key_pick = jax.random.split(key)
    sampled = jax.random.randint(key_count, (RECS,), L // 4, L + 1, dtype=jnp.int32)
    chosen = jax.random.randint(key_pick, (), 0, RECS, dtype=jnp.int32)
    return jnp.where(jnp.arange(RECS, dtype=jnp.int32) == chosen, L, sampled).astype(jnp.int32)


def set_ends(values, rng, least, high):
    longest = values.shape.index(max(values.shape))
    spots = []
    for shift in (0, 1):
        where = [jax.random.randint(jax.random.fold_in(rng, axis), (), 0, length) for axis, length in enumerate(values.shape)]
        where[longest] = (where[longest] + shift) % values.shape[longest]
        spots.append(tuple(where))
    return values.at[spots[0]].set(least).at[spots[1]].set(high)


def levels(stream_key, shape, cuts, smallest, top_value):
    level = 1.0
    for dim, shards_of in cuts:
        draws = jax.random.uniform(jax.random.fold_in(jax.random.fold_in(stream_key, 6), dim), (shards_of,), jnp.float32, smallest / len(cuts), top_value / len(cuts))
        level = level * jnp.repeat(jnp.exp(draws), shape[dim] // shards_of).reshape((-1,) + (1,) * (len(shape) - 1 - dim))
    return level


def noise(key, shape, scale, limit, cuts=(), kind=jnp.bfloat16):
    loudness = levels(key, shape, cuts, -0.22, 0.18) if cuts else 1.0
    values = jax.random.normal(key, shape, jnp.float32) * scale * loudness
    return jnp.minimum(jnp.maximum(values, -limit), limit).astype(kind)


def setup_inputs(seed: int = 0) -> dict:
    seeds = jax.random.split(jax.random.key(seed), 8)
    return {
        "signal": noise(seeds[0], (RECS, L, C), 1.0, 6.0, ((0, 4), (1, 8))),
        "cotangent": noise(seeds[1], (RECS, L, C), 1.0, 6.0, ((0, 4), (1, 8))),
        "w_in": noise(seeds[2], (C, C), C ** -0.5, 0.1875, ((0, 4),)),
        "w_conv": noise(seeds[3], (2, C, 2 * CG), (2 * CG) ** -0.5, 0.5, ((1, 8),)),
        "w_out": noise(seeds[4], (C, C), C ** -0.5, 0.1875, ((0, 4),)),
        "dilation": set_ends(jax.random.randint(seeds[5], (G,), T_DEV // 2, 4 * T_DEV), jax.random.fold_in(seeds[5], 1), T_DEV // 2, (4 * T_DEV) - 1).astype(jnp.int32),
        "lengths": draw_lengths(jax.random.fold_in(seeds[7], 71), 0),
    }


def delayed(series, amount):
    padded = jnp.concatenate([jnp.zeros_like(series), series], axis=0)
    return lax.dynamic_slice_in_dim(padded, (series.shape[0] - amount).astype(jnp.int32), series.shape[0], 0)

def advanced(series, amount):
    padded = jnp.concatenate([series, jnp.zeros_like(series)], axis=0)
    return lax.dynamic_slice_in_dim(padded, amount.astype(jnp.int32), series.shape[0], 0)

def group_pass(projected, grad_gated, kernel, amount, live_mask):
    group_width = kernel.shape[0] // 2
    stacked = jnp.concatenate([projected, delayed(projected, amount)], axis=1)
    pre_acts = jnp.dot(stacked, kernel, preferred_element_type=jnp.float32)
    tanh_act = jnp.tanh(pre_acts[:, :group_width])
    sig_act = jax.nn.sigmoid(pre_acts[:, group_width:])
    masked = live_mask[:, None]
    gated_out = (tanh_act * sig_act * masked).astype(jnp.bfloat16)
    grad_masked = grad_gated.astype(jnp.float32) * masked
    grad_filter = grad_masked * sig_act * (1.0 - tanh_act * tanh_act)
    grad_gate = grad_masked * tanh_act * sig_act * (1.0 - sig_act)
    grad_acts = jnp.concatenate([grad_filter, grad_gate], axis=1).astype(jnp.bfloat16)
    grad_kernel = jnp.dot(stacked.T, grad_acts, preferred_element_type=jnp.float32)
    paired = jnp.concatenate([grad_acts, advanced(grad_acts, amount)], axis=1)
    back_kernel = jnp.concatenate([kernel[:group_width].T, kernel[group_width:].T], axis=0)
    grad_mixed = jnp.dot(paired, back_kernel, preferred_element_type=jnp.float32).astype(jnp.bfloat16)
    return (gated_out, grad_mixed, grad_kernel)

def reference(signal, cotangent, w_in, w_conv, w_out, dilation, lengths):
    records, full_len, channels = signal.shape
    groups = dilation.shape[0]
    group_width = channels // groups
    kernels = jnp.concatenate([w_conv[0].reshape(groups, group_width, 2 * group_width), w_conv[1].reshape(groups, group_width, 2 * group_width)], axis=1)
    moments = jnp.arange(full_len, dtype=jnp.int32)

    def per_record(totals, entry_rec):
        record, upstream, length = entry_rec
        projected = jnp.dot(record, w_in, preferred_element_type=jnp.float32).astype(jnp.bfloat16)
        grad_gated = jnp.dot(upstream, w_out.T, preferred_element_type=jnp.float32).astype(jnp.bfloat16)
        live_mask = (moments < length).astype(jnp.float32)
        proj_groups = projected.reshape(full_len, groups, group_width).transpose(1, 0, 2)
        grad_groups = grad_gated.reshape(full_len, groups, group_width).transpose(1, 0, 2)

        def one_group(element):
            return group_pass(element[0], element[1], element[2], element[3], live_mask)
        gated_all, mixed_all, kernel_all = lax.map(one_group, (proj_groups, grad_groups, kernels, dilation))
        gated_all = gated_all.transpose(1, 0, 2).reshape(full_len, channels)
        mixed_all = mixed_all.transpose(1, 0, 2).reshape(full_len, channels)
        grad_record = (upstream.astype(jnp.float32) + jnp.dot(mixed_all, w_in.T, preferred_element_type=jnp.float32)).astype(jnp.bfloat16)
        sum_in, sum_out, sum_conv = totals
        sum_in = sum_in + jnp.dot(record.T, mixed_all, preferred_element_type=jnp.float32)
        sum_out = sum_out + jnp.dot(gated_all.T, upstream, preferred_element_type=jnp.float32)
        sum_conv = sum_conv + kernel_all
        return ((sum_in, sum_out, sum_conv), grad_record)
    initial = (jnp.zeros((channels, channels), jnp.float32), jnp.zeros((channels, channels), jnp.float32), jnp.zeros((groups, 2 * group_width, 2 * group_width), jnp.float32))
    (sum_in, sum_out, sum_conv), grad_signal = lax.scan(per_record, initial, (signal, cotangent, lengths))
    factor = 1.0 / math.sqrt(records * full_len)
    grad_conv = jnp.stack([sum_conv[:, :group_width, :].reshape(channels, 2 * group_width), sum_conv[:, group_width:, :].reshape(channels, 2 * group_width)], axis=0) * factor
    return (grad_signal, sum_in * factor, sum_out * factor, grad_conv)
```

```python
import functools
import math

import jax
import jax.numpy as jnp
from jax import lax
from jax.experimental import pallas as pl
from jax.experimental.pallas import tpu as pltpu
from jax.sharding import PartitionSpec as P


MAX_DILATION = 4095
LANES = 128
BF = jnp.bfloat16
F32 = jnp.float32
VM = pl.BlockSpec(memory_space=pltpu.VMEM)
SM = pl.BlockSpec(memory_space=pltpu.SMEM)


def dot(a, b, ca, cb):
    return lax.dot_general(a, b, (((ca,), (cb,)), ((), ())), preferred_element_type=F32)


def call(body, outs, ins, scratch=(), flops=0, scalars=1, name=None):
    moved = sum(math.prod(x.shape) * x.dtype.itemsize for x in list(ins) + list(outs))
    return pl.pallas_call(
        body,
        out_shape=tuple(outs),
        in_specs=[SM] * scalars + [VM] * (len(ins) - scalars),
        out_specs=tuple([VM] * len(outs)),
        scratch_shapes=list(scratch),
        cost_estimate=pl.CostEstimate(flops=flops, bytes_accessed=moved, transcendentals=0),
        compiler_params=pltpu.CompilerParams(vmem_limit_bytes=60 * 1024 * 1024),
        name=name,
    )(*ins)


def shape(dims, kind):
    return jax.ShapeDtypeStruct(dims, kind)


def forward_body(parts, tile, save, meta, own, partner, *rest):
    weights, outs = rest[:parts], rest[parts:]
    me = meta[0]
    rows = weights[0].shape[0]
    panel = outs[-1]
    for k in range(parts):
        panel[pl.ds(pl.multiple_of((me ^ k) * rows, rows), rows), :] = weights[k][...]
    targets = outs[:-1]
    for source, slot in ((own, 0), (partner, 1)):

        def step(i, carry, source=source, slot=slot):
            at = pl.multiple_of(i * tile, tile)
            got = dot(source[pl.ds(at, tile), :], panel[...], 1, 0).astype(BF)
            for j, target in enumerate(targets):
                target[slot, pl.ds(at, tile), :] = got[:, j * LANES : (j + 1) * LANES]
            return carry

        lax.fori_loop(0, source.shape[0] // tile, step, 0)


def upstream_body(parts, tile, meta, own, partner, *rest):
    weights, outs = rest[:parts], rest[parts:]
    me = meta[0]
    rows = weights[0].shape[0]
    panel = outs[-1]
    targets = outs[:-1]
    for k in range(parts):
        panel[me ^ k] = weights[k][...]
    for source, slot in ((own, 0), (partner, 1)):

        def step(i, carry, source=source, slot=slot):
            at = pl.multiple_of(i * tile, tile)
            whole = panel[...].reshape(parts * rows, panel.shape[2])
            got = dot(source[pl.ds(at, tile), :], whole, 1, 1).astype(BF)
            for j, target in enumerate(targets):
                target[slot, pl.ds(at, tile), :] = got[:, j * LANES : (j + 1) * LANES]
            return carry

        lax.fori_loop(0, source.shape[0] // tile, step, 0)


def select_lanes(a, b):
    lane = lax.broadcasted_iota(jnp.int32, a.shape, 1)
    return jnp.where(lane < LANES // 2, a, b)


def conv_body(hops, tile, meta, *rest):
    sources, rest = rest[: hops + 1], rest[hops + 1 :]
    upstream, kernel, gated, tap_zero, tap_one, grad_kernel, series, total = rest
    half = sources[0].shape[1]
    core, alive = meta[2], meta[3]
    for n in range(hops + 1):
        for h in range(2):
            series[(2 * (hops - n) + h) * half : (2 * (hops - n) + h + 1) * half, :] = (
                sources[n][h ^ core].astype(F32)
            )
    total[...] = jnp.zeros_like(total)
    per_half = half // tile

    def step(i, carry):
        slot = (i // per_half) ^ core
        row = pl.multiple_of((i % per_half) * tile, tile)
        start = 2 * hops * half + i * tile
        late = select_lanes(
            series[pl.ds(start - meta[0], tile), :], series[pl.ds(start - meta[1], tile), :]
        ).astype(BF)
        stacked = jnp.concatenate([sources[0][slot, pl.ds(row, tile), :], late], axis=1)
        pre = dot(stacked, kernel[...], 1, 0)
        tanh_act = jnp.tanh(pre[:, :LANES])
        sig_act = jax.nn.sigmoid(pre[:, LANES:])
        moment = i * tile + lax.broadcasted_iota(jnp.int32, tanh_act.shape, 0)
        mask = (moment < alive).astype(F32)
        gated[slot, pl.ds(row, tile), :] = (tanh_act * sig_act * mask).astype(BF)
        masked = upstream[slot, pl.ds(row, tile), :].astype(F32) * mask
        grad_filter = masked * sig_act * (1.0 - tanh_act * tanh_act)
        grad_gate = masked * tanh_act * sig_act * (1.0 - sig_act)
        acts = jnp.concatenate([grad_filter.astype(BF), grad_gate.astype(BF)], axis=1)
        total[...] += dot(stacked, acts, 0, 0)
        back = dot(acts, kernel[...], 1, 1)
        tap_zero[slot, pl.ds(row, tile), :] = back[:, :LANES]
        tap_one[slot, pl.ds(row, tile), :] = back[:, LANES:].astype(BF)
        return carry

    lax.fori_loop(0, 2 * per_half, step, 0)
    width = LANES // 2
    for tap in range(2):
        for g in range(2):
            top = tap * LANES + g * width
            left = total[top : top + width, :LANES]
            right = total[top : top + width, LANES:]
            if g == 0:
                right = pltpu.roll(right, width, 1)
            else:
                left = pltpu.roll(left, width, 1)
            grad_kernel[tap, g * width : (g + 1) * width, :] = select_lanes(left, right).astype(BF)


def mixed_body(hops, tile, meta, tap_zero, *rest):
    sources, (own, partner, series) = rest[: hops + 1], rest[hops + 1 :]
    half = tap_zero.shape[1]
    core = meta[2]
    for n in range(hops + 1):
        for h in range(2):
            series[(2 * n + h) * half : (2 * n + h + 1) * half, :] = sources[n][h ^ core].astype(
                F32
            )
    for slot, target in ((0, own), (1, partner)):

        def step(i, carry, slot=slot, target=target):
            row = pl.multiple_of(i * tile, tile)
            start = (slot ^ core) * half + row
            early = select_lanes(
                series[pl.ds(start + meta[0], tile), :], series[pl.ds(start + meta[1], tile), :]
            )
            target[pl.ds(row, tile), :] = (tap_zero[slot, pl.ds(row, tile), :] + early).astype(BF)
            return carry

        lax.fori_loop(0, half // tile, step, 0)


def outer_body(chunks, parts, tile, by_rows, meta, *rest):
    lefts, rest = rest[: 2 * chunks], rest[2 * chunks :]
    rights, outs, total = rest[:2], rest[2:-1], rest[-1]
    me = meta[0]
    total[...] = jnp.zeros_like(total)
    for slot in range(2):

        def step(i, carry, slot=slot):
            at = pl.multiple_of(i * tile, tile)
            left = jnp.concatenate(
                [lefts[2 * j + slot][pl.ds(at, tile), :] for j in range(chunks)], axis=1
            )
            total[...] += dot(left, rights[slot][pl.ds(at, tile), :], 0, 0)
            return carry

        lax.fori_loop(0, rights[slot].shape[0] // tile, step, 0)
    rows, columns = outs[0].shape
    for k in range(parts):
        if by_rows:
            at = pl.multiple_of((me ^ k) * rows, rows)
            got = total[pl.ds(at, rows), :]
        else:
            at = pl.multiple_of((me ^ k) * columns, columns)
            got = total[:, pl.ds(at, columns)]
        outs[k][...] = got.astype(outs[k].dtype)


def tree(values):
    while len(values) > 1:
        values = [values[i] + values[i + 1] for i in range(0, len(values), 2)]
    return values[0]


def split_body(count, parts, meta, *rest):
    ins, outs, total = rest[:count], rest[count:-1], rest[-1]
    total[...] = tree([x[...].astype(F32) for x in ins])
    rows = outs[0].shape[0]
    for k in range(parts):
        at = pl.multiple_of((meta[1] ^ k) * rows, rows)
        outs[k][...] = total[pl.ds(at, rows), :].astype(outs[k].dtype)


def sum_body(count, *rest):
    rest[count][...] = tree([x[...].astype(F32) for x in rest[:count]]).astype(rest[count].dtype)


def local(signal, cotangent, w_in, w_conv, w_out, dilation, lengths):
    record, upstream = signal[0], cotangent[0]
    samples, channels = record.shape
    seq_size, fsdp_size = lax.axis_size("seq"), lax.axis_size("fsdp")
    chips = seq_size // 2
    seq_at, fsdp_at = lax.axis_index("seq"), lax.axis_index("fsdp")
    core, chip = seq_at % 2, seq_at // 2
    factor = 1.0 / math.sqrt(samples * seq_size * fsdp_size)
    block = 2 * samples
    hops = -(-MAX_DILATION // block)
    share = channels // 2
    piece = share // fsdp_size
    conv_chans = w_conv.shape[1]
    local_groups = dilation.shape[0]
    width = conv_chans // local_groups
    assert 2 * width == LANES and chips == fsdp_size and piece == conv_chans
    chunks = share // LANES
    per_half = max(chunks // 2, 1)

    def to_partner(x):
        return lax.ppermute(x, "seq", [(i, i ^ 1) for i in range(seq_size)])

    def over_fsdp(x, k):
        return lax.ppermute(x, "fsdp", [(i, i ^ k) for i in range(fsdp_size)])

    def over_chips(x, k):
        return lax.ppermute(x, "seq", [(i, i ^ (2 * k)) for i in range(seq_size)])

    def up(x, hop):
        return lax.ppermute(x, "seq", [(i, i + 2) for i in range(2 * (hop - 1), seq_size - 2)])

    def down(x, hop):
        return lax.ppermute(x, "seq", [(i + 2, i) for i in range(seq_size - 2 * hop)])

    in_share = lax.dynamic_index_in_dim(
        w_in.reshape(-1, fsdp_size, 2, piece), core, 2, keepdims=False
    ).reshape(-1, share)
    out_share = lax.dynamic_index_in_dim(
        w_out.reshape(2, piece, channels), core, 0, keepdims=False
    )
    in_parts = [in_share] + [over_fsdp(in_share, k) for k in range(1, fsdp_size)]
    out_parts = [out_share] + [over_fsdp(out_share, k) for k in range(1, fsdp_size)]
    record_far = to_partner(record)
    upstream_far = to_partner(upstream)
    conv_parts = [w_conv] + [over_chips(w_conv, k) for k in range(1, chips)]
    dil_parts = [dilation] + [over_chips(dilation, k) for k in range(1, chips)]
    stack = jnp.stack(conv_parts)
    dils = jnp.stack(dil_parts)
    order = [chip ^ k for k in range(chips)]
    taps = jnp.concatenate(
        [lax.dynamic_index_in_dim(stack, k, 0, keepdims=False) for k in order], axis=1
    )
    amounts = jnp.concatenate(
        [lax.dynamic_index_in_dim(dils, k, 0, keepdims=False) for k in order]
    )
    cells = taps.reshape(2, chunks, 2, width, 2, width)
    kernels = jnp.einsum(
        "tcgwhv,gk->ctgwhkv", cells, jnp.eye(2, dtype=BF), preferred_element_type=BF
    ).reshape(chunks, 2 * LANES, 2 * LANES)
    alive = lengths[0] - chip * block
    where = jnp.stack([fsdp_at, chip]).astype(jnp.int32)
    metas = [
        jnp.stack([amounts[2 * j], amounts[2 * j + 1], core, alive]).astype(jnp.int32)
        for j in range(chunks)
    ]

    series = shape((2, samples, LANES), BF)
    tile = min(512, samples)
    projected, panels = [], []
    for start in range(0, chunks, per_half):
        wide = per_half * LANES
        cut = [x[:, start * LANES : start * LANES + wide] for x in in_parts]
        got = call(
            functools.partial(forward_body, fsdp_size, tile, True),
            [series] * per_half + [shape((channels, wide), BF)],
            [where, record, record_far] + cut,
            flops=2 * block * channels * wide,
            name="project",
        )
        projected += got[:-1]
        panels.append(got[-1])
    grad_gated = call(
        functools.partial(upstream_body, fsdp_size, tile),
        [series] * chunks,
        [where, upstream, upstream_far] + out_parts,
        scratch=[pltpu.VMEM((fsdp_size, piece, channels), BF)],
        flops=2 * block * channels * share,
        name="gate_grad",
    )
    panels_far = [to_partner(x) for x in panels]

    tile = min(256, samples)
    gated, own_mixed, far_mixed, kernel_grads = [], [], [], []
    long = pltpu.VMEM((2 * (hops + 1) * samples, LANES), F32)
    for j in range(chunks):
        chain = [projected[j]]
        for hop in range(1, hops + 1):
            chain.append(up(chain[-1], hop))
        out, tap_zero, tap_one, grad_kernel = call(
            functools.partial(conv_body, hops, tile),
            [series, shape((2, samples, LANES), F32), series, shape((2, LANES, LANES), BF)],
            [metas[j]] + chain + [grad_gated[j], kernels[j]],
            scratch=[long, pltpu.VMEM((2 * LANES, 2 * LANES), F32)],
            flops=6 * block * 4 * LANES * LANES,
            name="conv",
        )
        gated.append(out)
        kernel_grads.append(grad_kernel)
        back = [tap_one]
        for hop in range(1, hops + 1):
            back.append(down(back[-1], hop))
        own, far = call(
            functools.partial(mixed_body, hops, tile),
            [shape((samples, LANES), BF)] * 2,
            [metas[j], tap_zero] + back,
            scratch=[long],
            name="mix",
        )
        own_mixed.append(own)
        far_mixed.append(far)

    def over_all(blocks):
        got = [blocks[0]] + [over_fsdp(blocks[k], k) for k in range(1, fsdp_size)]
        rows, columns = blocks[0].shape
        part = rows // chips
        cut = call(
            functools.partial(split_body, fsdp_size, chips),
            [shape((part, columns), F32)] + [shape((part, columns), BF)] * (chips - 1),
            [where] + got,
            scratch=[pltpu.VMEM((rows, columns), F32)],
            name="split",
        )
        got = [cut[0]] + [over_chips(cut[k], k) for k in range(1, chips)]
        (mine,) = call(
            functools.partial(sum_body, chips),
            [shape((part, columns), BF)],
            got,
            scalars=0,
            name="sum",
        )
        got = [mine] + [over_chips(mine, k) for k in range(1, chips)]
        return got, [to_partner(x) for x in got]

    def outer(lefts, rights, by_rows, tile):
        rows, columns = LANES * len(lefts) // 2, channels
        one = (piece, columns) if by_rows else (rows, columns // fsdp_size)
        return call(
            functools.partial(outer_body, len(lefts) // 2, fsdp_size, tile, by_rows),
            [shape(one, F32)] + [shape(one, BF)] * (fsdp_size - 1),
            [where] + lefts + list(rights),
            scratch=[pltpu.VMEM((rows, columns), F32)],
            flops=2 * block * rows * columns,
            name="outer",
        )

    tile = min(512, samples)
    gated_sides = [x[s] for x in gated for s in range(2)]
    out_sum = over_all(outer(gated_sides, (upstream, upstream_far), True, tile))
    in_sums = []
    for start in range(0, chunks, per_half):
        sides = []
        for j in range(start, start + per_half):
            sides += [own_mixed[j], far_mixed[j]]
        in_sums.append(over_all(outer(sides, (record, record_far), False, tile)))

    all_kernel = jnp.concatenate(kernel_grads, axis=1)
    cuts = [
        lax.dynamic_slice_in_dim(all_kernel, (chip ^ k) * conv_chans, conv_chans, 1)
        for k in range(chips)
    ]
    got = [cuts[0]] + [over_chips(cuts[k], k) for k in range(1, chips)]
    mine = tree([x.astype(F32) for x in got]).astype(BF)
    got = [mine] + [over_fsdp(mine, k) for k in range(1, fsdp_size)]
    grad_conv = tree([x.astype(F32) for x in got]) * factor

    mixed_in = [to_partner(x) for x in far_mixed]
    tile = min(256, samples)

    def signal_body(base, *rest):
        target = rest[-1]
        mixes, sides = rest[: 2 * chunks], rest[2 * chunks : -1]

        acc = base[...].astype(F32)
        for n in range(len(sides)):
            mix = jnp.concatenate(
                [mixes[n * per_half + j][...] for j in range(per_half)], axis=1
            )
            acc += dot(mix, sides[n][...], 1, 1)
        target[...] = acc.astype(BF)

    sides = panels + panels_far
    mixes = own_mixed + mixed_in
    grad_signal = pl.pallas_call(
        signal_body,
        grid=(samples // tile,),
        out_shape=shape((samples, channels), BF),
        in_specs=[pl.BlockSpec((tile, channels), lambda i: (i, 0))]
        + [pl.BlockSpec((tile, LANES), lambda i: (i, 0))] * len(mixes)
        + [pl.BlockSpec(x.shape, lambda i: (0, 0)) for x in sides],
        out_specs=pl.BlockSpec((tile, channels), lambda i: (i, 0)),
        cost_estimate=pl.CostEstimate(
            flops=2 * samples * channels * channels,
            bytes_accessed=8 * samples * channels,
            transcendentals=0,
        ),
        compiler_params=pltpu.CompilerParams(vmem_limit_bytes=60 * 1024 * 1024),
        name="signal",
    )(upstream, *mixes, *sides)

    def finish_body(meta, *rest):
        ins, (grad_in, grad_out, turned) = rest[: 2 * chips * 3], rest[2 * chips * 3 :]
        chip_at, core_at = meta[1], meta[2]
        part = ins[0].shape[0]
        for side in range(2):
            for k in range(chips):
                at = (side ^ core_at) * piece + (chip_at ^ k) * part
                grad_out[pl.ds(pl.multiple_of(at, 8), part), :] = (
                    ins[side * chips + k][...].astype(F32) * factor
                )
        rows = per_half * LANES
        part = rows // chips
        for n in range(2):
            for side in range(2):
                for k in range(chips):
                    at = n * rows + (chip_at ^ k) * part
                    turned[side ^ core_at, pl.ds(pl.multiple_of(at, 8), part), :] = (
                        ins[2 * chips * (n + 1) + side * chips + k][...].astype(F32) * factor
                    )
        for f in range(fsdp_size):
            both = jnp.concatenate(
                [turned[c, f * piece : (f + 1) * piece, :] for c in range(2)], axis=0
            )
            grad_in[:, 2 * f * piece : 2 * (f + 1) * piece] = both.T

    finals = []
    for near, far in [out_sum] + in_sums:
        finals += near + far
    own_rows = channels // fsdp_size
    grad_in, grad_out = call(
        finish_body,
        [shape((own_rows, channels), F32)] * 2,
        [jnp.stack([fsdp_at, chip, core]).astype(jnp.int32)] + finals,
        scratch=[pltpu.VMEM((2, share, own_rows), F32)],
        name="finish",
    )
    return (grad_signal[None], grad_in, grad_out, grad_conv)


def solution(mesh):
    placed = (
        P("fsdp", "seq", None),
        P("fsdp", "seq", None),
        P("fsdp", None),
        P(None, "seq", None),
        P("fsdp", None),
        P("seq"),
        P("fsdp"),
    )
    return jax.shard_map(
        local,
        mesh=mesh,
        in_specs=placed,
        out_specs=(P("fsdp", "seq", None), P("fsdp", None), P("fsdp", None), P(None, "seq", None)),
        check_vma=False,
    )
```

```python
import functools
import math

import jax
import jax.numpy as jnp
from jax import lax
from jax.experimental import pallas as pl
from jax.experimental.pallas import tpu as pltpu
from jax.sharding import PartitionSpec as P


MAX_DILATION = 4095
LANES = 128
BF = jnp.bfloat16
F32 = jnp.float32
VM = pl.BlockSpec(memory_space=pltpu.VMEM)
SM = pl.BlockSpec(memory_space=pltpu.SMEM)


def dot(a, b, ca, cb):
    return lax.dot_general(a, b, (((ca,), (cb,)), ((), ())), preferred_element_type=F32)


def call(body, outs, ins, scratch=(), flops=0, scalars=1, small=0):
    moved = sum(math.prod(x.shape) * x.dtype.itemsize for x in list(ins) + list(outs))
    return pl.pallas_call(
        body,
        out_shape=tuple(outs),
        in_specs=[SM] * scalars + [VM] * (len(ins) - scalars),
        out_specs=tuple([SM] * small + [VM] * (len(outs) - small)),
        scratch_shapes=list(scratch),
        cost_estimate=pl.CostEstimate(flops=flops, bytes_accessed=moved, transcendentals=0),
        compiler_params=pltpu.CompilerParams(vmem_limit_bytes=60 * 1024 * 1024),
    )(*ins)


def shape(dims, kind):
    return jax.ShapeDtypeStruct(dims, kind)


def forward_body(parts, tile, meta, own, partner, *rest):
    weights, outs = rest[:parts], rest[parts:]
    me = meta[0]
    rows = weights[0].shape[0]
    panel = outs[-1]
    for k in range(parts):
        panel[pl.ds(pl.multiple_of((me ^ k) * rows, rows), rows), :] = weights[k][...]
    targets = outs[:-1]
    for source, slot in ((own, 0), (partner, 1)):

        def step(i, carry, source=source, slot=slot):
            at = pl.multiple_of(i * tile, tile)
            got = dot(source[pl.ds(at, tile), :], panel[...], 1, 0).astype(BF)
            for j, target in enumerate(targets):
                target[slot, pl.ds(at, tile), :] = got[:, j * LANES : (j + 1) * LANES]
            return carry

        lax.fori_loop(0, source.shape[0] // tile, step, 0)


def upstream_body(parts, tile, meta, own, partner, *rest):
    weights, outs = rest[:parts], rest[parts:]
    me = meta[0]
    rows = weights[0].shape[0]
    panel = outs[-1]
    targets = outs[:-1]
    for k in range(parts):
        panel[me ^ k] = weights[k][...]
    for source, slot in ((own, 0), (partner, 1)):

        def step(i, carry, source=source, slot=slot):
            at = pl.multiple_of(i * tile, tile)
            whole = panel[...].reshape(parts * rows, panel.shape[2])
            got = dot(source[pl.ds(at, tile), :], whole, 1, 1).astype(BF)
            for j, target in enumerate(targets):
                target[slot, pl.ds(at, tile), :] = got[:, j * LANES : (j + 1) * LANES]
            return carry

        lax.fori_loop(0, source.shape[0] // tile, step, 0)


def select_lanes(a, b):
    lane = lax.broadcasted_iota(jnp.int32, a.shape, 1)
    return jnp.where(lane < LANES // 2, a, b)


def conv_body(hops, tile, pair, meta, amounts, *rest):
    sources, rest = rest[: hops + 1], rest[hops + 1 :]
    upstream, kernel, gated, tap_zero, tap_one, grad_kernel, series, total = rest
    half = sources[0].shape[1]
    core, alive = meta[2], meta[3]
    late_a, late_b = amounts[2 * pair], amounts[2 * pair + 1]
    for n in range(hops + 1):
        for h in range(2):
            series[(2 * (hops - n) + h) * half : (2 * (hops - n) + h + 1) * half, :] = (
                sources[n][h ^ core].astype(F32)
            )
    total[...] = jnp.zeros_like(total)
    per_half = half // tile

    def step(i, carry):
        slot = (i // per_half) ^ core
        row = pl.multiple_of((i % per_half) * tile, tile)
        start = 2 * hops * half + i * tile
        late = select_lanes(
            series[pl.ds(start - late_a, tile), :], series[pl.ds(start - late_b, tile), :]
        ).astype(BF)
        stacked = jnp.concatenate([sources[0][slot, pl.ds(row, tile), :], late], axis=1)
        pre = dot(stacked, kernel[...], 1, 0)
        tanh_act = jnp.tanh(pre[:, :LANES])
        sig_act = jax.nn.sigmoid(pre[:, LANES:])
        moment = i * tile + lax.broadcasted_iota(jnp.int32, tanh_act.shape, 0)
        mask = (moment < alive).astype(F32)
        gated[slot, pl.ds(row, tile), :] = (tanh_act * sig_act * mask).astype(BF)
        masked = upstream[slot, pl.ds(row, tile), :].astype(F32) * mask
        grad_filter = masked * sig_act * (1.0 - tanh_act * tanh_act)
        grad_gate = masked * tanh_act * sig_act * (1.0 - sig_act)
        acts = jnp.concatenate([grad_filter.astype(BF), grad_gate.astype(BF)], axis=1)
        total[...] += dot(stacked, acts, 0, 0)
        back = dot(acts, kernel[...], 1, 1)
        tap_zero[slot, pl.ds(row, tile), :] = back[:, :LANES]
        tap_one[slot, pl.ds(row, tile), :] = back[:, LANES:].astype(BF)
        return carry

    lax.fori_loop(0, 2 * per_half, step, 0)
    width = LANES // 2
    for tap in range(2):
        for g in range(2):
            top = tap * LANES + g * width
            left = total[top : top + width, :LANES]
            right = total[top : top + width, LANES:]
            if g == 0:
                right = pltpu.roll(right, width, 1)
            else:
                left = pltpu.roll(left, width, 1)
            grad_kernel[tap, g * width : (g + 1) * width, :] = select_lanes(left, right).astype(BF)


def mixed_body(hops, tile, pair, meta, amounts, tap_zero, *rest):
    sources, (own, partner, series) = rest[: hops + 1], rest[hops + 1 :]
    half = tap_zero.shape[1]
    core = meta[2]
    early_a, early_b = amounts[2 * pair], amounts[2 * pair + 1]
    for n in range(hops + 1):
        for h in range(2):
            series[(2 * n + h) * half : (2 * n + h + 1) * half, :] = sources[n][h ^ core].astype(
                F32
            )
    for slot, target in ((0, own), (1, partner)):

        def step(i, carry, slot=slot, target=target):
            row = pl.multiple_of(i * tile, tile)
            start = (slot ^ core) * half + row
            early = select_lanes(
                series[pl.ds(start + early_a, tile), :], series[pl.ds(start + early_b, tile), :]
            )
            target[pl.ds(row, tile), :] = (tap_zero[slot, pl.ds(row, tile), :] + early).astype(BF)
            return carry

        lax.fori_loop(0, half // tile, step, 0)


def outer_body(chunks, parts, tile, by_rows, split, meta, *rest):
    count = chunks * (2 if split else 1)
    lefts, rest = rest[:count], rest[count:]
    rights, outs, total = rest[:2], rest[2:-1], rest[-1]
    me = meta[0]
    total[...] = jnp.zeros_like(total)
    for slot in range(2):

        def step(i, carry, slot=slot):
            at = pl.multiple_of(i * tile, tile)
            if split:
                left = [lefts[2 * j + slot][pl.ds(at, tile), :] for j in range(chunks)]
            else:
                left = [lefts[j][slot, pl.ds(at, tile), :] for j in range(chunks)]
            left = jnp.concatenate(left, axis=1)
            if split and slot == 1:
                outs[parts][pl.ds(at, tile), :] = left
            total[...] += dot(left, rights[slot][pl.ds(at, tile), :], 0, 0)
            return carry

        lax.fori_loop(0, rights[slot].shape[0] // tile, step, 0)
    rows, columns = outs[0].shape
    for k in range(parts):
        if by_rows:
            at = pl.multiple_of((me ^ k) * rows, rows)
            got = total[pl.ds(at, rows), :]
        else:
            at = pl.multiple_of((me ^ k) * columns, columns)
            got = total[:, pl.ds(at, columns)]
        outs[k][...] = got.astype(outs[k].dtype)


def tree(values):
    while len(values) > 1:
        values = [values[i] + values[i + 1] for i in range(0, len(values), 2)]
    return values[0]


def split_body(count, parts, meta, *rest):
    ins, outs, total = rest[:count], rest[count:-1], rest[-1]
    total[...] = tree([x[...].astype(F32) for x in ins])
    rows = outs[0].shape[0]
    for k in range(parts):
        at = pl.multiple_of((meta[1] ^ k) * rows, rows)
        outs[k][...] = total[pl.ds(at, rows), :].astype(outs[k].dtype)


def sum_body(count, factor, *rest):
    got = tree([x[...].astype(F32) for x in rest[:count]])
    rest[count][...] = (got if factor is None else got * factor).astype(rest[count].dtype)


def pack_body(count, meta, *rest):
    for k in range(count):
        rest[count][meta[1] ^ k] = rest[k][...]


def share_body(parts, meta, whole, *outs):
    piece = whole.shape[1] // (2 * parts)
    each = parts // len(outs)
    for n, out in enumerate(outs):
        got = []
        for f in range(n * each, (n + 1) * each):
            both = whole[:, 2 * f * piece : 2 * (f + 1) * piece]
            got.append(jnp.where(meta[2] == 0, both[:, :piece], both[:, piece:]))
        out[...] = jnp.concatenate(got, axis=1)


def taps_body(chips, groups, meta, *rest):
    delays, blocks = rest[:chips], rest[chips : 2 * chips]
    amounts, outs = rest[2 * chips], rest[2 * chips + 1 :]
    width = LANES // 2
    for out in outs:
        out[...] = jnp.zeros_like(out)
    for k in range(chips):
        at = meta[1] ^ k
        for n in range(groups):
            group = at * groups + n
            amounts[group] = delays[k][n]
            for spot in range(2 * len(outs)):

                @pl.when(group == spot)
                def _(k=k, n=n, spot=spot):
                    out, g = outs[spot // 2], spot % 2
                    for tap in range(2):
                        top = tap * LANES + g * width
                        block = blocks[k][tap, n * width : (n + 1) * width, :].astype(F32)
                        lane = lax.broadcasted_iota(jnp.int32, block.shape, 1)
                        here = (lane < width) == (g == 0)
                        other = pltpu.roll(block, width, 1)
                        left, right = (block, other) if g == 0 else (other, block)
                        zero = jnp.zeros_like(block)
                        out[top : top + width, :LANES] = jnp.where(here, left, zero).astype(BF)
                        out[top : top + width, LANES:] = jnp.where(here, right, zero).astype(BF)


def pick_body(chips, count, meta, *rest):
    ins, outs, held = rest[:count], rest[count:-1], rest[-1]
    rows = outs[0].shape[1]
    each = LANES // rows
    for j in range(count):
        for n in range(each):
            held[j * each + n] = ins[j][:, n * rows : (n + 1) * rows, :]
    for k in range(chips):
        outs[k][...] = held[meta[1] ^ k]


def local_step(signal, cotangent, w_in, w_conv, w_out, dilation, lengths):
    record, upstream = signal[0], cotangent[0]
    samples, channels = record.shape
    seq_size, fsdp_size = lax.axis_size("seq"), lax.axis_size("fsdp")
    chips = seq_size // 2
    seq_at, fsdp_at = lax.axis_index("seq"), lax.axis_index("fsdp")
    core, chip = seq_at % 2, seq_at // 2
    factor = 1.0 / math.sqrt(samples * seq_size * fsdp_size)
    block = 2 * samples
    hops = -(-MAX_DILATION // block)
    share = channels // 2
    piece = share // fsdp_size
    conv_chans = w_conv.shape[1]
    local_groups = dilation.shape[0]
    width = conv_chans // local_groups
    assert 2 * width == LANES and chips == fsdp_size and piece == conv_chans
    chunks = share // LANES
    per_half = max(chunks // 2, 1)

    def to_partner(x):
        return lax.ppermute(x, "seq", [(i, i ^ 1) for i in range(seq_size)])

    def from_fsdp(blocks):
        got = [blocks[0]]
        for k in range(1, fsdp_size):
            pairs = [(i, i ^ k) for i in range(fsdp_size)]
            got.append(lax.ppermute(blocks[k], "fsdp", pairs))
        return got

    def from_chips(blocks):
        got = [blocks[0]]
        for k in range(1, chips):
            pairs = [(i, i ^ (2 * k)) for i in range(seq_size)]
            got.append(lax.ppermute(blocks[k], "seq", pairs))
        return got

    def up(x, hop):
        return lax.ppermute(x, "seq", [(i, i + 2) for i in range(2 * (hop - 1), seq_size - 2)])

    def down(x, hop):
        return lax.ppermute(x, "seq", [(i + 2, i) for i in range(seq_size - 2 * hop)])

    where = jnp.stack([fsdp_at, chip, core, lengths[0] - chip * block]).astype(jnp.int32)
    wide = per_half * LANES
    halves = range(0, chunks, per_half)
    in_shares = call(
        functools.partial(share_body, fsdp_size),
        [shape((w_in.shape[0], wide), BF)] * len(halves),
        [where, w_in],
    )
    out_share = lax.dynamic_index_in_dim(
        w_out.reshape(2, piece, channels), core, 0, keepdims=False
    )
    record_far = to_partner(record)
    in_parts = [from_fsdp([x] * fsdp_size) for x in in_shares]
    upstream_far = to_partner(upstream)
    out_parts = from_fsdp([out_share] * fsdp_size)
    delays = from_chips([dilation] * chips)
    conv_parts = from_chips([w_conv] * chips)
    taps = call(
        functools.partial(taps_body, chips, local_groups),
        [shape((2 * chunks,), jnp.int32)] + [shape((2 * LANES, 2 * LANES), BF)] * chunks,
        [where] + delays + conv_parts,
        scalars=1 + chips,
        small=1,
    )
    amounts, kernels = taps[0], taps[1:]

    series = shape((2, samples, LANES), BF)
    tile = min(512, samples)
    projected, panels = [], []
    for n in range(len(halves)):
        got = call(
            functools.partial(forward_body, fsdp_size, tile),
            [series] * per_half + [shape((channels, wide), BF)],
            [where, record, record_far] + in_parts[n],
            flops=2 * block * channels * wide,
        )
        projected += got[:-1]
        panels.append(got[-1])
    grad_gated = call(
        functools.partial(upstream_body, fsdp_size, tile),
        [series] * chunks,
        [where, upstream, upstream_far] + out_parts,
        scratch=[pltpu.VMEM((fsdp_size, piece, channels), BF)],
        flops=2 * block * channels * share,
    )
    panels_far = [to_partner(x) for x in panels]

    tile = min(256, samples)
    gated, own_mixed, far_mixed, kernel_grads = [], [], [], []
    long = pltpu.VMEM((2 * (hops + 1) * samples, LANES), F32)
    for j in range(chunks):
        chain = [projected[j]]
        for hop in range(1, hops + 1):
            chain.append(up(chain[-1], hop))
        out, tap_zero, tap_one, grad_kernel = call(
            functools.partial(conv_body, hops, tile, j),
            [series, shape((2, samples, LANES), F32), series, shape((2, LANES, LANES), BF)],
            [where, amounts] + chain + [grad_gated[j], kernels[j]],
            scratch=[long, pltpu.VMEM((2 * LANES, 2 * LANES), F32)],
            flops=6 * block * 4 * LANES * LANES,
            scalars=2,
        )
        gated.append(out)
        kernel_grads.append(grad_kernel)
        back = [tap_one]
        for hop in range(1, hops + 1):
            back.append(down(back[-1], hop))
        own, far = call(
            functools.partial(mixed_body, hops, tile, j),
            [shape((samples, LANES), BF)] * 2,
            [where, amounts, tap_zero] + back,
            scratch=[long],
            scalars=2,
        )
        own_mixed.append(own)
        far_mixed.append(far)

    def over_all(blocks):
        got = from_fsdp(blocks)
        rows, columns = blocks[0].shape
        part = rows // chips
        cut = call(
            functools.partial(split_body, fsdp_size, chips),
            [shape((part, columns), F32)] + [shape((part, columns), BF)] * (chips - 1),
            [where] + got,
            scratch=[pltpu.VMEM((rows, columns), F32)],
        )
        got = from_chips(cut)
        (mine,) = call(
            functools.partial(sum_body, chips, None), [shape((part, columns), BF)], got, scalars=0
        )
        got = from_chips([mine] * chips)
        (packed,) = call(
            functools.partial(pack_body, chips), [shape((chips, part, columns), BF)], [where] + got
        )
        return [packed, to_partner(packed)]

    def outer(lefts, rights, by_rows, split, tile):
        count = len(lefts) // 2 if split else len(lefts)
        rows, columns = LANES * count, channels
        one = (piece, columns) if by_rows else (rows, columns // fsdp_size)
        return call(
            functools.partial(outer_body, count, fsdp_size, tile, by_rows, split),
            [shape(one, F32)]
            + [shape(one, BF)] * (fsdp_size - 1)
            + ([shape((samples, rows), BF)] if split else []),
            [where] + lefts + list(rights),
            scratch=[pltpu.VMEM((rows, columns), F32)],
            flops=2 * block * rows * columns,
        )

    tile = min(512, samples)
    finals = over_all(outer(gated, (upstream, upstream_far), True, False, tile))
    mixed_in = []
    for start in halves:
        sides = []
        for j in range(start, start + per_half):
            sides += [own_mixed[j], far_mixed[j]]
        got = outer(sides, (record, record_far), False, True, tile)
        mixed_in.append(to_partner(got[-1]))
        finals += over_all(got[:fsdp_size])

    cuts = call(
        functools.partial(pick_body, chips, chunks),
        [shape((2, conv_chans, LANES), BF)] * chips,
        [where] + kernel_grads,
        scratch=[pltpu.VMEM((chips, 2, conv_chans, LANES), BF)],
    )
    got = from_chips(cuts)
    (mine,) = call(
        functools.partial(sum_body, chips, None),
        [shape((2, conv_chans, LANES), BF)],
        got,
        scalars=0,
    )
    got = from_fsdp([mine] * fsdp_size)
    (grad_conv,) = call(
        functools.partial(sum_body, fsdp_size, factor),
        [shape((2, conv_chans, LANES), F32)],
        got,
        scalars=0,
    )

    tile = min(256, samples)

    def signal_body(base, *rest):
        target = rest[-1]
        mixes, others, sides = rest[:chunks], rest[chunks : chunks + len(halves)], rest[
            chunks + len(halves) : -1
        ]
        acc = base[...].astype(F32)
        for n in range(len(halves)):
            mix = jnp.concatenate(
                [mixes[n * per_half + j][...] for j in range(per_half)], axis=1
            )
            acc += dot(mix, sides[n][...], 1, 1)
            acc += dot(others[n][...], sides[len(halves) + n][...], 1, 1)
        target[...] = acc.astype(BF)

    sides = panels + panels_far
    grad_signal = pl.pallas_call(
        signal_body,
        grid=(samples // tile,),
        out_shape=shape((samples, channels), BF),
        in_specs=[pl.BlockSpec((tile, channels), lambda i: (i, 0))]
        + [pl.BlockSpec((tile, LANES), lambda i: (i, 0))] * chunks
        + [pl.BlockSpec((tile, wide), lambda i: (i, 0))] * len(halves)
        + [pl.BlockSpec(x.shape, lambda i: (0, 0)) for x in sides],
        out_specs=pl.BlockSpec((tile, channels), lambda i: (i, 0)),
        cost_estimate=pl.CostEstimate(
            flops=2 * samples * channels * channels,
            bytes_accessed=8 * samples * channels,
            transcendentals=0,
        ),
        compiler_params=pltpu.CompilerParams(vmem_limit_bytes=60 * 1024 * 1024),
        name="signal",
    )(upstream, *own_mixed, *mixed_in, *sides)

    def finish_body(meta, *rest):
        ins, (grad_in, grad_out, turned) = rest[:-3], rest[-3:]
        core_at = meta[2]
        for side in range(2):
            whole = ins[side][...].astype(F32) * factor
            at = pl.multiple_of((side ^ core_at) * piece, piece)
            grad_out[pl.ds(at, piece), :] = whole.reshape(piece, channels)
            for n in range(len(halves)):
                whole = ins[2 * (n + 1) + side][...].astype(F32) * factor
                turned[side ^ core_at, n * wide : (n + 1) * wide, :] = whole.reshape(
                    wide, turned.shape[2]
                )
        for f in range(fsdp_size):
            both = jnp.concatenate(
                [turned[c, f * piece : (f + 1) * piece, :] for c in range(2)], axis=0
            )
            grad_in[:, 2 * f * piece : 2 * (f + 1) * piece] = both.T

    own_rows = channels // fsdp_size
    grad_in, grad_out = call(
        finish_body,
        [shape((own_rows, channels), F32)] * 2,
        [where] + finals,
        scratch=[pltpu.VMEM((2, share, own_rows), F32)],
    )
    return (grad_signal[None], grad_in, grad_out, grad_conv)


def solution(mesh):
    placed = (
        P("fsdp", "seq", None),
        P("fsdp", "seq", None),
        P("fsdp", None),
        P(None, "seq", None),
        P("fsdp", None),
        P("seq"),
        P("fsdp"),
    )
    return jax.shard_map(
        local_step,
        mesh=mesh,
        in_specs=placed,
        out_specs=(P("fsdp", "seq", None), P("fsdp", None), P("fsdp", None), P(None, "seq", None)),
        check_vma=False,
    )
```

```python
import functools
import math

import jax
import jax.numpy as jnp
from jax import lax
from jax.experimental import pallas as pl
from jax.experimental.pallas import tpu as pltpu
from jax.sharding import PartitionSpec as P


MAX_DILATION = 4095
LANES = 128
BF = jnp.bfloat16
F32 = jnp.float32
VM = pl.BlockSpec(memory_space=pltpu.VMEM)
SM = pl.BlockSpec(memory_space=pltpu.SMEM)


def dot(a, b, ca, cb):
    return lax.dot_general(a, b, (((ca,), (cb,)), ((), ())), preferred_element_type=F32)


def call(body, outs, ins, scratch=(), flops=0, scalars=1, small=0):
    moved = sum(math.prod(x.shape) * x.dtype.itemsize for x in list(ins) + list(outs))
    return pl.pallas_call(
        body,
        out_shape=tuple(outs),
        in_specs=[SM] * scalars + [VM] * (len(ins) - scalars),
        out_specs=tuple([SM] * small + [VM] * (len(outs) - small)),
        scratch_shapes=list(scratch),
        cost_estimate=pl.CostEstimate(flops=flops, bytes_accessed=moved, transcendentals=0),
        compiler_params=pltpu.CompilerParams(vmem_limit_bytes=60 * 1024 * 1024),
    )(*ins)


def shape(dims, kind):
    return jax.ShapeDtypeStruct(dims, kind)


def tiled(body, steps, outs, ins, scratch=(), flops=0):
    moved = sum(math.prod(x[0].shape) * x[0].dtype.itemsize for x in list(ins) + list(outs))
    return pl.pallas_call(
        body,
        grid=(steps,),
        out_shape=tuple(x[0] for x in outs),
        in_specs=[SM] + [pl.BlockSpec(x[1], x[2]) for x in ins[1:]],
        out_specs=tuple(pl.BlockSpec(x[1], x[2]) for x in outs),
        scratch_shapes=list(scratch),
        cost_estimate=pl.CostEstimate(flops=flops, bytes_accessed=moved, transcendentals=0),
        compiler_params=pltpu.CompilerParams(vmem_limit_bytes=60 * 1024 * 1024),
    )(*[x[0] for x in ins])


def fixed(x):
    return (x, x.shape, lambda i: (0,) * len(x.shape))


def forward_body(parts, steps, meta, own, partner, *rest):
    weights, outs = rest[:parts], rest[parts:]
    targets, panel = outs[:-1], outs[-1]
    rows = weights[0].shape[0]
    at = pl.program_id(0)

    @pl.when(at == 0)
    def _():
        for k in range(parts):
            start = pl.multiple_of((meta[0] ^ k) * rows, rows)
            panel[pl.ds(start, rows), :] = weights[k][...]

    def work(source):
        got = dot(source[...], panel[...], 1, 0).astype(BF)
        for j, target in enumerate(targets):
            target[0] = got[:, j * LANES : (j + 1) * LANES]

    pl.when(at < steps)(lambda: work(own))
    pl.when(at >= steps)(lambda: work(partner))


def upstream_body(parts, steps, meta, own, partner, *rest):
    weights, outs = rest[:parts], rest[parts:]
    targets, panel = outs[:-1], outs[-1]
    rows = weights[0].shape[0]
    at = pl.program_id(0)

    @pl.when(at == 0)
    def _():
        for k in range(parts):
            start = pl.multiple_of((meta[0] ^ k) * rows, rows)
            panel[pl.ds(start, rows), :] = weights[k][...]

    def work(source):
        got = dot(source[...], panel[...], 1, 1).astype(BF)
        for j, target in enumerate(targets):
            target[0] = got[:, j * LANES : (j + 1) * LANES]

    pl.when(at < steps)(lambda: work(own))
    pl.when(at >= steps)(lambda: work(partner))


def select_lanes(a, b):
    lane = lax.broadcasted_iota(jnp.int32, a.shape, 1)
    return jnp.where(lane < LANES // 2, a, b)


def conv_body(hops, tile, pair, meta, amounts, *rest):
    sources, rest = rest[: hops + 1], rest[hops + 1 :]
    upstream, kernel, gated, tap_zero, tap_one, grad_kernel, series, total = rest
    half = sources[0].shape[1]
    core, alive = meta[2], meta[3]
    late_a, late_b = amounts[2 * pair], amounts[2 * pair + 1]
    for n in range(hops + 1):
        for h in range(2):
            series[(2 * (hops - n) + h) * half : (2 * (hops - n) + h + 1) * half, :] = (
                sources[n][h ^ core].astype(F32)
            )
    total[...] = jnp.zeros_like(total)
    per_half = half // tile

    def step(i, carry):
        slot = (i // per_half) ^ core
        row = pl.multiple_of((i % per_half) * tile, tile)
        start = 2 * hops * half + i * tile
        late = select_lanes(
            series[pl.ds(start - late_a, tile), :], series[pl.ds(start - late_b, tile), :]
        ).astype(BF)
        stacked = jnp.concatenate([sources[0][slot, pl.ds(row, tile), :], late], axis=1)
        pre = dot(stacked, kernel[...], 1, 0)
        tanh_act = jnp.tanh(pre[:, :LANES])
        sig_act = jax.nn.sigmoid(pre[:, LANES:])
        moment = i * tile + lax.broadcasted_iota(jnp.int32, tanh_act.shape, 0)
        mask = (moment < alive).astype(F32)
        gated[slot, pl.ds(row, tile), :] = (tanh_act * sig_act * mask).astype(BF)
        masked = upstream[slot, pl.ds(row, tile), :].astype(F32) * mask
        grad_filter = masked * sig_act * (1.0 - tanh_act * tanh_act)
        grad_gate = masked * tanh_act * sig_act * (1.0 - sig_act)
        acts = jnp.concatenate([grad_filter.astype(BF), grad_gate.astype(BF)], axis=1)
        total[...] += dot(stacked, acts, 0, 0)
        back = dot(acts, kernel[...], 1, 1)
        tap_zero[slot, pl.ds(row, tile), :] = back[:, :LANES]
        tap_one[slot, pl.ds(row, tile), :] = back[:, LANES:].astype(BF)
        return carry

    lax.fori_loop(0, 2 * per_half, step, 0)
    width = LANES // 2
    for tap in range(2):
        for g in range(2):
            top = tap * LANES + g * width
            left = total[top : top + width, :LANES]
            right = total[top : top + width, LANES:]
            if g == 0:
                right = pltpu.roll(right, width, 1)
            else:
                left = pltpu.roll(left, width, 1)
            grad_kernel[tap, g * width : (g + 1) * width, :] = select_lanes(left, right).astype(BF)


def mixed_body(hops, tile, pair, meta, amounts, tap_zero, *rest):
    sources, (own, partner, series) = rest[: hops + 1], rest[hops + 1 :]
    half = tap_zero.shape[1]
    core = meta[2]
    early_a, early_b = amounts[2 * pair], amounts[2 * pair + 1]
    for n in range(hops + 1):
        for h in range(2):
            series[(2 * n + h) * half : (2 * n + h + 1) * half, :] = sources[n][h ^ core].astype(
                F32
            )
    for slot, target in ((0, own), (1, partner)):

        def step(i, carry, slot=slot, target=target):
            row = pl.multiple_of(i * tile, tile)
            start = (slot ^ core) * half + row
            early = select_lanes(
                series[pl.ds(start + early_a, tile), :], series[pl.ds(start + early_b, tile), :]
            )
            target[pl.ds(row, tile), :] = (tap_zero[slot, pl.ds(row, tile), :] + early).astype(BF)
            return carry

        lax.fori_loop(0, half // tile, step, 0)


def outer_body(chunks, parts, steps, by_rows, split, meta, *rest):
    count = chunks * (2 if split else 1)
    lefts, rest = rest[:count], rest[count:]
    rights, outs, total = rest[:2], rest[2:-1], rest[-1]
    at = pl.program_id(0)

    @pl.when(at == 0)
    def _():
        total[...] = jnp.zeros_like(total)

    def work(slot):
        if split:
            left = [lefts[2 * j + slot][...] for j in range(chunks)]
        else:
            left = [lefts[j][0] for j in range(chunks)]
        left = jnp.concatenate(left, axis=1)
        if split and slot == 1:
            outs[parts][...] = left
        total[...] += dot(left, rights[slot][...], 0, 0)

    pl.when(at < steps)(lambda: work(0))
    pl.when(at >= steps)(lambda: work(1))

    @pl.when(at == 2 * steps - 1)
    def _():
        rows, columns = outs[0].shape
        for k in range(parts):
            if by_rows:
                start = pl.multiple_of((meta[0] ^ k) * rows, rows)
                got = total[pl.ds(start, rows), :]
            else:
                start = pl.multiple_of((meta[0] ^ k) * columns, columns)
                got = total[:, pl.ds(start, columns)]
            outs[k][...] = got.astype(outs[k].dtype)


def tree(values):
    while len(values) > 1:
        values = [values[i] + values[i + 1] for i in range(0, len(values), 2)]
    return values[0]


def split_body(count, parts, meta, *rest):
    ins, outs, total = rest[:count], rest[count:-1], rest[-1]
    total[...] = tree([x[...].astype(F32) for x in ins])
    rows = outs[0].shape[0]
    for k in range(parts):
        at = pl.multiple_of((meta[1] ^ k) * rows, rows)
        outs[k][...] = total[pl.ds(at, rows), :].astype(outs[k].dtype)


def gather_body(count, chips, pairs, meta, *rest):
    first, second = rest[:count], rest[count : 2 * count]
    kernels, rest = rest[2 * count : 2 * count + pairs], rest[2 * count + pairs :]
    outs, (sum_one, sum_two, held) = rest[:-3], rest[-3:]
    sum_one[...] = tree([x[...].astype(F32) for x in first])
    sum_two[...] = tree([x[...].astype(F32) for x in second])
    width = sum_one.shape[1]
    one, two, taps = sum_one.shape[0] // chips, sum_two.shape[0] // chips, held.shape[2]
    for j in range(pairs):
        for n in range(LANES // taps):
            held[j * (LANES // taps) + n] = kernels[j][:, n * taps : (n + 1) * taps, :]
    for k in range(chips):
        at, kind = meta[1] ^ k, outs[k].dtype
        outs[k][:one, :] = sum_one[pl.ds(pl.multiple_of(at * one, 8), one), :].astype(kind)
        block = sum_two[pl.ds(pl.multiple_of(at * two, 8), two), :].astype(kind)
        top = one
        for n in range(block.shape[1] // width):
            outs[k][top : top + two, :] = block[:, n * width : (n + 1) * width]
            top += two
        for tap in range(2):
            column = (tap * LANES) % width
            row = top + (tap * LANES) // width * taps
            outs[k][row : row + taps, column : column + LANES] = held[at, tap].astype(kind)


def divide_body(count, *rest):
    got = tree([x[...].astype(F32) for x in rest[:count]]).astype(BF)
    rows = rest[count].shape[0]
    rest[count][...] = got[:rows, :]
    rest[count + 1][...] = got[rows:, :]


def sum_body(count, factor, *rest):
    got = tree([x[...].astype(F32) for x in rest[:count]])
    rest[count][...] = (got if factor is None else got * factor).astype(rest[count].dtype)


def pack_body(count, meta, *rest):
    for k in range(count):
        rest[count][meta[1] ^ k] = rest[k][...]


def share_body(parts, meta, whole, *outs):
    piece = whole.shape[1] // (2 * parts)
    each = parts // len(outs)
    for n, out in enumerate(outs):
        got = []
        for f in range(n * each, (n + 1) * each):
            both = whole[:, 2 * f * piece : 2 * (f + 1) * piece]
            got.append(jnp.where(meta[2] == 0, both[:, :piece], both[:, piece:]))
        out[...] = jnp.concatenate(got, axis=1)


def taps_body(chips, groups, meta, *rest):
    delays, blocks = rest[:chips], rest[chips : 2 * chips]
    amounts, outs = rest[2 * chips], rest[2 * chips + 1 :]
    width = LANES // 2
    for out in outs:
        out[...] = jnp.zeros_like(out)
    for k in range(chips):
        at = meta[1] ^ k
        for n in range(groups):
            group = at * groups + n
            amounts[group] = delays[k][n]
            for spot in range(2 * len(outs)):

                @pl.when(group == spot)
                def _(k=k, n=n, spot=spot):
                    out, g = outs[spot // 2], spot % 2
                    for tap in range(2):
                        top = tap * LANES + g * width
                        block = blocks[k][tap, n * width : (n + 1) * width, :].astype(F32)
                        lane = lax.broadcasted_iota(jnp.int32, block.shape, 1)
                        here = (lane < width) == (g == 0)
                        other = pltpu.roll(block, width, 1)
                        left, right = (block, other) if g == 0 else (other, block)
                        zero = jnp.zeros_like(block)
                        out[top : top + width, :LANES] = jnp.where(here, left, zero).astype(BF)
                        out[top : top + width, LANES:] = jnp.where(here, right, zero).astype(BF)


def local_step(signal, cotangent, w_in, w_conv, w_out, dilation, lengths):
    record, upstream = signal[0], cotangent[0]
    samples, channels = record.shape
    seq_size, fsdp_size = lax.axis_size("seq"), lax.axis_size("fsdp")
    chips = seq_size // 2
    seq_at, fsdp_at = lax.axis_index("seq"), lax.axis_index("fsdp")
    core, chip = seq_at % 2, seq_at // 2
    factor = 1.0 / math.sqrt(samples * seq_size * fsdp_size)
    block = 2 * samples
    hops = -(-MAX_DILATION // block)
    share = channels // 2
    piece = share // fsdp_size
    conv_chans = w_conv.shape[1]
    local_groups = dilation.shape[0]
    width = conv_chans // local_groups
    assert 2 * width == LANES and chips == fsdp_size and piece == conv_chans
    chunks = share // LANES
    per_half = max(chunks // 2, 1)

    def to_partner(x):
        return lax.ppermute(x, "seq", [(i, i ^ 1) for i in range(seq_size)])

    def from_fsdp(blocks):
        got = [blocks[0]]
        for k in range(1, fsdp_size):
            pairs = [(i, i ^ k) for i in range(fsdp_size)]
            got.append(lax.ppermute(blocks[k], "fsdp", pairs))
        return got

    def from_chips(blocks):
        got = [blocks[0]]
        for k in range(1, chips):
            pairs = [(i, i ^ (2 * k)) for i in range(seq_size)]
            got.append(lax.ppermute(blocks[k], "seq", pairs))
        return got

    def up(x, hop):
        return lax.ppermute(x, "seq", [(i, i + 2) for i in range(2 * (hop - 1), seq_size - 2)])

    def down(x, hop):
        return lax.ppermute(x, "seq", [(i + 2, i) for i in range(seq_size - 2 * hop)])

    where = jnp.stack([fsdp_at, chip, core, lengths[0] - chip * block]).astype(jnp.int32)
    wide = per_half * LANES
    halves = range(0, chunks, per_half)
    (in_share,) = call(
        functools.partial(share_body, fsdp_size), [shape((w_in.shape[0], share), BF)], [where, w_in]
    )
    out_share = lax.dynamic_index_in_dim(
        w_out.reshape(2, piece, channels), core, 0, keepdims=False
    )
    record_far = to_partner(record)
    in_parts = from_fsdp([in_share] * fsdp_size)
    upstream_far = to_partner(upstream)
    out_parts = from_fsdp([out_share] * fsdp_size)
    delays = from_chips([dilation] * chips)
    conv_parts = from_chips([w_conv] * chips)
    taps = call(
        functools.partial(taps_body, chips, local_groups),
        [shape((2 * chunks,), jnp.int32)] + [shape((2 * LANES, 2 * LANES), BF)] * chunks,
        [where] + delays + conv_parts,
        scalars=1 + chips,
        small=1,
    )
    amounts, kernels = taps[0], taps[1:]

    series = shape((2, samples, LANES), BF)
    tile = min(256, samples)
    steps = samples // tile

    def near(x):
        block_shape = (tile, x.shape[1])
        return (x, block_shape, lambda i: (jnp.minimum(i, steps - 1), 0))

    def far(x):
        block_shape = (tile, x.shape[1])
        return (x, block_shape, lambda i: (jnp.maximum(i - steps, 0), 0))

    def both(x):
        return (x, (1, tile, LANES), lambda i: (i // steps, i % steps, 0))

    got = tiled(
        functools.partial(forward_body, fsdp_size, steps),
        2 * steps,
        [both(series)] * chunks + [fixed(shape((channels, share), BF))],
        [(where,), near(record), far(record_far)] + [fixed(x) for x in in_parts],
        flops=2 * block * channels * share,
    )
    projected, panel = got[:-1], got[-1]
    grad_gated = tiled(
        functools.partial(upstream_body, fsdp_size, steps),
        2 * steps,
        [both(series)] * chunks,
        [(where,), near(upstream), far(upstream_far)] + [fixed(x) for x in out_parts],
        scratch=[pltpu.VMEM((share, channels), BF)],
        flops=2 * block * channels * share,
    )
    panel_far = to_partner(panel)

    tile = min(256, samples)
    gated, own_mixed, far_mixed, kernel_grads = [], [], [], []
    long = pltpu.VMEM((2 * (hops + 1) * samples, LANES), F32)
    for j in range(chunks):
        chain = [projected[j]]
        for hop in range(1, hops + 1):
            chain.append(up(chain[-1], hop))
        out, tap_zero, tap_one, grad_kernel = call(
            functools.partial(conv_body, hops, tile, j),
            [series, shape((2, samples, LANES), F32), series, shape((2, LANES, LANES), BF)],
            [where, amounts] + chain + [grad_gated[j], kernels[j]],
            scratch=[long, pltpu.VMEM((2 * LANES, 2 * LANES), F32)],
            flops=6 * block * 4 * LANES * LANES,
            scalars=2,
        )
        gated.append(out)
        kernel_grads.append(grad_kernel)
        back = [tap_one]
        for hop in range(1, hops + 1):
            back.append(down(back[-1], hop))
        own, other = call(
            functools.partial(mixed_body, hops, tile, j),
            [shape((samples, LANES), BF)] * 2,
            [where, amounts, tap_zero] + back,
            scratch=[long],
            scalars=2,
        )
        own_mixed.append(own)
        far_mixed.append(other)

    tile = min(256, samples)

    def outer(lefts, rights, by_rows, split):
        count = len(lefts) // 2 if split else len(lefts)
        rows, columns = LANES * count, channels
        one = (piece, columns) if by_rows else (rows, columns // fsdp_size)
        outs = [fixed(shape(one, F32))] + [fixed(shape(one, BF))] * (fsdp_size - 1)
        if split:
            outs.append(far(shape((samples, rows), BF)))
            lefts = [(near, far)[n % 2](x) for n, x in enumerate(lefts)]
        else:
            lefts = [both(x) for x in lefts]
        return tiled(
            functools.partial(outer_body, count, fsdp_size, steps, by_rows, split),
            2 * steps,
            outs,
            [(where,)] + lefts + [near(rights[0]), far(rights[1])],
            scratch=[pltpu.VMEM((rows, columns), F32)],
            flops=2 * block * rows * columns,
        )

    def finish_sum(mine):
        rows, columns = mine.shape
        got = from_chips([mine] * chips)
        (packed,) = call(
            functools.partial(pack_body, chips), [shape((chips, rows, columns), BF)], [where] + got
        )
        return [packed, to_partner(packed)]

    mixed_in, flats = [], []
    for start in halves:
        sides = []
        for j in range(start, start + per_half):
            sides += [own_mixed[j], far_mixed[j]]
        got = outer(sides, (record, record_far), False, True)
        mixed_in.append(to_partner(got[-1]))
        flats.append(from_fsdp(got[:fsdp_size]))
    got = outer(gated, (upstream, upstream_far), True, False)
    flat_out = from_fsdp(got)

    own_rows = channels // fsdp_size
    in_part, out_part = wide // chips, piece // chips
    panel_rows = in_part + out_part * (channels // own_rows)
    kernel_rows = 2 * LANES * conv_chans // own_rows
    whole = (panel_rows + kernel_rows, own_rows)
    cut = call(
        functools.partial(gather_body, fsdp_size, chips, chunks),
        [shape(whole, F32)] + [shape(whole, BF)] * (chips - 1),
        [where] + flats[0] + flat_out + kernel_grads,
        scratch=[
            pltpu.VMEM((wide, own_rows), F32),
            pltpu.VMEM((piece, channels), F32),
            pltpu.VMEM((chips, 2, conv_chans, LANES), BF),
        ],
    )
    mine, mine_kernel = call(
        functools.partial(divide_body, chips),
        [shape((panel_rows, own_rows), BF), shape((kernel_rows, own_rows), BF)],
        from_chips(cut),
        scalars=0,
    )
    kernel_parts = from_fsdp([mine_kernel] * fsdp_size)
    finals = finish_sum(mine)

    last = (wide // chips, own_rows)
    cut = call(
        functools.partial(split_body, fsdp_size, chips),
        [shape(last, F32)] + [shape(last, BF)] * (chips - 1),
        [where] + flats[1],
        scratch=[pltpu.VMEM((wide, own_rows), F32)],
    )
    (mine,) = call(
        functools.partial(sum_body, chips, None), [shape(last, BF)], from_chips(cut), scalars=0
    )
    finals += finish_sum(mine)

    tile = min(256, samples)

    def signal_body(base, *rest):
        mixes, others = rest[:chunks], rest[chunks : chunks + len(halves)]
        side, side_far, target = rest[-3:]
        mix = jnp.concatenate([x[...] for x in mixes], axis=1)
        other = jnp.concatenate([x[...] for x in others], axis=1)
        acc = base[...].astype(F32) + dot(mix, side[...], 1, 1)
        target[...] = (acc + dot(other, side_far[...], 1, 1)).astype(BF)

    grad_signal = pl.pallas_call(
        signal_body,
        grid=(samples // tile,),
        out_shape=shape((samples, channels), BF),
        in_specs=[pl.BlockSpec((tile, channels), lambda i: (i, 0))]
        + [pl.BlockSpec((tile, LANES), lambda i: (i, 0))] * chunks
        + [pl.BlockSpec((tile, wide), lambda i: (i, 0))] * len(halves)
        + [pl.BlockSpec(panel.shape, lambda i: (0, 0))] * 2,
        out_specs=pl.BlockSpec((tile, channels), lambda i: (i, 0)),
        cost_estimate=pl.CostEstimate(
            flops=2 * samples * channels * channels,
            bytes_accessed=8 * samples * channels,
            transcendentals=0,
        ),
        compiler_params=pltpu.CompilerParams(vmem_limit_bytes=60 * 1024 * 1024),
        name="signal",
    )(upstream, *own_mixed, *mixed_in, panel, panel_far)

    def finish_body(meta, *rest):
        packs, parts = rest[:4], rest[4 : 4 + fsdp_size]
        grad_in, grad_out, grad_conv, turned = rest[4 + fsdp_size :]
        core_at = meta[2]
        for side in range(2):
            first = packs[side][...].astype(F32) * factor
            second = packs[2 + side][...].astype(F32) * factor
            for p in range(chips):
                at = pl.multiple_of((side ^ core_at) * piece + p * out_part, 8)
                for n in range(channels // own_rows):
                    top = in_part + n * out_part
                    grad_out[pl.ds(at, out_part), n * own_rows : (n + 1) * own_rows] = first[
                        p, top : top + out_part, :
                    ]
                at = p * in_part
                turned[side ^ core_at, at : at + in_part, :] = first[p, :in_part, :]
                turned[side ^ core_at, wide + at : wide + at + in_part, :] = second[p]
        for f in range(fsdp_size):
            pair = [turned[c, f * piece : (f + 1) * piece, :] for c in range(2)]
            grad_in[:, 2 * f * piece : 2 * (f + 1) * piece] = jnp.concatenate(pair, axis=0).T
        total = tree([x[...].astype(F32) for x in parts]) * factor
        for tap in range(2):
            column = (tap * LANES) % own_rows
            row = (tap * LANES) // own_rows * conv_chans
            grad_conv[tap] = total[row : row + conv_chans, column : column + LANES]

    grad_in, grad_out, grad_conv = call(
        finish_body,
        [shape((own_rows, channels), F32)] * 2 + [shape((2, conv_chans, LANES), F32)],
        [where] + finals + kernel_parts,
        scratch=[pltpu.VMEM((2, share, own_rows), F32)],
    )
    return (grad_signal[None], grad_in, grad_out, grad_conv)


def solution(mesh):
    placed = (
        P("fsdp", "seq", None),
        P("fsdp", "seq", None),
        P("fsdp", None),
        P(None, "seq", None),
        P("fsdp", None),
        P("seq"),
        P("fsdp"),
    )
    return jax.shard_map(
        local_step,
        mesh=mesh,
        in_specs=placed,
        out_specs=(P("fsdp", "seq", None), P("fsdp", None), P("fsdp", None), P(None, "seq", None)),
        check_vma=False,
    )
```

```python
import functools
import math

import jax
import jax.numpy as jnp
from jax import lax
from jax.experimental import pallas as pl
from jax.experimental.pallas import tpu as pltpu
from jax.sharding import PartitionSpec as P


MAX_DILATION = 4095
LANES = 128
BF = jnp.bfloat16
F32 = jnp.float32
VM = pl.BlockSpec(memory_space=pltpu.VMEM)
SM = pl.BlockSpec(memory_space=pltpu.SMEM)


def dot(a, b, ca, cb):
    return lax.dot_general(a, b, (((ca,), (cb,)), ((), ())), preferred_element_type=F32)


def call(body, outs, ins, scratch=(), flops=0, scalars=1, small=0):
    moved = sum(math.prod(x.shape) * x.dtype.itemsize for x in list(ins) + list(outs))
    return pl.pallas_call(
        body,
        out_shape=tuple(outs),
        in_specs=[SM] * scalars + [VM] * (len(ins) - scalars),
        out_specs=tuple([SM] * small + [VM] * (len(outs) - small)),
        scratch_shapes=list(scratch),
        cost_estimate=pl.CostEstimate(flops=flops, bytes_accessed=moved, transcendentals=0),
        compiler_params=pltpu.CompilerParams(vmem_limit_bytes=20 * 1024 * 1024),
    )(*ins)


def shape(dims, kind):
    return jax.ShapeDtypeStruct(dims, kind)


def product_body(parts, tile, turned, meta, own, partner, *rest):
    weights, outs = rest[:parts], rest[parts:]
    targets, panel = outs[:-1], outs[-1]
    rows = weights[0].shape[0]
    for k in range(parts):
        start = pl.multiple_of((meta[0] ^ k) * rows, rows)
        panel[pl.ds(start, rows), :] = weights[k][...]
    for slot, source in enumerate((own, partner)):

        def step(i, carry, slot=slot, source=source):
            at = pl.multiple_of(i * tile, tile)
            got = dot(source[pl.ds(at, tile), :], panel[...], 1, int(turned)).astype(BF)
            for j, target in enumerate(targets):
                target[slot, pl.ds(at, tile), :] = got[:, j * LANES : (j + 1) * LANES]
            return carry

        lax.fori_loop(0, source.shape[0] // tile, step, 0)


def select_lanes(a, b):
    lane = lax.broadcasted_iota(jnp.int32, a.shape, 1)
    return jnp.where(lane < LANES // 2, a, b)


def conv_body(hops, tile, pair, meta, amounts, *rest):
    sources, rest = rest[: hops + 1], rest[hops + 1 :]
    upstream, kernel, gated, tap_zero, tap_one, grad_kernel, series, total = rest
    half = sources[0].shape[1]
    core, alive = meta[2], meta[3]
    late_a, late_b = amounts[2 * pair], amounts[2 * pair + 1]
    for n in range(hops + 1):
        for h in range(2):
            series[(2 * (hops - n) + h) * half : (2 * (hops - n) + h + 1) * half, :] = (
                sources[n][h ^ core].astype(F32)
            )
    total[...] = jnp.zeros_like(total)
    per_half = half // tile

    def step(i, carry):
        slot = (i // per_half) ^ core
        row = pl.multiple_of((i % per_half) * tile, tile)
        start = 2 * hops * half + i * tile
        late = select_lanes(
            series[pl.ds(start - late_a, tile), :], series[pl.ds(start - late_b, tile), :]
        ).astype(BF)
        stacked = jnp.concatenate([sources[0][slot, pl.ds(row, tile), :], late], axis=1)
        pre = dot(stacked, kernel[...], 1, 0)
        tanh_act = jnp.tanh(pre[:, :LANES])
        sig_act = jax.nn.sigmoid(pre[:, LANES:])
        moment = i * tile + lax.broadcasted_iota(jnp.int32, tanh_act.shape, 0)
        mask = (moment < alive).astype(F32)
        gated[slot, pl.ds(row, tile), :] = (tanh_act * sig_act * mask).astype(BF)
        masked = upstream[slot, pl.ds(row, tile), :].astype(F32) * mask
        grad_filter = masked * sig_act * (1.0 - tanh_act * tanh_act)
        grad_gate = masked * tanh_act * sig_act * (1.0 - sig_act)
        acts = jnp.concatenate([grad_filter.astype(BF), grad_gate.astype(BF)], axis=1)
        total[...] += dot(stacked, acts, 0, 0)
        back = dot(acts, kernel[...], 1, 1)
        tap_zero[slot, pl.ds(row, tile), :] = back[:, :LANES]
        tap_one[slot, pl.ds(row, tile), :] = back[:, LANES:].astype(BF)
        return carry

    lax.fori_loop(0, 2 * per_half, step, 0)
    width = LANES // 2
    for tap in range(2):
        for g in range(2):
            top = tap * LANES + g * width
            left = total[top : top + width, :LANES]
            right = total[top : top + width, LANES:]
            if g == 0:
                right = pltpu.roll(right, width, 1)
            else:
                left = pltpu.roll(left, width, 1)
            grad_kernel[tap, g * width : (g + 1) * width, :] = select_lanes(left, right).astype(BF)


def mixed_body(hops, tile, pair, meta, amounts, tap_zero, *rest):
    sources, (own, partner, series) = rest[: hops + 1], rest[hops + 1 :]
    half = tap_zero.shape[1]
    core = meta[2]
    early_a, early_b = amounts[2 * pair], amounts[2 * pair + 1]
    for n in range(hops + 1):
        for h in range(2):
            series[(2 * n + h) * half : (2 * n + h + 1) * half, :] = sources[n][h ^ core].astype(
                F32
            )
    for slot, target in ((0, own), (1, partner)):

        def step(i, carry, slot=slot, target=target):
            row = pl.multiple_of(i * tile, tile)
            start = (slot ^ core) * half + row
            early = select_lanes(
                series[pl.ds(start + early_a, tile), :], series[pl.ds(start + early_b, tile), :]
            )
            target[pl.ds(row, tile), :] = (tap_zero[slot, pl.ds(row, tile), :] + early).astype(BF)
            return carry

        lax.fori_loop(0, half // tile, step, 0)


def outer_body(chunks, parts, tile, by_rows, split, meta, *rest):
    count = chunks * (2 if split else 1)
    lefts, rest = rest[:count], rest[count:]
    rights, outs, total = rest[:2], rest[2:-1], rest[-1]
    total[...] = jnp.zeros_like(total)
    for slot in range(2):

        def step(i, carry, slot=slot):
            at = pl.multiple_of(i * tile, tile)
            if split:
                left = [lefts[2 * j + slot][pl.ds(at, tile), :] for j in range(chunks)]
            else:
                left = [lefts[j][slot, pl.ds(at, tile), :] for j in range(chunks)]
            left = jnp.concatenate(left, axis=1)
            if split and slot == 1:
                outs[parts][pl.ds(at, tile), :] = left
            total[...] += dot(left, rights[slot][pl.ds(at, tile), :], 0, 0)
            return carry

        lax.fori_loop(0, rights[slot].shape[0] // tile, step, 0)
    rows, columns = outs[0].shape
    for k in range(parts):
        if by_rows:
            start = pl.multiple_of((meta[0] ^ k) * rows, rows)
            got = total[pl.ds(start, rows), :]
        else:
            start = pl.multiple_of((meta[0] ^ k) * columns, columns)
            got = total[:, pl.ds(start, columns)]
        outs[k][...] = got.astype(outs[k].dtype)


def signal_body(tile, base, *rest):
    side, side_far, target = rest[-3:]
    count = (len(rest) - 3) // 3 * 2
    mixes, others = rest[:count], rest[count:-3]

    def step(i, carry):
        at = pl.multiple_of(i * tile, tile)
        mix = jnp.concatenate([x[pl.ds(at, tile), :] for x in mixes], axis=1)
        other = jnp.concatenate([x[pl.ds(at, tile), :] for x in others], axis=1)
        acc = base[pl.ds(at, tile), :].astype(F32) + dot(mix, side[...], 1, 1)
        target[pl.ds(at, tile), :] = (acc + dot(other, side_far[...], 1, 1)).astype(BF)
        return carry

    lax.fori_loop(0, base.shape[0] // tile, step, 0)


def tree(values):
    while len(values) > 1:
        values = [values[i] + values[i + 1] for i in range(0, len(values), 2)]
    return values[0]


def split_body(count, parts, meta, *rest):
    ins, outs, total = rest[:count], rest[count:-1], rest[-1]
    total[...] = tree([x[...].astype(F32) for x in ins])
    rows = outs[0].shape[0]
    for k in range(parts):
        at = pl.multiple_of((meta[1] ^ k) * rows, rows)
        outs[k][...] = total[pl.ds(at, rows), :].astype(outs[k].dtype)


def gather_body(count, chips, pairs, meta, *rest):
    first, second = rest[:count], rest[count : 2 * count]
    kernels, rest = rest[2 * count : 2 * count + pairs], rest[2 * count + pairs :]
    outs, (sum_one, sum_two, held) = rest[:-3], rest[-3:]
    sum_one[...] = tree([x[...].astype(F32) for x in first])
    sum_two[...] = tree([x[...].astype(F32) for x in second])
    width = sum_one.shape[1]
    one, two, taps = sum_one.shape[0] // chips, sum_two.shape[0] // chips, held.shape[2]
    for j in range(pairs):
        for n in range(LANES // taps):
            held[j * (LANES // taps) + n] = kernels[j][:, n * taps : (n + 1) * taps, :]
    for k in range(chips):
        at, kind = meta[1] ^ k, outs[k].dtype
        outs[k][:one, :] = sum_one[pl.ds(pl.multiple_of(at * one, 8), one), :].astype(kind)
        block = sum_two[pl.ds(pl.multiple_of(at * two, 8), two), :].astype(kind)
        top = one
        for n in range(block.shape[1] // width):
            outs[k][top : top + two, :] = block[:, n * width : (n + 1) * width]
            top += two
        for tap in range(2):
            column = (tap * LANES) % width
            row = top + (tap * LANES) // width * taps
            outs[k][row : row + taps, column : column + LANES] = held[at, tap].astype(kind)


def divide_body(count, *rest):
    got = tree([x[...].astype(F32) for x in rest[:count]]).astype(BF)
    rows = rest[count].shape[0]
    rest[count][...] = got[:rows, :]
    rest[count + 1][...] = got[rows:, :]


def sum_body(count, factor, *rest):
    got = tree([x[...].astype(F32) for x in rest[:count]])
    rest[count][...] = (got if factor is None else got * factor).astype(rest[count].dtype)


def pack_body(count, meta, *rest):
    for k in range(count):
        rest[count][meta[1] ^ k] = rest[k][...]


def share_body(parts, meta, whole, *outs):
    piece = whole.shape[1] // (2 * parts)
    each = parts // len(outs)
    for n, out in enumerate(outs):
        got = []
        for f in range(n * each, (n + 1) * each):
            both = whole[:, 2 * f * piece : 2 * (f + 1) * piece]
            got.append(jnp.where(meta[2] == 0, both[:, :piece], both[:, piece:]))
        out[...] = jnp.concatenate(got, axis=1)


def taps_body(chips, groups, meta, *rest):
    delays, blocks = rest[:chips], rest[chips : 2 * chips]
    amounts, outs = rest[2 * chips], rest[2 * chips + 1 :]
    width = LANES // 2
    for out in outs:
        out[...] = jnp.zeros_like(out)
    for k in range(chips):
        at = meta[1] ^ k
        for n in range(groups):
            group = at * groups + n
            amounts[group] = delays[k][n]
            for spot in range(2 * len(outs)):

                @pl.when(group == spot)
                def _(k=k, n=n, spot=spot):
                    out, g = outs[spot // 2], spot % 2
                    for tap in range(2):
                        top = tap * LANES + g * width
                        block = blocks[k][tap, n * width : (n + 1) * width, :].astype(F32)
                        lane = lax.broadcasted_iota(jnp.int32, block.shape, 1)
                        here = (lane < width) == (g == 0)
                        other = pltpu.roll(block, width, 1)
                        left, right = (block, other) if g == 0 else (other, block)
                        zero = jnp.zeros_like(block)
                        out[top : top + width, :LANES] = jnp.where(here, left, zero).astype(BF)
                        out[top : top + width, LANES:] = jnp.where(here, right, zero).astype(BF)


def local_step(signal, cotangent, w_in, w_conv, w_out, dilation, lengths):
    record, upstream = signal[0], cotangent[0]
    samples, channels = record.shape
    seq_size, fsdp_size = lax.axis_size("seq"), lax.axis_size("fsdp")
    chips = seq_size // 2
    seq_at, fsdp_at = lax.axis_index("seq"), lax.axis_index("fsdp")
    core, chip = seq_at % 2, seq_at // 2
    factor = 1.0 / math.sqrt(samples * seq_size * fsdp_size)
    block = 2 * samples
    hops = -(-MAX_DILATION // block)
    share = channels // 2
    piece = share // fsdp_size
    conv_chans = w_conv.shape[1]
    local_groups = dilation.shape[0]
    width = conv_chans // local_groups
    assert 2 * width == LANES and chips == fsdp_size and piece == conv_chans
    chunks = share // LANES
    per_half = max(chunks // 2, 1)

    def to_partner(x):
        return lax.ppermute(x, "seq", [(i, i ^ 1) for i in range(seq_size)])

    def from_fsdp(blocks):
        got = [blocks[0]]
        for k in range(1, fsdp_size):
            pairs = [(i, i ^ k) for i in range(fsdp_size)]
            got.append(lax.ppermute(blocks[k], "fsdp", pairs))
        return got

    def from_chips(blocks):
        got = [blocks[0]]
        for k in range(1, chips):
            pairs = [(i, i ^ (2 * k)) for i in range(seq_size)]
            got.append(lax.ppermute(blocks[k], "seq", pairs))
        return got

    def up(x, hop):
        return lax.ppermute(x, "seq", [(i, i + 2) for i in range(2 * (hop - 1), seq_size - 2)])

    def down(x, hop):
        return lax.ppermute(x, "seq", [(i + 2, i) for i in range(seq_size - 2 * hop)])

    where = jnp.stack([fsdp_at, chip, core, lengths[0] - chip * block]).astype(jnp.int32)
    wide = per_half * LANES
    halves = range(0, chunks, per_half)
    (in_share,) = call(
        functools.partial(share_body, fsdp_size), [shape((w_in.shape[0], share), BF)], [where, w_in]
    )
    out_share = lax.dynamic_index_in_dim(
        w_out.reshape(2, piece, channels), core, 0, keepdims=False
    )
    record_far = to_partner(record)
    in_parts = from_fsdp([in_share] * fsdp_size)
    upstream_far = to_partner(upstream)
    out_parts = from_fsdp([out_share] * fsdp_size)
    delays = from_chips([dilation] * chips)
    conv_parts = from_chips([w_conv] * chips)
    taps = call(
        functools.partial(taps_body, chips, local_groups),
        [shape((2 * chunks,), jnp.int32)] + [shape((2 * LANES, 2 * LANES), BF)] * chunks,
        [where] + delays + conv_parts,
        scalars=1 + chips,
        small=1,
    )
    amounts, kernels = taps[0], taps[1:]

    series = shape((2, samples, LANES), BF)
    tile = min(512, samples)
    got = call(
        functools.partial(product_body, fsdp_size, tile, False),
        [series] * chunks + [shape((channels, share), BF)],
        [where, record, record_far] + in_parts,
        flops=2 * block * channels * share,
    )
    projected, panel = got[:-1], got[-1]
    grad_gated = call(
        functools.partial(product_body, fsdp_size, tile, True),
        [series] * chunks,
        [where, upstream, upstream_far] + out_parts,
        scratch=[pltpu.VMEM((share, channels), BF)],
        flops=2 * block * channels * share,
    )
    panel_far = to_partner(panel)

    tile = min(256, samples)
    gated, own_mixed, far_mixed, kernel_grads = [], [], [], []
    long = pltpu.VMEM((2 * (hops + 1) * samples, LANES), F32)
    for j in range(chunks):
        chain = [projected[j]]
        for hop in range(1, hops + 1):
            chain.append(up(chain[-1], hop))
        out, tap_zero, tap_one, grad_kernel = call(
            functools.partial(conv_body, hops, tile, j),
            [series, shape((2, samples, LANES), F32), series, shape((2, LANES, LANES), BF)],
            [where, amounts] + chain + [grad_gated[j], kernels[j]],
            scratch=[long, pltpu.VMEM((2 * LANES, 2 * LANES), F32)],
            flops=6 * block * 4 * LANES * LANES,
            scalars=2,
        )
        gated.append(out)
        kernel_grads.append(grad_kernel)
        back = [tap_one]
        for hop in range(1, hops + 1):
            back.append(down(back[-1], hop))
        own, other = call(
            functools.partial(mixed_body, hops, tile, j),
            [shape((samples, LANES), BF)] * 2,
            [where, amounts, tap_zero] + back,
            scratch=[long],
            scalars=2,
        )
        own_mixed.append(own)
        far_mixed.append(other)

    tile = min(512, samples)

    def outer(lefts, rights, by_rows, split):
        count = len(lefts) // 2 if split else len(lefts)
        rows, columns = LANES * count, channels
        one = (piece, columns) if by_rows else (rows, columns // fsdp_size)
        return call(
            functools.partial(outer_body, count, fsdp_size, tile, by_rows, split),
            [shape(one, F32)]
            + [shape(one, BF)] * (fsdp_size - 1)
            + ([shape((samples, rows), BF)] if split else []),
            [where] + list(lefts) + list(rights),
            scratch=[pltpu.VMEM((rows, columns), F32)],
            flops=2 * block * rows * columns,
        )

    def finish_sum(mine):
        rows, columns = mine.shape
        got = from_chips([mine] * chips)
        (packed,) = call(
            functools.partial(pack_body, chips), [shape((chips, rows, columns), BF)], [where] + got
        )
        return [packed, to_partner(packed)]

    mixed_in, flats = [], []
    for start in halves:
        sides = []
        for j in range(start, start + per_half):
            sides += [own_mixed[j], far_mixed[j]]
        got = outer(sides, (record, record_far), False, True)
        mixed_in.append(to_partner(got[-1]))
        flats.append(from_fsdp(got[:fsdp_size]))
    got = outer(gated, (upstream, upstream_far), True, False)
    flat_out = from_fsdp(got)

    own_rows = channels // fsdp_size
    in_part, out_part = wide // chips, piece // chips
    panel_rows = in_part + out_part * (channels // own_rows)
    kernel_rows = 2 * LANES * conv_chans // own_rows
    whole = (panel_rows + kernel_rows, own_rows)
    cut = call(
        functools.partial(gather_body, fsdp_size, chips, chunks),
        [shape(whole, F32)] + [shape(whole, BF)] * (chips - 1),
        [where] + flats[0] + flat_out + kernel_grads,
        scratch=[
            pltpu.VMEM((wide, own_rows), F32),
            pltpu.VMEM((piece, channels), F32),
            pltpu.VMEM((chips, 2, conv_chans, LANES), BF),
        ],
    )
    mine, mine_kernel = call(
        functools.partial(divide_body, chips),
        [shape((panel_rows, own_rows), BF), shape((kernel_rows, own_rows), BF)],
        from_chips(cut),
        scalars=0,
    )
    kernel_parts = from_fsdp([mine_kernel] * fsdp_size)
    finals = finish_sum(mine)

    last = (wide // chips, own_rows)
    cut = call(
        functools.partial(split_body, fsdp_size, chips),
        [shape(last, F32)] + [shape(last, BF)] * (chips - 1),
        [where] + flats[1],
        scratch=[pltpu.VMEM((wide, own_rows), F32)],
    )
    (mine,) = call(
        functools.partial(sum_body, chips, None), [shape(last, BF)], from_chips(cut), scalars=0
    )
    finals += finish_sum(mine)

    tile = min(256, samples)

    (grad_signal,) = call(
        functools.partial(signal_body, tile),
        [shape((samples, channels), BF)],
        [upstream] + own_mixed + mixed_in + [panel, panel_far],
        scalars=0,
        flops=2 * samples * channels * channels,
    )

    def finish_body(meta, *rest):
        packs, parts = rest[:4], rest[4 : 4 + fsdp_size]
        grad_in, grad_out, grad_conv, turned = rest[4 + fsdp_size :]
        core_at = meta[2]
        for side in range(2):
            first = packs[side][...].astype(F32) * factor
            second = packs[2 + side][...].astype(F32) * factor
            for p in range(chips):
                at = pl.multiple_of((side ^ core_at) * piece + p * out_part, 8)
                for n in range(channels // own_rows):
                    top = in_part + n * out_part
                    grad_out[pl.ds(at, out_part), n * own_rows : (n + 1) * own_rows] = first[
                        p, top : top + out_part, :
                    ]
                at = p * in_part
                turned[side ^ core_at, at : at + in_part, :] = first[p, :in_part, :]
                turned[side ^ core_at, wide + at : wide + at + in_part, :] = second[p]
        for f in range(fsdp_size):
            pair = [turned[c, f * piece : (f + 1) * piece, :] for c in range(2)]
            grad_in[:, 2 * f * piece : 2 * (f + 1) * piece] = jnp.concatenate(pair, axis=0).T
        total = tree([x[...].astype(F32) for x in parts]) * factor
        for tap in range(2):
            column = (tap * LANES) % own_rows
            row = (tap * LANES) // own_rows * conv_chans
            grad_conv[tap] = total[row : row + conv_chans, column : column + LANES]

    grad_in, grad_out, grad_conv = call(
        finish_body,
        [shape((own_rows, channels), F32)] * 2 + [shape((2, conv_chans, LANES), F32)],
        [where] + finals + kernel_parts,
        scratch=[pltpu.VMEM((2, share, own_rows), F32)],
    )
    return (grad_signal[None], grad_in, grad_out, grad_conv)


def solution(mesh):
    placed = (
        P("fsdp", "seq", None),
        P("fsdp", "seq", None),
        P("fsdp", None),
        P(None, "seq", None),
        P("fsdp", None),
        P("seq"),
        P("fsdp"),
    )
    return jax.shard_map(
        local_step,
        mesh=mesh,
        in_specs=placed,
        out_specs=(P("fsdp", "seq", None), P("fsdp", None), P("fsdp", None), P(None, "seq", None)),
        check_vma=False,
    )
```

```python
import functools
import math

import jax
import jax.numpy as jnp
from jax import lax
from jax.experimental import pallas as pl
from jax.experimental.pallas import tpu as pltpu
from jax.sharding import PartitionSpec as P


MAX_DILATION = 4095
LANES = 128
BF = jnp.bfloat16
F32 = jnp.float32
VM = pl.BlockSpec(memory_space=pltpu.VMEM)
SM = pl.BlockSpec(memory_space=pltpu.SMEM)


def dot(a, b, ca, cb):
    return lax.dot_general(a, b, (((ca,), (cb,)), ((), ())), preferred_element_type=F32)


def call(body, outs, ins, scratch=(), flops=0, scalars=1, small=0):
    moved = sum(math.prod(x.shape) * x.dtype.itemsize for x in list(ins) + list(outs))
    return pl.pallas_call(
        body,
        out_shape=tuple(outs),
        in_specs=[SM] * scalars + [VM] * (len(ins) - scalars),
        out_specs=tuple([SM] * small + [VM] * (len(outs) - small)),
        scratch_shapes=list(scratch),
        cost_estimate=pl.CostEstimate(flops=flops, bytes_accessed=moved, transcendentals=0),
        compiler_params=pltpu.CompilerParams(vmem_limit_bytes=20 * 1024 * 1024),
    )(*ins)


def shape(dims, kind):
    return jax.ShapeDtypeStruct(dims, kind)


def product_body(parts, tile, turned, skip, meta, own, partner, *rest):
    weights, outs = rest[:parts], rest[parts:]
    if skip:
        outs[-1][:, :skip] = outs[0][...]
        outs = outs[1:]
    targets, panel = outs[:-1], outs[-1]
    rows = weights[0].shape[0]
    for k in range(parts):
        start = pl.multiple_of((meta[0] ^ k) * rows, rows)
        panel[pl.ds(start, rows), skip:] = weights[k][...]
    for slot, source in enumerate((own, partner)):

        def step(i, carry, slot=slot, source=source):
            at = pl.multiple_of(i * tile, tile)
            side = panel[:, skip:]
            got = dot(source[pl.ds(at, tile), :], side, 1, int(turned)).astype(BF)
            for j, target in enumerate(targets):
                target[slot, pl.ds(at, tile), :] = got[:, j * LANES : (j + 1) * LANES]
            return carry

        lax.fori_loop(0, source.shape[0] // tile, step, 0)


def select_lanes(a, b):
    lane = lax.broadcasted_iota(jnp.int32, a.shape, 1)
    return jnp.where(lane < LANES // 2, a, b)


def conv_body(hops, tile, pair, meta, amounts, *rest):
    sources, rest = rest[: hops + 1], rest[hops + 1 :]
    upstream, kernel, gated, tap_zero, tap_one, grad_kernel, series, total = rest
    half = sources[0].shape[1]
    core, alive = meta[2], meta[3]
    late_a, late_b = amounts[2 * pair], amounts[2 * pair + 1]
    for n in range(hops + 1):
        for h in range(2):
            series[(2 * (hops - n) + h) * half : (2 * (hops - n) + h + 1) * half, :] = (
                sources[n][h ^ core].astype(F32)
            )
    total[...] = jnp.zeros_like(total)
    per_half = half // tile

    def step(i, carry):
        slot = (i // per_half) ^ core
        row = pl.multiple_of((i % per_half) * tile, tile)
        start = 2 * hops * half + i * tile
        late = select_lanes(
            series[pl.ds(start - late_a, tile), :], series[pl.ds(start - late_b, tile), :]
        ).astype(BF)
        stacked = jnp.concatenate([sources[0][slot, pl.ds(row, tile), :], late], axis=1)
        pre = dot(stacked, kernel[...], 1, 0)
        tanh_act = jnp.tanh(pre[:, :LANES])
        sig_act = jax.nn.sigmoid(pre[:, LANES:])
        moment = i * tile + lax.broadcasted_iota(jnp.int32, tanh_act.shape, 0)
        mask = (moment < alive).astype(F32)
        gated[slot, pl.ds(row, tile), :] = (tanh_act * sig_act * mask).astype(BF)
        masked = upstream[slot, pl.ds(row, tile), :].astype(F32) * mask
        grad_filter = masked * sig_act * (1.0 - tanh_act * tanh_act)
        grad_gate = masked * tanh_act * sig_act * (1.0 - sig_act)
        acts = jnp.concatenate([grad_filter.astype(BF), grad_gate.astype(BF)], axis=1)
        total[...] += dot(stacked, acts, 0, 0)
        back = dot(acts, kernel[...], 1, 1)
        tap_zero[slot, pl.ds(row, tile), :] = back[:, :LANES]
        tap_one[slot, pl.ds(row, tile), :] = back[:, LANES:].astype(BF)
        return carry

    lax.fori_loop(0, 2 * per_half, step, 0)
    width = LANES // 2
    for tap in range(2):
        for g in range(2):
            top = tap * LANES + g * width
            left = total[top : top + width, :LANES]
            right = total[top : top + width, LANES:]
            if g == 0:
                right = pltpu.roll(right, width, 1)
            else:
                left = pltpu.roll(left, width, 1)
            grad_kernel[tap, g * width : (g + 1) * width, :] = select_lanes(left, right).astype(BF)


def mixed_body(hops, tile, pair, meta, amounts, tap_zero, *rest):
    sources, (own, partner, series) = rest[: hops + 1], rest[hops + 1 :]
    half = tap_zero.shape[1]
    core = meta[2]
    early_a, early_b = amounts[2 * pair], amounts[2 * pair + 1]
    for n in range(hops + 1):
        for h in range(2):
            series[(2 * n + h) * half : (2 * n + h + 1) * half, :] = sources[n][h ^ core].astype(
                F32
            )
    for slot, target in ((0, own), (1, partner)):

        def step(i, carry, slot=slot, target=target):
            row = pl.multiple_of(i * tile, tile)
            start = (slot ^ core) * half + row
            early = select_lanes(
                series[pl.ds(start + early_a, tile), :], series[pl.ds(start + early_b, tile), :]
            )
            target[pl.ds(row, tile), :] = (tap_zero[slot, pl.ds(row, tile), :] + early).astype(BF)
            return carry

        lax.fori_loop(0, half // tile, step, 0)


def outer_body(chunks, parts, tile, by_rows, split, meta, *rest):
    count = chunks * (2 if split else 1)
    lefts, rest = rest[:count], rest[count:]
    rights, outs, total = rest[:2], rest[2:-1], rest[-1]
    total[...] = jnp.zeros_like(total)
    for slot in range(2):

        def step(i, carry, slot=slot):
            at = pl.multiple_of(i * tile, tile)
            if split:
                left = [lefts[2 * j + slot][pl.ds(at, tile), :] for j in range(chunks)]
            else:
                left = [lefts[j][slot, pl.ds(at, tile), :] for j in range(chunks)]
            left = jnp.concatenate(left, axis=1)
            if split and slot == 1:
                outs[parts][pl.ds(at, tile), :] = left
            total[...] += dot(left, rights[slot][pl.ds(at, tile), :], 0, 0)
            return carry

        lax.fori_loop(0, rights[slot].shape[0] // tile, step, 0)
    rows, columns = outs[0].shape
    for k in range(parts):
        if by_rows:
            start = pl.multiple_of((meta[0] ^ k) * rows, rows)
            got = total[pl.ds(start, rows), :]
        else:
            start = pl.multiple_of((meta[0] ^ k) * columns, columns)
            got = total[:, pl.ds(start, columns)]
        outs[k][...] = got.astype(outs[k].dtype)


def signal_body(tile, base, *rest):
    side, side_far, target = rest[-3:]
    mixes, others = rest[:-5], rest[-5:-3]

    def step(i, carry):
        at = pl.multiple_of(i * tile, tile)
        mix = jnp.concatenate([x[pl.ds(at, tile), :] for x in mixes], axis=1)
        other = jnp.concatenate([x[pl.ds(at, tile), :] for x in others], axis=1)
        acc = base[pl.ds(at, tile), :].astype(F32) + dot(mix, side[...], 1, 1)
        target[pl.ds(at, tile), :] = (acc + dot(other, side_far[...], 1, 1)).astype(BF)
        return carry

    lax.fori_loop(0, base.shape[0] // tile, step, 0)


def tree(values):
    while len(values) > 1:
        values = [values[i] + values[i + 1] for i in range(0, len(values), 2)]
    return values[0]


def split_body(count, parts, meta, *rest):
    ins, outs, total = rest[:count], rest[count:-1], rest[-1]
    total[...] = tree([x[...].astype(F32) for x in ins])
    rows = outs[0].shape[0]
    for k in range(parts):
        at = pl.multiple_of((meta[1] ^ k) * rows, rows)
        outs[k][...] = total[pl.ds(at, rows), :].astype(outs[k].dtype)


def gather_body(count, chips, pairs, meta, *rest):
    first, second = rest[:count], rest[count : 2 * count]
    kernels, rest = rest[2 * count : 2 * count + pairs], rest[2 * count + pairs :]
    outs, (sum_one, sum_two, held) = rest[:-3], rest[-3:]
    sum_one[...] = tree([x[...].astype(F32) for x in first])
    sum_two[...] = tree([x[...].astype(F32) for x in second])
    width = sum_one.shape[1]
    one, two, taps = sum_one.shape[0] // chips, sum_two.shape[0] // chips, held.shape[2]
    for j in range(pairs):
        for n in range(LANES // taps):
            held[j * (LANES // taps) + n] = kernels[j][:, n * taps : (n + 1) * taps, :]
    for k in range(chips):
        at, kind = meta[1] ^ k, outs[k].dtype
        outs[k][:one, :] = sum_one[pl.ds(pl.multiple_of(at * one, 8), one), :].astype(kind)
        block = sum_two[pl.ds(pl.multiple_of(at * two, 8), two), :].astype(kind)
        top = one
        for n in range(block.shape[1] // width):
            outs[k][top : top + two, :] = block[:, n * width : (n + 1) * width]
            top += two
        for tap in range(2):
            column = (tap * LANES) % width
            row = top + (tap * LANES) // width * taps
            outs[k][row : row + taps, column : column + LANES] = held[at, tap].astype(kind)


def divide_body(count, *rest):
    got = tree([x[...].astype(F32) for x in rest[:count]]).astype(BF)
    rows = rest[count].shape[0]
    rest[count][...] = got[:rows, :]
    rest[count + 1][...] = got[rows:, :]


def sum_body(count, factor, *rest):
    got = tree([x[...].astype(F32) for x in rest[:count]])
    rest[count][...] = (got if factor is None else got * factor).astype(rest[count].dtype)


def pack_body(count, meta, *rest):
    for k in range(count):
        rest[count][meta[1] ^ k] = rest[k][...]


def share_body(parts, meta, whole, *outs):
    piece = whole.shape[1] // (2 * parts)
    got = []
    for f in range(parts):
        both = whole[:, 2 * f * piece : 2 * (f + 1) * piece]
        got.append(jnp.where(meta[2] == 0, both[:, :piece], both[:, piece:]))
    first = outs[0].shape[1] // piece
    outs[0][...] = jnp.concatenate(got[:first], axis=1)
    outs[1][...] = jnp.concatenate(got[first:], axis=1)


def taps_body(chips, groups, meta, *rest):
    delays, blocks = rest[:chips], rest[chips : 2 * chips]
    amounts, outs = rest[2 * chips], rest[2 * chips + 1 :]
    width = LANES // 2
    for out in outs:
        out[...] = jnp.zeros_like(out)
    for k in range(chips):
        at = meta[1] ^ k
        for n in range(groups):
            group = at * groups + n
            amounts[group] = delays[k][n]
            for spot in range(2 * len(outs)):

                @pl.when(group == spot)
                def _(k=k, n=n, spot=spot):
                    out, g = outs[spot // 2], spot % 2
                    for tap in range(2):
                        top = tap * LANES + g * width
                        block = blocks[k][tap, n * width : (n + 1) * width, :].astype(F32)
                        lane = lax.broadcasted_iota(jnp.int32, block.shape, 1)
                        here = (lane < width) == (g == 0)
                        other = pltpu.roll(block, width, 1)
                        left, right = (block, other) if g == 0 else (other, block)
                        zero = jnp.zeros_like(block)
                        out[top : top + width, :LANES] = jnp.where(here, left, zero).astype(BF)
                        out[top : top + width, LANES:] = jnp.where(here, right, zero).astype(BF)


def local_step(signal, cotangent, w_in, w_conv, w_out, dilation, lengths):
    record, upstream = signal[0], cotangent[0]
    samples, channels = record.shape
    seq_size, fsdp_size = lax.axis_size("seq"), lax.axis_size("fsdp")
    chips = seq_size // 2
    seq_at, fsdp_at = lax.axis_index("seq"), lax.axis_index("fsdp")
    core, chip = seq_at % 2, seq_at // 2
    factor = 1.0 / math.sqrt(samples * seq_size * fsdp_size)
    block = 2 * samples
    hops = -(-MAX_DILATION // block)
    share = channels // 2
    piece = share // fsdp_size
    conv_chans = w_conv.shape[1]
    local_groups = dilation.shape[0]
    width = conv_chans // local_groups
    assert 2 * width == LANES and chips == fsdp_size and piece == conv_chans
    chunks = share // LANES

    def to_partner(x):
        return lax.ppermute(x, "seq", [(i, i ^ 1) for i in range(seq_size)])

    def from_fsdp(blocks):
        got = [blocks[0]]
        for k in range(1, fsdp_size):
            pairs = [(i, i ^ k) for i in range(fsdp_size)]
            got.append(lax.ppermute(blocks[k], "fsdp", pairs))
        return got

    def from_chips(blocks):
        got = [blocks[0]]
        for k in range(1, chips):
            pairs = [(i, i ^ (2 * k)) for i in range(seq_size)]
            got.append(lax.ppermute(blocks[k], "seq", pairs))
        return got

    def up(x, hop):
        return lax.ppermute(x, "seq", [(i, i + 2) for i in range(2 * (hop - 1), seq_size - 2)])

    def down(x, hop):
        return lax.ppermute(x, "seq", [(i + 2, i) for i in range(seq_size - 2 * hop)])

    where = jnp.stack([fsdp_at, chip, core, lengths[0] - chip * block]).astype(jnp.int32)
    wides = [share - LANES, LANES]
    in_shares = call(
        functools.partial(share_body, fsdp_size),
        [shape((w_in.shape[0], x), BF) for x in (LANES, share - LANES)],
        [where, w_in],
    )
    out_share = lax.dynamic_index_in_dim(
        w_out.reshape(2, piece, channels), core, 0, keepdims=False
    )
    record_far = to_partner(record)
    in_parts = [from_fsdp([x] * fsdp_size) for x in in_shares]
    upstream_far = to_partner(upstream)
    out_parts = from_fsdp([out_share] * fsdp_size)
    delays = from_chips([dilation] * chips)
    conv_parts = from_chips([w_conv] * chips)
    taps = call(
        functools.partial(taps_body, chips, local_groups),
        [shape((2 * chunks,), jnp.int32)] + [shape((2 * LANES, 2 * LANES), BF)] * chunks,
        [where] + delays + conv_parts,
        scalars=1 + chips,
        small=1,
    )
    amounts, kernels = taps[0], taps[1:]

    series = shape((2, samples, LANES), BF)
    tile = min(512, samples)
    first, lead = call(
        functools.partial(product_body, fsdp_size, tile, False, 0),
        [series, shape((channels, LANES), BF)],
        [where, record, record_far] + in_parts[0],
        flops=2 * block * channels * LANES,
    )
    got = call(
        functools.partial(product_body, fsdp_size, tile, False, LANES),
        [series] * (chunks - 1) + [shape((channels, share), BF)],
        [where, record, record_far] + in_parts[1] + [lead],
        flops=2 * block * channels * (share - LANES),
    )
    projected, panel = (first,) + got[:-1], got[-1]
    grad_gated = call(
        functools.partial(product_body, fsdp_size, tile, True, 0),
        [series] * chunks,
        [where, upstream, upstream_far] + out_parts,
        scratch=[pltpu.VMEM((share, channels), BF)],
        flops=2 * block * channels * share,
    )
    panel_far = to_partner(panel)

    tile = min(256, samples)
    gated, own_mixed, far_mixed, kernel_grads = [], [], [], []
    long = pltpu.VMEM((2 * (hops + 1) * samples, LANES), F32)
    for j in range(chunks):
        chain = [projected[j]]
        for hop in range(1, hops + 1):
            chain.append(up(chain[-1], hop))
        out, tap_zero, tap_one, grad_kernel = call(
            functools.partial(conv_body, hops, tile, j),
            [series, shape((2, samples, LANES), F32), series, shape((2, LANES, LANES), BF)],
            [where, amounts] + chain + [grad_gated[j], kernels[j]],
            scratch=[long, pltpu.VMEM((2 * LANES, 2 * LANES), F32)],
            flops=6 * block * 4 * LANES * LANES,
            scalars=2,
        )
        gated.append(out)
        kernel_grads.append(grad_kernel)
        back = [tap_one]
        for hop in range(1, hops + 1):
            back.append(down(back[-1], hop))
        own, other = call(
            functools.partial(mixed_body, hops, tile, j),
            [shape((samples, LANES), BF)] * 2,
            [where, amounts, tap_zero] + back,
            scratch=[long],
            scalars=2,
        )
        own_mixed.append(own)
        far_mixed.append(other)

    tile = min(512, samples)

    def outer(lefts, rights, by_rows, split):
        count = len(lefts) // 2 if split else len(lefts)
        rows, columns = LANES * count, channels
        one = (piece, columns) if by_rows else (rows, columns // fsdp_size)
        return call(
            functools.partial(outer_body, count, fsdp_size, tile, by_rows, split),
            [shape(one, F32)]
            + [shape(one, BF)] * (fsdp_size - 1)
            + ([shape((samples, rows), BF)] if split else []),
            [where] + list(lefts) + list(rights),
            scratch=[pltpu.VMEM((rows, columns), F32)],
            flops=2 * block * rows * columns,
        )

    def finish_sum(mine):
        rows, columns = mine.shape
        got = from_chips([mine] * chips)
        (packed,) = call(
            functools.partial(pack_body, chips), [shape((chips, rows, columns), BF)], [where] + got
        )
        return [packed, to_partner(packed)]

    mixed_in, flats = [], []
    for pick in (range(chunks - 1), range(chunks - 1, chunks)):
        sides = []
        for j in pick:
            sides += [own_mixed[j], far_mixed[j]]
        got = outer(sides, (record, record_far), False, True)
        mixed_in.append(to_partner(got[-1]))
        flats.append(from_fsdp(got[:fsdp_size]))
    got = outer(gated, (upstream, upstream_far), True, False)
    flat_out = from_fsdp(got)

    own_rows = channels // fsdp_size
    in_part, out_part = wides[0] // chips, piece // chips
    panel_rows = in_part + out_part * (channels // own_rows)
    kernel_rows = 2 * LANES * conv_chans // own_rows
    whole = (panel_rows + kernel_rows, own_rows)
    cut = call(
        functools.partial(gather_body, fsdp_size, chips, chunks),
        [shape(whole, F32)] + [shape(whole, BF)] * (chips - 1),
        [where] + flats[0] + flat_out + kernel_grads,
        scratch=[
            pltpu.VMEM((wides[0], own_rows), F32),
            pltpu.VMEM((piece, channels), F32),
            pltpu.VMEM((chips, 2, conv_chans, LANES), BF),
        ],
    )
    mine, mine_kernel = call(
        functools.partial(divide_body, chips),
        [shape((panel_rows, own_rows), BF), shape((kernel_rows, own_rows), BF)],
        from_chips(cut),
        scalars=0,
    )
    kernel_parts = from_fsdp([mine_kernel] * fsdp_size)
    finals = finish_sum(mine)

    last = (wides[1] // chips, own_rows)
    cut = call(
        functools.partial(split_body, fsdp_size, chips),
        [shape(last, F32)] + [shape(last, BF)] * (chips - 1),
        [where] + flats[1],
        scratch=[pltpu.VMEM((wides[1], own_rows), F32)],
    )
    (mine,) = call(
        functools.partial(sum_body, chips, None), [shape(last, BF)], from_chips(cut), scalars=0
    )
    finals += finish_sum(mine)

    tile = min(256, samples)

    (grad_signal,) = call(
        functools.partial(signal_body, tile),
        [shape((samples, channels), BF)],
        [upstream] + own_mixed + mixed_in + [panel, panel_far],
        scalars=0,
        flops=2 * samples * channels * channels,
    )

    def finish_body(meta, *rest):
        packs, parts = rest[:4], rest[4 : 4 + fsdp_size]
        grad_in, grad_out, grad_conv, turned = rest[4 + fsdp_size :]
        core_at = meta[2]
        for side in range(2):
            first = packs[side][...].astype(F32) * factor
            second = packs[2 + side][...].astype(F32) * factor
            for p in range(chips):
                at = pl.multiple_of((side ^ core_at) * piece + p * out_part, 8)
                for n in range(channels // own_rows):
                    top = in_part + n * out_part
                    grad_out[pl.ds(at, out_part), n * own_rows : (n + 1) * own_rows] = first[
                        p, top : top + out_part, :
                    ]
                at = p * in_part
                turned[side ^ core_at, at : at + in_part, :] = first[p, :in_part, :]
                at, rows = wides[0] + p * last[0], last[0]
                turned[side ^ core_at, at : at + rows, :] = second[p]
        for f in range(fsdp_size):
            pair = [turned[c, f * piece : (f + 1) * piece, :] for c in range(2)]
            grad_in[:, 2 * f * piece : 2 * (f + 1) * piece] = jnp.concatenate(pair, axis=0).T
        total = tree([x[...].astype(F32) for x in parts]) * factor
        for tap in range(2):
            column = (tap * LANES) % own_rows
            row = (tap * LANES) // own_rows * conv_chans
            grad_conv[tap] = total[row : row + conv_chans, column : column + LANES]

    grad_in, grad_out, grad_conv = call(
        finish_body,
        [shape((own_rows, channels), F32)] * 2 + [shape((2, conv_chans, LANES), F32)],
        [where] + finals + kernel_parts,
        scratch=[pltpu.VMEM((2, share, own_rows), F32)],
    )
    return (grad_signal[None], grad_in, grad_out, grad_conv)


def solution(mesh):
    placed = (
        P("fsdp", "seq", None),
        P("fsdp", "seq", None),
        P("fsdp", None),
        P(None, "seq", None),
        P("fsdp", None),
        P("seq"),
        P("fsdp"),
    )
    return jax.shard_map(
        local_step,
        mesh=mesh,
        in_specs=placed,
        out_specs=(P("fsdp", "seq", None), P("fsdp", None), P("fsdp", None), P(None, "seq", None)),
        check_vma=False,
    )
```

```python
import functools
import math

import jax
import jax.numpy as jnp
from jax import lax
from jax.experimental import pallas as pl
from jax.experimental.pallas import tpu as pltpu
from jax.sharding import PartitionSpec as P


MAX_DILATION = 4095
LANES = 128
BF = jnp.bfloat16
F32 = jnp.float32
VM = pl.BlockSpec(memory_space=pltpu.VMEM)
SM = pl.BlockSpec(memory_space=pltpu.SMEM)


def dot(a, b, ca, cb):
    return lax.dot_general(a, b, (((ca,), (cb,)), ((), ())), preferred_element_type=F32)


def call(body, outs, ins, scratch=(), flops=0, scalars=1, small=0):
    moved = sum(math.prod(x.shape) * x.dtype.itemsize for x in list(ins) + list(outs))
    return pl.pallas_call(
        body,
        out_shape=tuple(outs),
        in_specs=[SM] * scalars + [VM] * (len(ins) - scalars),
        out_specs=tuple([SM] * small + [VM] * (len(outs) - small)),
        scratch_shapes=list(scratch),
        cost_estimate=pl.CostEstimate(flops=flops, bytes_accessed=moved, transcendentals=0),
        compiler_params=pltpu.CompilerParams(vmem_limit_bytes=20 * 1024 * 1024),
    )(*ins)


def shape(dims, kind):
    return jax.ShapeDtypeStruct(dims, kind)


def product_body(parts, tile, turned, skip, meta, own, partner, *rest):
    weights, outs = rest[:parts], rest[parts:]
    if skip:
        outs[-1][:, :skip] = outs[0][...]
        outs = outs[1:]
    targets, panel = outs[:-1], outs[-1]
    rows = weights[0].shape[0]
    for k in range(parts):
        start = pl.multiple_of((meta[0] ^ k) * rows, rows)
        panel[pl.ds(start, rows), skip:] = weights[k][...]
    for slot, source in enumerate((own, partner)):

        def step(i, carry, slot=slot, source=source):
            at = pl.multiple_of(i * tile, tile)
            side = panel[:, skip:]
            got = dot(source[pl.ds(at, tile), :], side, 1, int(turned)).astype(BF)
            for j, target in enumerate(targets):
                target[slot, pl.ds(at, tile), :] = got[:, j * LANES : (j + 1) * LANES]
            return carry

        lax.fori_loop(0, source.shape[0] // tile, step, 0)


def select_lanes(a, b):
    lane = lax.broadcasted_iota(jnp.int32, a.shape, 1)
    return jnp.where(lane < LANES // 2, a, b)


def conv_body(hops, tile, pair, meta, amounts, *rest):
    sources, rest = rest[: hops + 1], rest[hops + 1 :]
    upstream, kernel, gated, tap_zero, tap_one, grad_kernel, series, total = rest
    half = sources[0].shape[1]
    core, alive = meta[2], meta[3]
    late_a, late_b = amounts[2 * pair], amounts[2 * pair + 1]
    for n in range(hops + 1):
        for h in range(2):
            series[(2 * (hops - n) + h) * half : (2 * (hops - n) + h + 1) * half, :] = (
                sources[n][h ^ core].astype(F32)
            )
    total[...] = jnp.zeros_like(total)
    per_half = half // tile

    def step(i, carry):
        slot = (i // per_half) ^ core
        row = pl.multiple_of((i % per_half) * tile, tile)
        start = 2 * hops * half + i * tile
        late = select_lanes(
            series[pl.ds(start - late_a, tile), :], series[pl.ds(start - late_b, tile), :]
        ).astype(BF)
        stacked = jnp.concatenate([sources[0][slot, pl.ds(row, tile), :], late], axis=1)
        pre = dot(stacked, kernel[...], 1, 0)
        tanh_act = jnp.tanh(pre[:, :LANES])
        sig_act = jax.nn.sigmoid(pre[:, LANES:])
        moment = i * tile + lax.broadcasted_iota(jnp.int32, tanh_act.shape, 0)
        mask = (moment < alive).astype(F32)
        gated[slot, pl.ds(row, tile), :] = (tanh_act * sig_act * mask).astype(BF)
        masked = upstream[slot, pl.ds(row, tile), :].astype(F32) * mask
        grad_filter = masked * sig_act * (1.0 - tanh_act * tanh_act)
        grad_gate = masked * tanh_act * sig_act * (1.0 - sig_act)
        acts = jnp.concatenate([grad_filter.astype(BF), grad_gate.astype(BF)], axis=1)
        total[...] += dot(stacked, acts, 0, 0)
        back = dot(acts, kernel[...], 1, 1)
        tap_zero[slot, pl.ds(row, tile), :] = back[:, :LANES]
        tap_one[slot, pl.ds(row, tile), :] = back[:, LANES:].astype(BF)
        return carry

    lax.fori_loop(0, 2 * per_half, step, 0)
    width = LANES // 2
    for tap in range(2):
        for g in range(2):
            top = tap * LANES + g * width
            left = total[top : top + width, :LANES]
            right = total[top : top + width, LANES:]
            if g == 0:
                right = pltpu.roll(right, width, 1)
            else:
                left = pltpu.roll(left, width, 1)
            grad_kernel[tap, g * width : (g + 1) * width, :] = select_lanes(left, right)


def mixed_body(hops, tile, pair, meta, amounts, tap_zero, *rest):
    sources, (own, partner, series) = rest[: hops + 1], rest[hops + 1 :]
    half = tap_zero.shape[1]
    core = meta[2]
    early_a, early_b = amounts[2 * pair], amounts[2 * pair + 1]
    for n in range(hops + 1):
        for h in range(2):
            series[(2 * n + h) * half : (2 * n + h + 1) * half, :] = sources[n][h ^ core].astype(
                F32
            )
    for slot, target in ((0, own), (1, partner)):

        def step(i, carry, slot=slot, target=target):
            row = pl.multiple_of(i * tile, tile)
            start = (slot ^ core) * half + row
            early = select_lanes(
                series[pl.ds(start + early_a, tile), :], series[pl.ds(start + early_b, tile), :]
            )
            target[pl.ds(row, tile), :] = (tap_zero[slot, pl.ds(row, tile), :] + early).astype(BF)
            return carry

        lax.fori_loop(0, half // tile, step, 0)


def outer_body(chunks, parts, tile, split, taps, meta, *rest):
    count = chunks * (2 if split else 1)
    lefts, rest = rest[:count], rest[count:]
    rights, rest = rest[:2], rest[2:]
    kernels, outs, total = rest[: -1 - parts - split], rest[-1 - parts - split : -1], rest[-1]
    total[...] = jnp.zeros_like(total)
    for slot in range(2):

        def step(i, carry, slot=slot):
            at = pl.multiple_of(i * tile, tile)
            if split:
                left = [lefts[2 * j + slot][pl.ds(at, tile), :] for j in range(chunks)]
            else:
                left = [lefts[j][slot, pl.ds(at, tile), :] for j in range(chunks)]
            left = jnp.concatenate(left, axis=1)
            if split and slot == 1:
                outs[parts][pl.ds(at, tile), :] = left
            total[...] += dot(left, rights[slot][pl.ds(at, tile), :], 0, 0)
            return carry

        lax.fori_loop(0, rights[slot].shape[0] // tile, step, 0)
    columns = outs[0].shape[1]
    for k in range(parts):
        if split:
            start = pl.multiple_of((meta[0] ^ k) * columns, columns)
            outs[k][...] = total[:, pl.ds(start, columns)].astype(outs[k].dtype)
            continue
        rows = total.shape[0] // parts
        start = pl.multiple_of((meta[0] ^ k) * rows, rows)
        outs[k][:rows, :] = total[pl.ds(start, rows), :].astype(outs[k].dtype)
        few = taps // parts
        spot = 0
        for kernel in kernels:
            for low in range(0, LANES, taps):
                for tap in range(2):
                    start = pl.multiple_of(low + (meta[0] ^ k) * few, 8)
                    top, left = rows + spot // columns * few, spot % columns
                    outs[k][top : top + few, left : left + LANES] = kernel[
                        tap, pl.ds(start, few), :
                    ].astype(outs[k].dtype)
                    spot += LANES


def signal_body(tile, base, *rest):
    side, side_far, target = rest[-3:]
    mixes, others = rest[:-5], rest[-5:-3]

    def step(i, carry):
        at = pl.multiple_of(i * tile, tile)
        mix = jnp.concatenate([x[pl.ds(at, tile), :] for x in mixes], axis=1)
        other = jnp.concatenate([x[pl.ds(at, tile), :] for x in others], axis=1)
        acc = base[pl.ds(at, tile), :].astype(F32) + dot(mix, side[...], 1, 1)
        target[pl.ds(at, tile), :] = (acc + dot(other, side_far[...], 1, 1)).astype(BF)
        return carry

    lax.fori_loop(0, base.shape[0] // tile, step, 0)


def tree(values):
    while len(values) > 1:
        values = [values[i] + values[i + 1] for i in range(0, len(values), 2)]
    return values[0]


def split_body(count, parts, meta, *rest):
    ins, outs, total = rest[:count], rest[count:-1], rest[-1]
    total[...] = tree([x[...].astype(F32) for x in ins])
    rows = outs[0].shape[0]
    for k in range(parts):
        at = pl.multiple_of((meta[1] ^ k) * rows, rows)
        outs[k][...] = total[pl.ds(at, rows), :].astype(outs[k].dtype)


def gather_body(count, chips, few, meta, *rest):
    first, second = rest[:count], rest[count : 2 * count]
    outs, (sum_one, sum_two) = rest[2 * count : -2], rest[-2:]
    sum_one[...] = tree([x[...].astype(F32) for x in first])
    sum_two[...] = tree([x[...].astype(F32) for x in second])
    width, wide = sum_one.shape[1], sum_two.shape[1]
    one = sum_one.shape[0] // chips
    flat = sum_two.shape[0] - 2 * LANES * chips * few // wide
    two = flat // chips
    for k in range(chips):
        at, kind = meta[1] ^ k, outs[k].dtype
        outs[k][:one, :] = sum_one[pl.ds(pl.multiple_of(at * one, 8), one), :].astype(kind)
        block = sum_two[pl.ds(pl.multiple_of(at * two, 8), two), :].astype(kind)
        top = one
        for n in range(wide // width):
            outs[k][top : top + two, :] = block[:, n * width : (n + 1) * width]
            top += two
        each = wide // (2 * LANES)
        row = pl.multiple_of(flat + at // each * few, 8)
        lane = pl.multiple_of(at % each * (2 * LANES), 2 * LANES)
        block = sum_two[pl.ds(row, few), pl.ds(lane, 2 * LANES)].astype(kind)
        for n in range(2 * LANES // width):
            outs[k][top : top + few, :] = block[:, n * width : (n + 1) * width]
            top += few


def divide_body(count, *rest):
    got = tree([x[...].astype(F32) for x in rest[:count]]).astype(BF)
    rows = rest[count].shape[0]
    rest[count][...] = got[:rows, :]
    rest[count + 1][...] = got[rows:, :]


def sum_body(count, factor, *rest):
    got = tree([x[...].astype(F32) for x in rest[:count]])
    rest[count][...] = (got if factor is None else got * factor).astype(rest[count].dtype)


def pack_body(count, meta, *rest):
    for k in range(count):
        rest[count][meta[1] ^ k] = rest[k][...]


def share_body(parts, meta, whole, *outs):
    piece = whole.shape[1] // (2 * parts)
    got = []
    for f in range(parts):
        both = whole[:, 2 * f * piece : 2 * (f + 1) * piece]
        got.append(jnp.where(meta[2] == 0, both[:, :piece], both[:, piece:]))
    first = outs[0].shape[1] // piece
    outs[0][...] = jnp.concatenate(got[:first], axis=1)
    outs[1][...] = jnp.concatenate(got[first:], axis=1)


def taps_body(chips, groups, meta, *rest):
    delays, blocks = rest[:chips], rest[chips : 2 * chips]
    amounts, outs = rest[2 * chips], rest[2 * chips + 1 :]
    width = LANES // 2
    for out in outs:
        out[...] = jnp.zeros_like(out)
    for k in range(chips):
        at = meta[1] ^ k
        for n in range(groups):
            group = at * groups + n
            amounts[group] = delays[k][n]
            for spot in range(2 * len(outs)):

                @pl.when(group == spot)
                def _(k=k, n=n, spot=spot):
                    out, g = outs[spot // 2], spot % 2
                    for tap in range(2):
                        top = tap * LANES + g * width
                        block = blocks[k][tap, n * width : (n + 1) * width, :].astype(F32)
                        lane = lax.broadcasted_iota(jnp.int32, block.shape, 1)
                        here = (lane < width) == (g == 0)
                        other = pltpu.roll(block, width, 1)
                        left, right = (block, other) if g == 0 else (other, block)
                        zero = jnp.zeros_like(block)
                        out[top : top + width, :LANES] = jnp.where(here, left, zero).astype(BF)
                        out[top : top + width, LANES:] = jnp.where(here, right, zero).astype(BF)


def local_step(signal, cotangent, w_in, w_conv, w_out, dilation, lengths):
    record, upstream = signal[0], cotangent[0]
    samples, channels = record.shape
    seq_size, fsdp_size = lax.axis_size("seq"), lax.axis_size("fsdp")
    chips = seq_size // 2
    seq_at, fsdp_at = lax.axis_index("seq"), lax.axis_index("fsdp")
    core, chip = seq_at % 2, seq_at // 2
    factor = 1.0 / math.sqrt(samples * seq_size * fsdp_size)
    block = 2 * samples
    hops = -(-MAX_DILATION // block)
    share = channels // 2
    piece = share // fsdp_size
    conv_chans = w_conv.shape[1]
    local_groups = dilation.shape[0]
    width = conv_chans // local_groups
    assert 2 * width == LANES and chips == fsdp_size and piece == conv_chans
    chunks = share // LANES

    def to_partner(x):
        return lax.ppermute(x, "seq", [(i, i ^ 1) for i in range(seq_size)])

    def from_fsdp(blocks):
        got = [blocks[0]]
        for k in range(1, fsdp_size):
            pairs = [(i, i ^ k) for i in range(fsdp_size)]
            got.append(lax.ppermute(blocks[k], "fsdp", pairs))
        return got

    def from_chips(blocks):
        got = [blocks[0]]
        for k in range(1, chips):
            pairs = [(i, i ^ (2 * k)) for i in range(seq_size)]
            got.append(lax.ppermute(blocks[k], "seq", pairs))
        return got

    def up(x, hop):
        return lax.ppermute(x, "seq", [(i, i + 2) for i in range(2 * (hop - 1), seq_size - 2)])

    def down(x, hop):
        return lax.ppermute(x, "seq", [(i + 2, i) for i in range(seq_size - 2 * hop)])

    where = jnp.stack([fsdp_at, chip, core, lengths[0] - chip * block]).astype(jnp.int32)
    wides = [share // 2, share // 2]
    in_shares = call(
        functools.partial(share_body, fsdp_size),
        [shape((w_in.shape[0], x), BF) for x in (LANES, share - LANES)],
        [where, w_in],
    )
    out_share = lax.dynamic_index_in_dim(
        w_out.reshape(2, piece, channels), core, 0, keepdims=False
    )
    record_far = to_partner(record)
    in_parts = [from_fsdp([x] * fsdp_size) for x in in_shares]
    upstream_far = to_partner(upstream)
    out_parts = from_fsdp([out_share] * fsdp_size)
    delays = from_chips([dilation] * chips)
    conv_parts = from_chips([w_conv] * chips)
    taps = call(
        functools.partial(taps_body, chips, local_groups),
        [shape((2 * chunks,), jnp.int32)] + [shape((2 * LANES, 2 * LANES), BF)] * chunks,
        [where] + delays + conv_parts,
        scalars=1 + chips,
        small=1,
    )
    amounts, kernels = taps[0], taps[1:]

    series = shape((2, samples, LANES), BF)
    tile = min(512, samples)
    first, lead = call(
        functools.partial(product_body, fsdp_size, tile, False, 0),
        [series, shape((channels, LANES), BF)],
        [where, record, record_far] + in_parts[0],
        flops=2 * block * channels * LANES,
    )
    got = call(
        functools.partial(product_body, fsdp_size, tile, False, LANES),
        [series] * (chunks - 1) + [shape((channels, share), BF)],
        [where, record, record_far] + in_parts[1] + [lead],
        flops=2 * block * channels * (share - LANES),
    )
    projected, panel = (first,) + got[:-1], got[-1]
    grad_gated = call(
        functools.partial(product_body, fsdp_size, tile, True, 0),
        [series] * chunks,
        [where, upstream, upstream_far] + out_parts,
        scratch=[pltpu.VMEM((share, channels), BF)],
        flops=2 * block * channels * share,
    )
    panel_far = to_partner(panel)

    tile = min(256, samples)
    gated, own_mixed, far_mixed, kernel_grads = [], [], [], []
    long = pltpu.VMEM((2 * (hops + 1) * samples, LANES), F32)
    for j in range(chunks):
        chain = [projected[j]]
        for hop in range(1, hops + 1):
            chain.append(up(chain[-1], hop))
        out, tap_zero, tap_one, grad_kernel = call(
            functools.partial(conv_body, hops, tile, j),
            [series, shape((2, samples, LANES), F32), series, shape((2, LANES, LANES), F32)],
            [where, amounts] + chain + [grad_gated[j], kernels[j]],
            scratch=[long, pltpu.VMEM((2 * LANES, 2 * LANES), F32)],
            flops=6 * block * 4 * LANES * LANES,
            scalars=2,
        )
        gated.append(out)
        kernel_grads.append(grad_kernel)
        back = [tap_one]
        for hop in range(1, hops + 1):
            back.append(down(back[-1], hop))
        own, other = call(
            functools.partial(mixed_body, hops, tile, j),
            [shape((samples, LANES), BF)] * 2,
            [where, amounts, tap_zero] + back,
            scratch=[long],
            scalars=2,
        )
        own_mixed.append(own)
        far_mixed.append(other)

    tile = min(512, samples)

    few = conv_chans // fsdp_size

    def outer(lefts, rights, split):
        count = len(lefts) // 2 if split else len(lefts)
        rows, columns = LANES * count, channels
        more = [] if split else kernel_grads
        tall = piece + 2 * LANES * chips * few // channels
        one = (rows, columns // fsdp_size) if split else (tall, columns)
        return call(
            functools.partial(outer_body, count, fsdp_size, tile, split, conv_chans),
            [shape(one, F32)]
            + [shape(one, BF)] * (fsdp_size - 1)
            + ([shape((samples, rows), BF)] if split else []),
            [where] + list(lefts) + list(rights) + more,
            scratch=[pltpu.VMEM((rows, columns), F32)],
            flops=2 * block * rows * columns,
        )

    def finish_sum(mine):
        rows, columns = mine.shape
        got = from_chips([mine] * chips)
        (packed,) = call(
            functools.partial(pack_body, chips), [shape((chips, rows, columns), BF)], [where] + got
        )
        return [packed, to_partner(packed)]

    mixed_in, flats = [], []
    for pick in (range(chunks // 2), range(chunks // 2, chunks)):
        sides = []
        for j in pick:
            sides += [own_mixed[j], far_mixed[j]]
        got = outer(sides, (record, record_far), True)
        mixed_in.append(to_partner(got[-1]))
        flats.append(from_fsdp(got[:fsdp_size]))
    got = outer(gated, (upstream, upstream_far), False)
    flat_out = from_fsdp(got)

    own_rows = channels // fsdp_size
    in_part, out_part = wides[0] // chips, piece // chips
    panel_rows = in_part + out_part * (channels // own_rows)
    kernel_rows = 2 * LANES * few // own_rows
    whole = (panel_rows + kernel_rows, own_rows)
    cut = call(
        functools.partial(gather_body, fsdp_size, chips, few),
        [shape(whole, F32)] + [shape(whole, BF)] * (chips - 1),
        [where] + flats[0] + flat_out,
        scratch=[pltpu.VMEM((wides[0], own_rows), F32), pltpu.VMEM(flat_out[0].shape, F32)],
    )
    mine, mine_kernel = call(
        functools.partial(divide_body, chips),
        [shape((panel_rows, own_rows), BF), shape((kernel_rows, own_rows), BF)],
        from_chips(cut),
        scalars=0,
    )
    kernel_parts = from_fsdp([mine_kernel] * fsdp_size)
    finals = finish_sum(mine)

    last = (wides[1] // chips, own_rows)
    cut = call(
        functools.partial(split_body, fsdp_size, chips),
        [shape(last, F32)] + [shape(last, BF)] * (chips - 1),
        [where] + flats[1],
        scratch=[pltpu.VMEM((wides[1], own_rows), F32)],
    )
    (mine,) = call(
        functools.partial(sum_body, chips, None), [shape(last, BF)], from_chips(cut), scalars=0
    )
    finals += finish_sum(mine)

    tile = min(256, samples)

    (grad_signal,) = call(
        functools.partial(signal_body, tile),
        [shape((samples, channels), BF)],
        [upstream] + own_mixed + mixed_in + [panel, panel_far],
        scalars=0,
        flops=2 * samples * channels * channels,
    )

    def finish_body(meta, *rest):
        packs, parts = rest[:4], rest[4 : 4 + fsdp_size]
        grad_in, grad_out, grad_conv, turned = rest[4 + fsdp_size :]
        core_at = meta[2]
        for side in range(2):
            first = packs[side][...].astype(F32) * factor
            second = packs[2 + side][...].astype(F32) * factor
            for p in range(chips):
                at = pl.multiple_of((side ^ core_at) * piece + p * out_part, 8)
                for n in range(channels // own_rows):
                    top = in_part + n * out_part
                    grad_out[pl.ds(at, out_part), n * own_rows : (n + 1) * own_rows] = first[
                        p, top : top + out_part, :
                    ]
                at = p * in_part
                turned[side ^ core_at, at : at + in_part, :] = first[p, :in_part, :]
                at, rows = wides[0] + p * last[0], last[0]
                turned[side ^ core_at, at : at + rows, :] = second[p]
        for f in range(fsdp_size):
            pair = [turned[c, f * piece : (f + 1) * piece, :] for c in range(2)]
            grad_in[:, 2 * f * piece : 2 * (f + 1) * piece] = jnp.concatenate(pair, axis=0).T
        for k, x in enumerate(parts):
            total = x[...].astype(F32) * factor
            at = pl.multiple_of((meta[0] ^ k) * few, 8)
            for tap in range(2):
                left, top = (tap * LANES) % own_rows, (tap * LANES) // own_rows * few
                grad_conv[tap, pl.ds(at, few), :] = total[top : top + few, left : left + LANES]

    grad_in, grad_out, grad_conv = call(
        finish_body,
        [shape((own_rows, channels), F32)] * 2 + [shape((2, conv_chans, LANES), F32)],
        [where] + finals + kernel_parts,
        scratch=[pltpu.VMEM((2, share, own_rows), F32)],
    )
    return (grad_signal[None], grad_in, grad_out, grad_conv)


def solution(mesh):
    placed = (
        P("fsdp", "seq", None),
        P("fsdp", "seq", None),
        P("fsdp", None),
        P(None, "seq", None),
        P("fsdp", None),
        P("seq"),
        P("fsdp"),
    )
    return jax.shard_map(
        local_step,
        mesh=mesh,
        in_specs=placed,
        out_specs=(P("fsdp", "seq", None), P("fsdp", None), P("fsdp", None), P(None, "seq", None)),
        check_vma=False,
    )
```

```python
import functools
import math

import jax
import jax.numpy as jnp
from jax import lax
from jax.experimental import pallas as pl
from jax.experimental.pallas import tpu as pltpu
from jax.sharding import PartitionSpec as P


MAX_DILATION = 4095
LANES = 128
BF = jnp.bfloat16
F32 = jnp.float32
VM = pl.BlockSpec(memory_space=pltpu.VMEM)
SM = pl.BlockSpec(memory_space=pltpu.SMEM)
ANY = pl.BlockSpec(memory_space=pl.ANY)


def dot(a, b, ca, cb):
    return lax.dot_general(a, b, (((ca,), (cb,)), ((), ())), preferred_element_type=F32)


def call(body, outs, ins, scratch=(), flops=0, scalars=1, small=0, stay=()):
    moved = sum(math.prod(x.shape) * x.dtype.itemsize for x in list(ins) + list(outs))
    return pl.pallas_call(
        body,
        out_shape=tuple(outs),
        in_specs=[SM if n < scalars else ANY if n in stay else VM for n in range(len(ins))],
        out_specs=tuple([SM] * small + [VM] * (len(outs) - small)),
        scratch_shapes=list(scratch),
        cost_estimate=pl.CostEstimate(flops=flops, bytes_accessed=moved, transcendentals=0),
        compiler_params=pltpu.CompilerParams(vmem_limit_bytes=20 * 1024 * 1024),
    )(*ins)


def shape(dims, kind):
    return jax.ShapeDtypeStruct(dims, kind)


def product_body(parts, tile, turned, skip, meta, own, partner, *rest):
    weights, outs = rest[:parts], rest[parts:]
    if skip:
        outs[-1][:, :skip] = outs[0][...]
        outs = outs[1:]
    targets, panel = outs[:-1], outs[-1]
    rows = weights[0].shape[0]
    for k in range(parts):
        start = pl.multiple_of((meta[0] ^ k) * rows, rows)
        panel[pl.ds(start, rows), skip:] = weights[k][...]
    for slot, source in enumerate((own, partner)):

        def step(i, carry, slot=slot, source=source):
            at = pl.multiple_of(i * tile, tile)
            side = panel[:, skip:]
            got = dot(source[pl.ds(at, tile), :], side, 1, int(turned)).astype(BF)
            for j, target in enumerate(targets):
                target[slot, pl.ds(at, tile), :] = got[:, j * LANES : (j + 1) * LANES]
            return carry

        lax.fori_loop(0, source.shape[0] // tile, step, 0)


def first_body(parts, tile, meta, own, partner, *rest):
    held, sem = rest[-2:]
    copy = pltpu.make_async_copy(own, held, sem)
    copy.start()
    weights, (target, panel) = rest[:parts], rest[parts:-2]
    rows = weights[0].shape[0]
    for k in range(parts):
        start = pl.multiple_of((meta[0] ^ k) * rows, rows)
        panel[pl.ds(start, rows), :] = weights[k][...]
    for slot, source in ((1, partner), (0, held)):
        if slot == 0:
            copy.wait()

        def step(i, carry, slot=slot, source=source):
            at = pl.multiple_of(i * tile, tile)
            got = dot(source[pl.ds(at, tile), :], panel[...], 1, 0).astype(BF)
            target[slot, pl.ds(at, tile), :] = got
            return carry

        lax.fori_loop(0, source.shape[0] // tile, step, 0)


def select_lanes(a, b):
    lane = lax.broadcasted_iota(jnp.int32, a.shape, 1)
    return jnp.where(lane < LANES // 2, a, b)


def conv_body(hops, tile, pair, meta, amounts, *rest):
    sources, rest = rest[: hops + 1], rest[hops + 1 :]
    upstream, kernel, gated, tap_zero, tap_one, grad_kernel, series, total = rest
    half = sources[0].shape[1]
    core, alive = meta[2], meta[3]
    late_a, late_b = amounts[2 * pair], amounts[2 * pair + 1]
    for n in range(hops + 1):
        for h in range(2):
            series[(2 * (hops - n) + h) * half : (2 * (hops - n) + h + 1) * half, :] = (
                sources[n][h ^ core].astype(F32)
            )
    total[...] = jnp.zeros_like(total)
    per_half = half // tile

    def step(i, carry):
        slot = (i // per_half) ^ core
        row = pl.multiple_of((i % per_half) * tile, tile)
        start = 2 * hops * half + i * tile
        late = select_lanes(
            series[pl.ds(start - late_a, tile), :], series[pl.ds(start - late_b, tile), :]
        ).astype(BF)
        stacked = jnp.concatenate([sources[0][slot, pl.ds(row, tile), :], late], axis=1)
        pre = dot(stacked, kernel[...], 1, 0)
        tanh_act = jnp.tanh(pre[:, :LANES])
        sig_act = jax.nn.sigmoid(pre[:, LANES:])
        moment = i * tile + lax.broadcasted_iota(jnp.int32, tanh_act.shape, 0)
        mask = (moment < alive).astype(F32)
        gated[slot, pl.ds(row, tile), :] = (tanh_act * sig_act * mask).astype(BF)
        masked = upstream[slot, pl.ds(row, tile), :].astype(F32) * mask
        grad_filter = masked * sig_act * (1.0 - tanh_act * tanh_act)
        grad_gate = masked * tanh_act * sig_act * (1.0 - sig_act)
        acts = jnp.concatenate([grad_filter.astype(BF), grad_gate.astype(BF)], axis=1)
        total[...] += dot(stacked, acts, 0, 0)
        back = dot(acts, kernel[...], 1, 1)
        tap_zero[slot, pl.ds(row, tile), :] = back[:, :LANES]
        tap_one[slot, pl.ds(row, tile), :] = back[:, LANES:].astype(BF)
        return carry

    lax.fori_loop(0, 2 * per_half, step, 0)
    width = LANES // 2
    for tap in range(2):
        for g in range(2):
            top = tap * LANES + g * width
            left = total[top : top + width, :LANES]
            right = total[top : top + width, LANES:]
            if g == 0:
                right = pltpu.roll(right, width, 1)
            else:
                left = pltpu.roll(left, width, 1)
            grad_kernel[tap, g * width : (g + 1) * width, :] = select_lanes(left, right)


def mixed_body(hops, tile, pair, meta, amounts, tap_zero, *rest):
    sources, (own, partner, series) = rest[: hops + 1], rest[hops + 1 :]
    half = tap_zero.shape[1]
    core = meta[2]
    early_a, early_b = amounts[2 * pair], amounts[2 * pair + 1]
    for n in range(hops + 1):
        for h in range(2):
            series[(2 * n + h) * half : (2 * n + h + 1) * half, :] = sources[n][h ^ core].astype(
                F32
            )
    for slot, target in ((0, own), (1, partner)):

        def step(i, carry, slot=slot, target=target):
            row = pl.multiple_of(i * tile, tile)
            start = (slot ^ core) * half + row
            early = select_lanes(
                series[pl.ds(start + early_a, tile), :], series[pl.ds(start + early_b, tile), :]
            )
            target[pl.ds(row, tile), :] = (tap_zero[slot, pl.ds(row, tile), :] + early).astype(BF)
            return carry

        lax.fori_loop(0, half // tile, step, 0)


def outer_body(chunks, parts, tile, split, taps, meta, *rest):
    count = chunks * (2 if split else 1)
    lefts, rest = rest[:count], rest[count:]
    rights, rest = rest[:2], rest[2:]
    kernels, outs, total = rest[: -1 - parts - split], rest[-1 - parts - split : -1], rest[-1]
    total[...] = jnp.zeros_like(total)
    for slot in range(2):

        def step(i, carry, slot=slot):
            at = pl.multiple_of(i * tile, tile)
            if split:
                left = [lefts[2 * j + slot][pl.ds(at, tile), :] for j in range(chunks)]
            else:
                left = [lefts[j][slot, pl.ds(at, tile), :] for j in range(chunks)]
            left = jnp.concatenate(left, axis=1)
            if split and slot == 1:
                outs[parts][pl.ds(at, tile), :] = left
            total[...] += dot(left, rights[slot][pl.ds(at, tile), :], 0, 0)
            return carry

        lax.fori_loop(0, rights[slot].shape[0] // tile, step, 0)
    columns = outs[0].shape[1]
    for k in range(parts):
        if split:
            start = pl.multiple_of((meta[0] ^ k) * columns, columns)
            outs[k][...] = total[:, pl.ds(start, columns)].astype(outs[k].dtype)
            continue
        rows = total.shape[0] // parts
        start = pl.multiple_of((meta[0] ^ k) * rows, rows)
        outs[k][:rows, :] = total[pl.ds(start, rows), :].astype(outs[k].dtype)
        few = taps // parts
        spot = 0
        for kernel in kernels:
            for low in range(0, LANES, taps):
                for tap in range(2):
                    start = pl.multiple_of(low + (meta[0] ^ k) * few, 8)
                    top, left = rows + spot // columns * few, spot % columns
                    outs[k][top : top + few, left : left + LANES] = kernel[
                        tap, pl.ds(start, few), :
                    ].astype(outs[k].dtype)
                    spot += LANES


def signal_body(tile, base, *rest):
    target, lanes = rest[-1], rest[-2].shape[1] // 2
    low = 0 if target.dtype == F32 else lanes
    side, side_far = (x[:, low : low + lanes] for x in rest[-3:-1])
    mixes, other = rest[:-4], rest[-4]

    def step(i, carry):
        at = pl.multiple_of(i * tile, tile)
        mix = jnp.concatenate([x[pl.ds(at, tile), :] for x in mixes], axis=1)
        acc = base[pl.ds(at, tile), :].astype(F32) + dot(mix, side, 1, 1)
        acc = acc + dot(other[pl.ds(at, tile), :], side_far, 1, 1)
        target[pl.ds(at, tile), :] = acc.astype(target.dtype)
        return carry

    lax.fori_loop(0, base.shape[0] // tile, step, 0)


def tree(values):
    while len(values) > 1:
        values = [values[i] + values[i + 1] for i in range(0, len(values), 2)]
    return values[0]


def split_body(count, parts, meta, *rest):
    ins, outs, total = rest[:count], rest[count:-1], rest[-1]
    total[...] = tree([x[...].astype(F32) for x in ins])
    rows = outs[0].shape[0]
    for k in range(parts):
        at = pl.multiple_of((meta[1] ^ k) * rows, rows)
        outs[k][...] = total[pl.ds(at, rows), :].astype(outs[k].dtype)


def gather_body(count, chips, few, meta, *rest):
    first, second = rest[:count], rest[count : 2 * count]
    outs, (sum_one, sum_two) = rest[2 * count : -2], rest[-2:]
    sum_one[...] = tree([x[...].astype(F32) for x in first])
    sum_two[...] = tree([x[...].astype(F32) for x in second])
    width, wide = sum_one.shape[1], sum_two.shape[1]
    one = sum_one.shape[0] // chips
    flat = sum_two.shape[0] - 2 * LANES * chips * few // wide
    two = flat // chips
    for k in range(chips):
        at, kind = meta[1] ^ k, outs[k].dtype
        outs[k][:one, :] = sum_one[pl.ds(pl.multiple_of(at * one, 8), one), :].astype(kind)
        block = sum_two[pl.ds(pl.multiple_of(at * two, 8), two), :].astype(kind)
        top = one
        for n in range(wide // width):
            outs[k][top : top + two, :] = block[:, n * width : (n + 1) * width]
            top += two
        each = wide // (2 * LANES)
        row = pl.multiple_of(flat + at // each * few, 8)
        lane = pl.multiple_of(at % each * (2 * LANES), 2 * LANES)
        block = sum_two[pl.ds(row, few), pl.ds(lane, 2 * LANES)].astype(kind)
        for n in range(2 * LANES // width):
            outs[k][top : top + few, :] = block[:, n * width : (n + 1) * width]
            top += few


def divide_body(count, *rest):
    got = tree([x[...].astype(F32) for x in rest[:count]]).astype(BF)
    rows = rest[count].shape[0]
    rest[count][...] = got[:rows, :]
    rest[count + 1][...] = got[rows:, :]


def sum_body(count, factor, *rest):
    got = tree([x[...].astype(F32) for x in rest[:count]])
    rest[count][...] = (got if factor is None else got * factor).astype(rest[count].dtype)


def pack_body(count, meta, *rest):
    out = rest[-1]
    rows = rest[0].shape[0]
    for k in range(count):
        out[meta[1] ^ k, :rows, :] = rest[k][...]
        out[meta[1] ^ k, rows:, :] = rest[count + k][...]


def share_body(parts, skip, meta, whole, out):
    piece = whole.shape[1] // (2 * parts)
    got = []
    for f in range(skip // piece, parts):
        both = whole[:, 2 * f * piece : 2 * (f + 1) * piece]
        got.append(jnp.where(meta[2] == 0, both[:, :piece], both[:, piece:]))
    out[...] = jnp.concatenate(got, axis=1)


def taps_body(chips, groups, meta, *rest):
    delays, blocks = rest[:chips], rest[chips : 2 * chips]
    amounts, outs = rest[2 * chips], rest[2 * chips + 1 :]
    width = LANES // 2
    for out in outs:
        out[...] = jnp.zeros_like(out)
    for k in range(chips):
        at = meta[1] ^ k
        for n in range(groups):
            group = at * groups + n
            amounts[group] = delays[k][n]
            for spot in range(2 * len(outs)):

                @pl.when(group == spot)
                def _(k=k, n=n, spot=spot):
                    out, g = outs[spot // 2], spot % 2
                    for tap in range(2):
                        top = tap * LANES + g * width
                        block = blocks[k][tap, n * width : (n + 1) * width, :].astype(F32)
                        lane = lax.broadcasted_iota(jnp.int32, block.shape, 1)
                        here = (lane < width) == (g == 0)
                        other = pltpu.roll(block, width, 1)
                        left, right = (block, other) if g == 0 else (other, block)
                        zero = jnp.zeros_like(block)
                        out[top : top + width, :LANES] = jnp.where(here, left, zero).astype(BF)
                        out[top : top + width, LANES:] = jnp.where(here, right, zero).astype(BF)


def local_step(signal, cotangent, w_in, w_conv, w_out, dilation, lengths):
    record, upstream = signal[0], cotangent[0]
    samples, channels = record.shape
    seq_size, fsdp_size = lax.axis_size("seq"), lax.axis_size("fsdp")
    chips = seq_size // 2
    seq_at, fsdp_at = lax.axis_index("seq"), lax.axis_index("fsdp")
    core, chip = seq_at % 2, seq_at // 2
    factor = 1.0 / math.sqrt(samples * seq_size * fsdp_size)
    block = 2 * samples
    hops = -(-MAX_DILATION // block)
    share = channels // 2
    piece = share // fsdp_size
    conv_chans = w_conv.shape[1]
    local_groups = dilation.shape[0]
    width = conv_chans // local_groups
    assert 2 * width == LANES and chips == fsdp_size and piece == conv_chans
    chunks = share // LANES

    def to_partner(x):
        return lax.ppermute(x, "seq", [(i, i ^ 1) for i in range(seq_size)])

    def from_fsdp(blocks):
        got = [blocks[0]]
        for k in range(1, fsdp_size):
            pairs = [(i, i ^ k) for i in range(fsdp_size)]
            got.append(lax.ppermute(blocks[k], "fsdp", pairs))
        return got

    def from_chips(blocks):
        got = [blocks[0]]
        for k in range(1, chips):
            pairs = [(i, i ^ (2 * k)) for i in range(seq_size)]
            got.append(lax.ppermute(blocks[k], "seq", pairs))
        return got

    def up(x, hop):
        return lax.ppermute(x, "seq", [(i, i + 2) for i in range(2 * (hop - 1), seq_size - 2)])

    def down(x, hop):
        return lax.ppermute(x, "seq", [(i + 2, i) for i in range(seq_size - 2 * hop)])

    where = jnp.stack([fsdp_at, chip, core, lengths[0] - chip * block]).astype(jnp.int32)
    wides = [share // 2, share // 2]
    lead_share = jnp.concatenate(
        [
            lax.dynamic_slice_in_dim(w_in, (2 * f + core) * piece, piece, 1)
            for f in range(LANES // piece)
        ],
        axis=1,
    )
    (rest_share,) = call(
        functools.partial(share_body, fsdp_size, LANES),
        [shape((w_in.shape[0], share - LANES), BF)],
        [where, w_in],
    )
    in_shares = [lead_share, rest_share]
    out_share = lax.dynamic_index_in_dim(
        w_out.reshape(2, piece, channels), core, 0, keepdims=False
    )
    record_far = to_partner(record)
    in_parts = [from_fsdp([x] * fsdp_size) for x in in_shares]
    upstream_far = to_partner(upstream)
    out_parts = from_fsdp([out_share] * fsdp_size)
    delays = from_chips([dilation] * chips)
    conv_parts = from_chips([w_conv] * chips)
    taps = call(
        functools.partial(taps_body, chips, local_groups),
        [shape((2 * chunks,), jnp.int32)] + [shape((2 * LANES, 2 * LANES), BF)] * chunks,
        [where] + delays + conv_parts,
        scalars=1 + chips,
        small=1,
    )
    amounts, kernels = taps[0], taps[1:]

    series = shape((2, samples, LANES), BF)
    tile = min(512, samples)
    first, lead = call(
        functools.partial(first_body, fsdp_size, tile),
        [series, shape((channels, LANES), BF)],
        [where, record, record_far] + in_parts[0],
        scratch=[pltpu.VMEM((samples, channels), BF), pltpu.SemaphoreType.DMA],
        flops=2 * block * channels * LANES,
        stay=(1,),
    )
    got = call(
        functools.partial(product_body, fsdp_size, tile, False, LANES),
        [series] * (chunks - 1) + [shape((channels, share), BF)],
        [where, record, record_far] + in_parts[1] + [lead],
        flops=2 * block * channels * (share - LANES),
    )
    projected, panel = (first,) + got[:-1], got[-1]
    grad_gated = call(
        functools.partial(product_body, fsdp_size, tile, True, 0),
        [series] * chunks,
        [where, upstream, upstream_far] + out_parts,
        scratch=[pltpu.VMEM((share, channels), BF)],
        flops=2 * block * channels * share,
    )
    panel_far = to_partner(panel)

    tile = min(256, samples)
    gated, own_mixed, far_mixed, kernel_grads = [], [], [], []
    long = pltpu.VMEM((2 * (hops + 1) * samples, LANES), F32)
    for j in range(chunks):
        chain = [projected[j]]
        for hop in range(1, hops + 1):
            chain.append(up(chain[-1], hop))
        out, tap_zero, tap_one, grad_kernel = call(
            functools.partial(conv_body, hops, tile, j),
            [series, shape((2, samples, LANES), F32), series, shape((2, LANES, LANES), F32)],
            [where, amounts] + chain + [grad_gated[j], kernels[j]],
            scratch=[long, pltpu.VMEM((2 * LANES, 2 * LANES), F32)],
            flops=6 * block * 4 * LANES * LANES,
            scalars=2,
        )
        gated.append(out)
        kernel_grads.append(grad_kernel)
        back = [tap_one]
        for hop in range(1, hops + 1):
            back.append(down(back[-1], hop))
        own, other = call(
            functools.partial(mixed_body, hops, tile, j),
            [shape((samples, LANES), BF)] * 2,
            [where, amounts, tap_zero] + back,
            scratch=[long],
            scalars=2,
        )
        own_mixed.append(own)
        far_mixed.append(other)

    tile = min(512, samples)

    few = conv_chans // fsdp_size

    def outer(lefts, rights, split):
        count = len(lefts) // 2 if split else len(lefts)
        rows, columns = LANES * count, channels
        more = [] if split else kernel_grads
        tall = piece + 2 * LANES * chips * few // channels
        one = (rows, columns // fsdp_size) if split else (tall, columns)
        return call(
            functools.partial(outer_body, count, fsdp_size, tile, split, conv_chans),
            [shape(one, F32)]
            + [shape(one, BF)] * (fsdp_size - 1)
            + ([shape((samples, rows), BF)] if split else []),
            [where] + list(lefts) + list(rights) + more,
            scratch=[pltpu.VMEM((rows, columns), F32)],
            flops=2 * block * rows * columns,
        )

    mixed_in, flats = [], []
    for pick in (range(chunks // 2), range(chunks // 2, chunks)):
        sides = []
        for j in pick:
            sides += [own_mixed[j], far_mixed[j]]
        got = outer(sides, (record, record_far), True)
        mixed_in.append(to_partner(got[-1]))
        flats.append(from_fsdp(got[:fsdp_size]))
    got = outer(gated, (upstream, upstream_far), False)
    flat_out = from_fsdp(got)

    own_rows = channels // fsdp_size
    in_part, out_part = wides[0] // chips, piece // chips
    panel_rows = in_part + out_part * (channels // own_rows)
    kernel_rows = 2 * LANES * few // own_rows
    whole = (panel_rows + kernel_rows, own_rows)
    cut = call(
        functools.partial(gather_body, fsdp_size, chips, few),
        [shape(whole, F32)] + [shape(whole, BF)] * (chips - 1),
        [where] + flats[0] + flat_out,
        scratch=[pltpu.VMEM((wides[0], own_rows), F32), pltpu.VMEM(flat_out[0].shape, F32)],
    )
    mine, mine_kernel = call(
        functools.partial(divide_body, chips),
        [shape((panel_rows, own_rows), BF), shape((kernel_rows, own_rows), BF)],
        from_chips(cut),
        scalars=0,
    )
    kernel_parts = from_fsdp([mine_kernel] * fsdp_size)
    gathered = from_chips([mine] * chips)

    last = (wides[1] // chips, own_rows)
    cut = call(
        functools.partial(split_body, fsdp_size, chips),
        [shape(last, F32)] + [shape(last, BF)] * (chips - 1),
        [where] + flats[1],
        scratch=[pltpu.VMEM((wides[1], own_rows), F32)],
    )
    (mine,) = call(
        functools.partial(sum_body, chips, None), [shape(last, BF)], from_chips(cut), scalars=0
    )
    gathered += from_chips([mine] * chips)
    (packed,) = call(
        functools.partial(pack_body, chips),
        [shape((chips, panel_rows + last[0], own_rows), BF)],
        [where] + gathered,
    )
    finals = [packed, to_partner(packed)]

    tile = min(256, samples)

    total = upstream
    for n in range(2):
        (total,) = call(
            functools.partial(signal_body, tile),
            [shape((samples, channels), BF if n else F32)],
            [total] + own_mixed[n * chunks // 2 :][: chunks // 2] + [mixed_in[n], panel, panel_far],
            scalars=0,
            flops=samples * channels * channels,
        )
    grad_signal = total

    def finish_body(meta, *rest):
        packs, parts = rest[:2], rest[2 : 2 + fsdp_size]
        grad_in, grad_out, grad_conv, turned = rest[2 + fsdp_size :]
        core_at = meta[2]
        for side in range(2):
            first = packs[side][...].astype(F32) * factor
            for p in range(chips):
                at = pl.multiple_of((side ^ core_at) * piece + p * out_part, 8)
                for n in range(channels // own_rows):
                    top = in_part + n * out_part
                    grad_out[pl.ds(at, out_part), n * own_rows : (n + 1) * own_rows] = first[
                        p, top : top + out_part, :
                    ]
                at = p * in_part
                turned[side ^ core_at, at : at + in_part, :] = first[p, :in_part, :]
                at, rows = wides[0] + p * last[0], last[0]
                turned[side ^ core_at, at : at + rows, :] = first[p, panel_rows:, :]
        for f in range(fsdp_size):
            pair = [turned[c, f * piece : (f + 1) * piece, :] for c in range(2)]
            grad_in[:, 2 * f * piece : 2 * (f + 1) * piece] = jnp.concatenate(pair, axis=0).T
        for k, x in enumerate(parts):
            total = x[...].astype(F32) * factor
            at = pl.multiple_of((meta[0] ^ k) * few, 8)
            for tap in range(2):
                left, top = (tap * LANES) % own_rows, (tap * LANES) // own_rows * few
                grad_conv[tap, pl.ds(at, few), :] = total[top : top + few, left : left + LANES]

    grad_in, grad_out, grad_conv = call(
        finish_body,
        [shape((own_rows, channels), F32)] * 2 + [shape((2, conv_chans, LANES), F32)],
        [where] + finals + kernel_parts,
        scratch=[pltpu.VMEM((2, share, own_rows), F32)],
    )
    return (grad_signal[None], grad_in, grad_out, grad_conv)


def solution(mesh):
    placed = (
        P("fsdp", "seq", None),
        P("fsdp", "seq", None),
        P("fsdp", None),
        P(None, "seq", None),
        P("fsdp", None),
        P("seq"),
        P("fsdp"),
    )
    return jax.shard_map(
        local_step,
        mesh=mesh,
        in_specs=placed,
        out_specs=(P("fsdp", "seq", None), P("fsdp", None), P("fsdp", None), P(None, "seq", None)),
        check_vma=False,
    )
```

```python
import functools
import math

import jax
import jax.numpy as jnp
from jax import lax
from jax.experimental import pallas as pl
from jax.experimental.pallas import tpu as pltpu
from jax.sharding import PartitionSpec as P


MAX_DILATION = 4095
LANES = 128
BF = jnp.bfloat16
F32 = jnp.float32
VM = pl.BlockSpec(memory_space=pltpu.VMEM)
SM = pl.BlockSpec(memory_space=pltpu.SMEM)
FAR = pl.BlockSpec(memory_space=pltpu.HBM)


def dot(a, b, ca, cb):
    return lax.dot_general(a, b, (((ca,), (cb,)), ((), ())), preferred_element_type=F32)


def call(body, outs, ins, scratch=(), flops=0, scalars=1, small=0, stay=()):
    moved = sum(math.prod(x.shape) * x.dtype.itemsize for x in list(ins) + list(outs))
    return pl.pallas_call(
        body,
        out_shape=tuple(outs),
        in_specs=[SM if n < scalars else FAR if n in stay else VM for n in range(len(ins))],
        out_specs=tuple([SM] * small + [VM] * (len(outs) - small)),
        scratch_shapes=list(scratch),
        cost_estimate=pl.CostEstimate(flops=flops, bytes_accessed=moved, transcendentals=0),
        compiler_params=pltpu.CompilerParams(vmem_limit_bytes=20 * 1024 * 1024),
    )(*ins)


def shape(dims, kind):
    return jax.ShapeDtypeStruct(dims, kind)


def product_body(parts, tile, turned, skip, meta, own, partner, *rest):
    weights, outs = rest[:parts], rest[parts:]
    if skip:
        outs[-1][:, :skip] = outs[0][...]
        outs = outs[1:]
    targets, panel = outs[:-1], outs[-1]
    rows = weights[0].shape[0]
    for k in range(parts):
        start = pl.multiple_of((meta[0] ^ k) * rows, rows)
        panel[pl.ds(start, rows), skip:] = weights[k][...]
    for slot, source in enumerate((own, partner)):

        def step(i, carry, slot=slot, source=source):
            at = pl.multiple_of(i * tile, tile)
            side = panel[:, skip:]
            got = dot(source[pl.ds(at, tile), :], side, 1, int(turned)).astype(BF)
            for j, target in enumerate(targets):
                target[slot, pl.ds(at, tile), :] = got[:, j * LANES : (j + 1) * LANES]
            return carry

        lax.fori_loop(0, source.shape[0] // tile, step, 0)


def first_body(parts, tile, meta, own, partner, *rest):
    held, sem = rest[-2:]
    copy = pltpu.make_async_copy(own, held, sem)
    copy.start()
    weights, (target, panel) = rest[:parts], rest[parts:-2]
    rows = weights[0].shape[0]
    for k in range(parts):
        start = pl.multiple_of((meta[0] ^ k) * rows, rows)
        panel[pl.ds(start, rows), :] = weights[k][...]
    for slot, source in ((1, partner), (0, held)):
        if slot == 0:
            copy.wait()

        def step(i, carry, slot=slot, source=source):
            at = pl.multiple_of(i * tile, tile)
            got = dot(source[pl.ds(at, tile), :], panel[...], 1, 0).astype(BF)
            target[slot, pl.ds(at, tile), :] = got
            return carry

        lax.fori_loop(0, source.shape[0] // tile, step, 0)


def select_lanes(a, b):
    lane = lax.broadcasted_iota(jnp.int32, a.shape, 1)
    return jnp.where(lane < LANES // 2, a, b)


def conv_body(hops, tile, pair, meta, amounts, *rest):
    sources, rest = rest[: hops + 1], rest[hops + 1 :]
    upstream, kernel, gated, acts, late, tap_one, series = rest
    half = sources[0].shape[1]
    core, alive = meta[2], meta[3]
    late_a, late_b = amounts[2 * pair], amounts[2 * pair + 1]
    for n in range(hops + 1):
        for h in range(2):
            series[(2 * (hops - n) + h) * half : (2 * (hops - n) + h + 1) * half, :] = (
                sources[n][h ^ core].astype(F32)
            )
    per_half = half // tile

    def step(i, carry):
        slot = (i // per_half) ^ core
        row = pl.multiple_of((i % per_half) * tile, tile)
        start = 2 * hops * half + i * tile
        before = select_lanes(
            series[pl.ds(start - late_a, tile), :], series[pl.ds(start - late_b, tile), :]
        ).astype(BF)
        late[slot, pl.ds(row, tile), :] = before
        stacked = jnp.concatenate([sources[0][slot, pl.ds(row, tile), :], before], axis=1)
        pre = dot(stacked, kernel[...], 1, 0)
        tanh_act = jnp.tanh(pre[:, :LANES])
        sig_act = jax.nn.sigmoid(pre[:, LANES:])
        moment = i * tile + lax.broadcasted_iota(jnp.int32, tanh_act.shape, 0)
        mask = (moment < alive).astype(F32)
        gated[slot, pl.ds(row, tile), :] = (tanh_act * sig_act * mask).astype(BF)
        masked = upstream[slot, pl.ds(row, tile), :].astype(F32) * mask
        grad_filter = masked * sig_act * (1.0 - tanh_act * tanh_act)
        grad_gate = masked * tanh_act * sig_act * (1.0 - sig_act)
        both = jnp.concatenate([grad_filter.astype(BF), grad_gate.astype(BF)], axis=1)
        acts[slot, pl.ds(row, tile), :] = both
        tap_one[slot, pl.ds(row, tile), :] = dot(both, kernel[LANES:, :], 1, 1).astype(BF)
        return carry

    lax.fori_loop(0, 2 * per_half, step, 0)


def taps_grad_body(tile, own, late, acts, kernel, tap_zero, grad_kernel, total):
    total[...] = jnp.zeros_like(total)
    for slot in range(2):

        def step(i, carry, slot=slot):
            row = pl.multiple_of(i * tile, tile)
            both = acts[slot, pl.ds(row, tile), :]
            stacked = jnp.concatenate(
                [own[slot, pl.ds(row, tile), :], late[slot, pl.ds(row, tile), :]], axis=1
            )
            total[...] += dot(stacked, both, 0, 0)
            tap_zero[slot, pl.ds(row, tile), :] = dot(both, kernel[:LANES, :], 1, 1)
            return carry

        lax.fori_loop(0, own.shape[1] // tile, step, 0)
    width = LANES // 2
    for tap in range(2):
        for g in range(2):
            top = tap * LANES + g * width
            left = total[top : top + width, :LANES]
            right = total[top : top + width, LANES:]
            if g == 0:
                right = pltpu.roll(right, width, 1)
            else:
                left = pltpu.roll(left, width, 1)
            grad_kernel[tap, g * width : (g + 1) * width, :] = select_lanes(left, right)


def mixed_body(hops, tile, pair, meta, amounts, tap_zero, *rest):
    sources, (own, partner, series) = rest[: hops + 1], rest[hops + 1 :]
    half = tap_zero.shape[1]
    core = meta[2]
    early_a, early_b = amounts[2 * pair], amounts[2 * pair + 1]
    for n in range(hops + 1):
        for h in range(2):
            series[(2 * n + h) * half : (2 * n + h + 1) * half, :] = sources[n][h ^ core].astype(
                F32
            )
    for slot, target in ((0, own), (1, partner)):

        def step(i, carry, slot=slot, target=target):
            row = pl.multiple_of(i * tile, tile)
            start = (slot ^ core) * half + row
            early = select_lanes(
                series[pl.ds(start + early_a, tile), :], series[pl.ds(start + early_b, tile), :]
            )
            target[pl.ds(row, tile), :] = (tap_zero[slot, pl.ds(row, tile), :] + early).astype(BF)
            return carry

        lax.fori_loop(0, half // tile, step, 0)


def outer_body(chunks, parts, tile, split, taps, meta, *rest):
    count = chunks * (2 if split else 1)
    lefts, rest = rest[:count], rest[count:]
    rights, rest = rest[:2], rest[2:]
    kernels, outs, total = rest[: -1 - parts - split], rest[-1 - parts - split : -1], rest[-1]
    total[...] = jnp.zeros_like(total)
    for slot in range(2):

        def step(i, carry, slot=slot):
            at = pl.multiple_of(i * tile, tile)
            if split:
                left = [lefts[2 * j + slot][pl.ds(at, tile), :] for j in range(chunks)]
            else:
                left = [lefts[j][slot, pl.ds(at, tile), :] for j in range(chunks)]
            left = jnp.concatenate(left, axis=1)
            if split and slot == 1:
                outs[parts][pl.ds(at, tile), :] = left
            total[...] += dot(left, rights[slot][pl.ds(at, tile), :], 0, 0)
            return carry

        lax.fori_loop(0, rights[slot].shape[0] // tile, step, 0)
    columns = outs[0].shape[1]
    for k in range(parts):
        if split:
            start = pl.multiple_of((meta[0] ^ k) * columns, columns)
            outs[k][...] = total[:, pl.ds(start, columns)].astype(outs[k].dtype)
            continue
        rows = total.shape[0] // parts
        start = pl.multiple_of((meta[0] ^ k) * rows, rows)
        outs[k][:rows, :] = total[pl.ds(start, rows), :].astype(outs[k].dtype)
        few = taps // parts
        spot = 0
        for kernel in kernels:
            for low in range(0, LANES, taps):
                for tap in range(2):
                    start = pl.multiple_of(low + (meta[0] ^ k) * few, 8)
                    top, left = rows + spot // columns * few, spot % columns
                    outs[k][top : top + few, left : left + LANES] = kernel[
                        tap, pl.ds(start, few), :
                    ].astype(outs[k].dtype)
                    spot += LANES


def signal_body(tile, base, *rest):
    target, lanes = rest[-1], rest[-2].shape[1] // 2
    low = 0 if target.dtype == F32 else lanes
    side, side_far = (x[:, low : low + lanes] for x in rest[-3:-1])
    mixes, other = rest[:-4], rest[-4]

    def step(i, carry):
        at = pl.multiple_of(i * tile, tile)
        mix = jnp.concatenate([x[pl.ds(at, tile), :] for x in mixes], axis=1)
        acc = base[pl.ds(at, tile), :].astype(F32) + dot(mix, side, 1, 1)
        acc = acc + dot(other[pl.ds(at, tile), :], side_far, 1, 1)
        target[pl.ds(at, tile), :] = acc.astype(target.dtype)
        return carry

    lax.fori_loop(0, base.shape[0] // tile, step, 0)


def tree(values):
    while len(values) > 1:
        values = [values[i] + values[i + 1] for i in range(0, len(values), 2)]
    return values[0]


def split_body(count, parts, meta, *rest):
    ins, outs, total = rest[:count], rest[count:-1], rest[-1]
    total[...] = tree([x[...].astype(F32) for x in ins])
    rows = outs[0].shape[0]
    for k in range(parts):
        at = pl.multiple_of((meta[1] ^ k) * rows, rows)
        outs[k][...] = total[pl.ds(at, rows), :].astype(outs[k].dtype)


def gather_body(count, chips, few, meta, *rest):
    first, second = rest[:count], rest[count : 2 * count]
    outs, (sum_one, sum_two) = rest[2 * count : -2], rest[-2:]
    sum_one[...] = tree([x[...].astype(F32) for x in first])
    sum_two[...] = tree([x[...].astype(F32) for x in second])
    width, wide = sum_one.shape[1], sum_two.shape[1]
    one = sum_one.shape[0] // chips
    flat = sum_two.shape[0] - 2 * LANES * chips * few // wide
    two = flat // chips
    for k in range(chips):
        at, kind = meta[1] ^ k, outs[k].dtype
        outs[k][:one, :] = sum_one[pl.ds(pl.multiple_of(at * one, 8), one), :].astype(kind)
        block = sum_two[pl.ds(pl.multiple_of(at * two, 8), two), :].astype(kind)
        top = one
        for n in range(wide // width):
            outs[k][top : top + two, :] = block[:, n * width : (n + 1) * width]
            top += two
        each = wide // (2 * LANES)
        row = pl.multiple_of(flat + at // each * few, 8)
        lane = pl.multiple_of(at % each * (2 * LANES), 2 * LANES)
        block = sum_two[pl.ds(row, few), pl.ds(lane, 2 * LANES)].astype(kind)
        for n in range(2 * LANES // width):
            outs[k][top : top + few, :] = block[:, n * width : (n + 1) * width]
            top += few


def divide_body(count, *rest):
    got = tree([x[...].astype(F32) for x in rest[:count]]).astype(BF)
    rows = rest[count].shape[0]
    rest[count][...] = got[:rows, :]
    rest[count + 1][...] = got[rows:, :]


def sum_body(count, factor, *rest):
    got = tree([x[...].astype(F32) for x in rest[:count]])
    rest[count][...] = (got if factor is None else got * factor).astype(rest[count].dtype)


def pack_body(count, meta, *rest):
    out = rest[-1]
    rows = rest[0].shape[0]
    for k in range(count):
        out[meta[1] ^ k, :rows, :] = rest[k][...]
        out[meta[1] ^ k, rows:, :] = rest[count + k][...]


def share_body(parts, skip, meta, whole, out):
    piece = whole.shape[1] // (2 * parts)
    got = []
    for f in range(skip // piece, parts):
        both = whole[:, 2 * f * piece : 2 * (f + 1) * piece]
        got.append(jnp.where(meta[2] == 0, both[:, :piece], both[:, piece:]))
    out[...] = jnp.concatenate(got, axis=1)


def taps_body(chips, groups, meta, *rest):
    delays, blocks = rest[:chips], rest[chips : 2 * chips]
    amounts, outs = rest[2 * chips], rest[2 * chips + 1 :]
    width = LANES // 2
    for out in outs:
        out[...] = jnp.zeros_like(out)
    for k in range(chips):
        at = meta[1] ^ k
        for n in range(groups):
            group = at * groups + n
            amounts[group] = delays[k][n]
            for spot in range(2 * len(outs)):

                @pl.when(group == spot)
                def _(k=k, n=n, spot=spot):
                    out, g = outs[spot // 2], spot % 2
                    for tap in range(2):
                        top = tap * LANES + g * width
                        block = blocks[k][tap, n * width : (n + 1) * width, :].astype(F32)
                        lane = lax.broadcasted_iota(jnp.int32, block.shape, 1)
                        here = (lane < width) == (g == 0)
                        other = pltpu.roll(block, width, 1)
                        left, right = (block, other) if g == 0 else (other, block)
                        zero = jnp.zeros_like(block)
                        out[top : top + width, :LANES] = jnp.where(here, left, zero).astype(BF)
                        out[top : top + width, LANES:] = jnp.where(here, right, zero).astype(BF)


def local_step(signal, cotangent, w_in, w_conv, w_out, dilation, lengths):
    record, upstream = signal[0], cotangent[0]
    samples, channels = record.shape
    seq_size, fsdp_size = lax.axis_size("seq"), lax.axis_size("fsdp")
    chips = seq_size // 2
    seq_at, fsdp_at = lax.axis_index("seq"), lax.axis_index("fsdp")
    core, chip = seq_at % 2, seq_at // 2
    factor = 1.0 / math.sqrt(samples * seq_size * fsdp_size)
    block = 2 * samples
    hops = -(-MAX_DILATION // block)
    share = channels // 2
    piece = share // fsdp_size
    conv_chans = w_conv.shape[1]
    local_groups = dilation.shape[0]
    width = conv_chans // local_groups
    assert 2 * width == LANES and chips == fsdp_size and piece == conv_chans
    chunks = share // LANES

    def to_partner(x):
        return lax.ppermute(x, "seq", [(i, i ^ 1) for i in range(seq_size)])

    def from_fsdp(blocks):
        got = [blocks[0]]
        for k in range(1, fsdp_size):
            pairs = [(i, i ^ k) for i in range(fsdp_size)]
            got.append(lax.ppermute(blocks[k], "fsdp", pairs))
        return got

    def from_chips(blocks):
        got = [blocks[0]]
        for k in range(1, chips):
            pairs = [(i, i ^ (2 * k)) for i in range(seq_size)]
            got.append(lax.ppermute(blocks[k], "seq", pairs))
        return got

    def up(x, hop):
        return lax.ppermute(x, "seq", [(i, i + 2) for i in range(2 * (hop - 1), seq_size - 2)])

    def down(x, hop):
        return lax.ppermute(x, "seq", [(i + 2, i) for i in range(seq_size - 2 * hop)])

    where = jnp.stack([fsdp_at, chip, core, lengths[0] - chip * block]).astype(jnp.int32)
    wides = [share // 2, share // 2]
    lead_share = jnp.concatenate(
        [
            lax.dynamic_slice_in_dim(w_in, (2 * f + core) * piece, piece, 1)
            for f in range(LANES // piece)
        ],
        axis=1,
    )
    (rest_share,) = call(
        functools.partial(share_body, fsdp_size, LANES),
        [shape((w_in.shape[0], share - LANES), BF)],
        [where, w_in],
    )
    in_shares = [lead_share, rest_share]
    out_share = lax.dynamic_index_in_dim(
        w_out.reshape(2, piece, channels), core, 0, keepdims=False
    )
    record_far = to_partner(record)
    in_parts = [from_fsdp([x] * fsdp_size) for x in in_shares]
    upstream_far = to_partner(upstream)
    out_parts = from_fsdp([out_share] * fsdp_size)
    delays = from_chips([dilation] * chips)
    conv_parts = from_chips([w_conv] * chips)
    taps = call(
        functools.partial(taps_body, chips, local_groups),
        [shape((2 * chunks,), jnp.int32)] + [shape((2 * LANES, 2 * LANES), BF)] * chunks,
        [where] + delays + conv_parts,
        scalars=1 + chips,
        small=1,
    )
    amounts, kernels = taps[0], taps[1:]

    series = shape((2, samples, LANES), BF)
    tile = min(512, samples)
    first, lead = call(
        functools.partial(first_body, fsdp_size, tile),
        [series, shape((channels, LANES), BF)],
        [where, record, record_far] + in_parts[0],
        scratch=[pltpu.VMEM((samples, channels), BF), pltpu.SemaphoreType.DMA],
        flops=2 * block * channels * LANES,
        stay=(1,),
    )
    got = call(
        functools.partial(product_body, fsdp_size, tile, False, LANES),
        [series] * (chunks - 1) + [shape((channels, share), BF)],
        [where, record, record_far] + in_parts[1] + [lead],
        flops=2 * block * channels * (share - LANES),
    )
    projected, panel = (first,) + got[:-1], got[-1]
    grad_gated = call(
        functools.partial(product_body, fsdp_size, tile, True, 0),
        [series] * chunks,
        [where, upstream, upstream_far] + out_parts,
        scratch=[pltpu.VMEM((share, channels), BF)],
        flops=2 * block * channels * share,
    )
    panel_far = to_partner(panel)

    tile = min(256, samples)
    gated, own_mixed, far_mixed, kernel_grads = [], [], [], []
    long = pltpu.VMEM((2 * (hops + 1) * samples, LANES), F32)
    for j in range(chunks):
        chain = [projected[j]]
        for hop in range(1, hops + 1):
            chain.append(up(chain[-1], hop))
        out, acts, late, tap_one = call(
            functools.partial(conv_body, hops, tile, j),
            [series, shape((2, samples, 2 * LANES), BF), series, series],
            [where, amounts] + chain + [grad_gated[j], kernels[j]],
            scratch=[long],
            flops=4 * block * 4 * LANES * LANES,
            scalars=2,
        )
        tap_zero, grad_kernel = call(
            functools.partial(taps_grad_body, 512 if samples % 512 == 0 else samples),
            [shape((2, samples, LANES), F32), shape((2, LANES, LANES), F32)],
            [projected[j], late, acts, kernels[j]],
            scratch=[pltpu.VMEM((2 * LANES, 2 * LANES), F32)],
            flops=4 * block * 4 * LANES * LANES,
            scalars=0,
        )
        gated.append(out)
        kernel_grads.append(grad_kernel)
        back = [tap_one]
        for hop in range(1, hops + 1):
            back.append(down(back[-1], hop))
        own, other = call(
            functools.partial(mixed_body, hops, tile, j),
            [shape((samples, LANES), BF)] * 2,
            [where, amounts, tap_zero] + back,
            scratch=[long],
            scalars=2,
        )
        own_mixed.append(own)
        far_mixed.append(other)

    tile = min(512, samples)

    few = conv_chans // fsdp_size

    def outer(lefts, rights, split):
        count = len(lefts) // 2 if split else len(lefts)
        rows, columns = LANES * count, channels
        more = [] if split else kernel_grads
        tall = piece + 2 * LANES * chips * few // channels
        one = (rows, columns // fsdp_size) if split else (tall, columns)
        return call(
            functools.partial(outer_body, count, fsdp_size, tile, split, conv_chans),
            [shape(one, F32)]
            + [shape(one, BF)] * (fsdp_size - 1)
            + ([shape((samples, rows), BF)] if split else []),
            [where] + list(lefts) + list(rights) + more,
            scratch=[pltpu.VMEM((rows, columns), F32)],
            flops=2 * block * rows * columns,
        )

    mixed_in, flats = [], []
    for pick in (range(chunks // 2), range(chunks // 2, chunks)):
        sides = []
        for j in pick:
            sides += [own_mixed[j], far_mixed[j]]
        got = outer(sides, (record, record_far), True)
        mixed_in.append(to_partner(got[-1]))
        flats.append(from_fsdp(got[:fsdp_size]))
    got = outer(gated, (upstream, upstream_far), False)
    flat_out = from_fsdp(got)

    own_rows = channels // fsdp_size
    in_part, out_part = wides[0] // chips, piece // chips
    panel_rows = in_part + out_part * (channels // own_rows)
    kernel_rows = 2 * LANES * few // own_rows
    whole = (panel_rows + kernel_rows, own_rows)
    cut = call(
        functools.partial(gather_body, fsdp_size, chips, few),
        [shape(whole, F32)] + [shape(whole, BF)] * (chips - 1),
        [where] + flats[0] + flat_out,
        scratch=[pltpu.VMEM((wides[0], own_rows), F32), pltpu.VMEM(flat_out[0].shape, F32)],
    )
    mine, mine_kernel = call(
        functools.partial(divide_body, chips),
        [shape((panel_rows, own_rows), BF), shape((kernel_rows, own_rows), BF)],
        from_chips(cut),
        scalars=0,
    )
    kernel_parts = from_fsdp([mine_kernel] * fsdp_size)
    gathered = from_chips([mine] * chips)

    last = (wides[1] // chips, own_rows)
    cut = call(
        functools.partial(split_body, fsdp_size, chips),
        [shape(last, F32)] + [shape(last, BF)] * (chips - 1),
        [where] + flats[1],
        scratch=[pltpu.VMEM((wides[1], own_rows), F32)],
    )
    (mine,) = call(
        functools.partial(sum_body, chips, None), [shape(last, BF)], from_chips(cut), scalars=0
    )
    gathered += from_chips([mine] * chips)
    (packed,) = call(
        functools.partial(pack_body, chips),
        [shape((chips, panel_rows + last[0], own_rows), BF)],
        [where] + gathered,
    )
    finals = [packed, to_partner(packed)]

    tile = min(256, samples)

    total = upstream
    for n in range(2):
        (total,) = call(
            functools.partial(signal_body, tile),
            [shape((samples, channels), BF if n else F32)],
            [total] + own_mixed[n * chunks // 2 :][: chunks // 2] + [mixed_in[n], panel, panel_far],
            scalars=0,
            flops=samples * channels * channels,
        )
    grad_signal = total

    def finish_body(meta, *rest):
        packs, parts = rest[:2], rest[2 : 2 + fsdp_size]
        grad_in, grad_out, grad_conv, turned = rest[2 + fsdp_size :]
        core_at = meta[2]
        for side in range(2):
            first = packs[side][...].astype(F32) * factor
            for p in range(chips):
                at = pl.multiple_of((side ^ core_at) * piece + p * out_part, 8)
                for n in range(channels // own_rows):
                    top = in_part + n * out_part
                    grad_out[pl.ds(at, out_part), n * own_rows : (n + 1) * own_rows] = first[
                        p, top : top + out_part, :
                    ]
                at = p * in_part
                turned[side ^ core_at, at : at + in_part, :] = first[p, :in_part, :]
                at, rows = wides[0] + p * last[0], last[0]
                turned[side ^ core_at, at : at + rows, :] = first[p, panel_rows:, :]
        for f in range(fsdp_size):
            pair = [turned[c, f * piece : (f + 1) * piece, :] for c in range(2)]
            grad_in[:, 2 * f * piece : 2 * (f + 1) * piece] = jnp.concatenate(pair, axis=0).T
        for k, x in enumerate(parts):
            total = x[...].astype(F32) * factor
            at = pl.multiple_of((meta[0] ^ k) * few, 8)
            for tap in range(2):
                left, top = (tap * LANES) % own_rows, (tap * LANES) // own_rows * few
                grad_conv[tap, pl.ds(at, few), :] = total[top : top + few, left : left + LANES]

    grad_in, grad_out, grad_conv = call(
        finish_body,
        [shape((own_rows, channels), F32)] * 2 + [shape((2, conv_chans, LANES), F32)],
        [where] + finals + kernel_parts,
        scratch=[pltpu.VMEM((2, share, own_rows), F32)],
    )
    return (grad_signal[None], grad_in, grad_out, grad_conv)


def solution(mesh):
    placed = (
        P("fsdp", "seq", None),
        P("fsdp", "seq", None),
        P("fsdp", None),
        P(None, "seq", None),
        P("fsdp", None),
        P("seq"),
        P("fsdp"),
    )
    return jax.shard_map(
        local_step,
        mesh=mesh,
        in_specs=placed,
        out_specs=(P("fsdp", "seq", None), P("fsdp", None), P("fsdp", None), P(None, "seq", None)),
        check_vma=False,
    )
```

```python
import functools
import math

import jax
import jax.numpy as jnp
from jax import lax
from jax.experimental import pallas as pl
from jax.experimental.pallas import tpu as pltpu
from jax.sharding import PartitionSpec as P


MAX_DILATION = 4095
LANES = 128
NOTE = 16
BF = jnp.bfloat16
F32 = jnp.float32
VM = pl.BlockSpec(memory_space=pltpu.VMEM)
SM = pl.BlockSpec(memory_space=pltpu.SMEM)
FAR = pl.BlockSpec(memory_space=pltpu.HBM)


def dot(a, b, ca, cb):
    return lax.dot_general(a, b, (((ca,), (cb,)), ((), ())), preferred_element_type=F32)


def call(body, outs, ins, scratch=(), flops=0, scalars=1, small=0, stay=()):
    moved = sum(math.prod(x.shape) * x.dtype.itemsize for x in list(ins) + list(outs))
    return pl.pallas_call(
        body,
        out_shape=tuple(outs),
        in_specs=[SM if n < scalars else FAR if n in stay else VM for n in range(len(ins))],
        out_specs=tuple([SM] * small + [VM] * (len(outs) - small)),
        scratch_shapes=list(scratch),
        cost_estimate=pl.CostEstimate(flops=flops, bytes_accessed=moved, transcendentals=0),
        compiler_params=pltpu.CompilerParams(vmem_limit_bytes=20 * 1024 * 1024),
    )(*ins)


def shape(dims, kind):
    return jax.ShapeDtypeStruct(dims, kind)


def product_body(parts, tile, turned, skip, meta, own, partner, *rest):
    weights, outs = rest[:parts], rest[parts:]
    if skip:
        outs[-1][:, :skip] = outs[0][...]
        outs = outs[1:]
    targets, panel = outs[:-1], outs[-1]
    rows = weights[0].shape[0]
    for k in range(parts):
        start = pl.multiple_of((meta[0] ^ k) * rows, rows)
        panel[pl.ds(start, rows), skip:] = weights[k][...]
    for slot, source in enumerate((own, partner)):

        def step(i, carry, slot=slot, source=source):
            at = pl.multiple_of(i * tile, tile)
            side = panel[:, skip:]
            got = dot(source[pl.ds(at, tile), :], side, 1, int(turned)).astype(BF)
            for j, target in enumerate(targets):
                target[slot, pl.ds(at, tile), :] = got[:, j * LANES : (j + 1) * LANES]
            return carry

        lax.fori_loop(0, source.shape[0] // tile, step, 0)


def first_body(parts, tile, meta, own, partner, *rest):
    held, sem = rest[-2:]
    copy = pltpu.make_async_copy(own, held, sem)
    copy.start()
    weights, (target, panel) = rest[:parts], rest[parts:-2]
    rows = weights[0].shape[0]
    for k in range(parts):
        start = pl.multiple_of((meta[0] ^ k) * rows, rows)
        panel[pl.ds(start, rows), :] = weights[k][...]
    for slot, source in ((1, partner), (0, held)):
        if slot == 0:
            copy.wait()

        def step(i, carry, slot=slot, source=source):
            at = pl.multiple_of(i * tile, tile)
            got = dot(source[pl.ds(at, tile), :], panel[...], 1, 0).astype(BF)
            target[slot, pl.ds(at, tile), :] = got
            return carry

        lax.fori_loop(0, source.shape[0] // tile, step, 0)


def select_lanes(a, b):
    lane = lax.broadcasted_iota(jnp.int32, a.shape, 1)
    return jnp.where(lane < LANES // 2, a, b)


def conv_body(hops, tile, pair, meta, amounts, *rest):
    sources, rest = rest[: hops + 1], rest[hops + 1 :]
    upstream, kernel, gated, acts, late, tap_one, series = rest
    half = sources[0].shape[1]
    core, alive = meta[2], meta[3]
    late_a, late_b = amounts[2 * pair], amounts[2 * pair + 1]
    for n in range(hops + 1):
        for h in range(2):
            series[(2 * (hops - n) + h) * half : (2 * (hops - n) + h + 1) * half, :] = (
                sources[n][h ^ core].astype(F32)
            )
    per_half = half // tile

    def step(i, carry):
        slot = (i // per_half) ^ core
        row = pl.multiple_of((i % per_half) * tile, tile)
        start = 2 * hops * half + i * tile
        before = select_lanes(
            series[pl.ds(start - late_a, tile), :], series[pl.ds(start - late_b, tile), :]
        ).astype(BF)
        late[slot, pl.ds(row, tile), :] = before
        stacked = jnp.concatenate([sources[0][slot, pl.ds(row, tile), :], before], axis=1)
        pre = dot(stacked, kernel[...], 1, 0)
        tanh_act = jnp.tanh(pre[:, :LANES])
        sig_act = jax.nn.sigmoid(pre[:, LANES:])
        moment = i * tile + lax.broadcasted_iota(jnp.int32, tanh_act.shape, 0)
        mask = (moment < alive).astype(F32)
        gated[slot, pl.ds(row, tile), :] = (tanh_act * sig_act * mask).astype(BF)
        masked = upstream[slot, pl.ds(row, tile), :].astype(F32) * mask
        grad_filter = masked * sig_act * (1.0 - tanh_act * tanh_act)
        grad_gate = masked * tanh_act * sig_act * (1.0 - sig_act)
        both = jnp.concatenate([grad_filter.astype(BF), grad_gate.astype(BF)], axis=1)
        acts[slot, pl.ds(row, tile), :] = both
        tap_one[slot, pl.ds(row, tile), :] = dot(both, kernel[LANES:, :], 1, 1).astype(BF)
        return carry

    lax.fori_loop(0, 2 * per_half, step, 0)


def taps_grad_body(tile, own, late, acts, kernel, tap_zero, grad_kernel, total):
    total[...] = jnp.zeros_like(total)
    for slot in range(2):

        def step(i, carry, slot=slot):
            row = pl.multiple_of(i * tile, tile)
            both = acts[slot, pl.ds(row, tile), :]
            stacked = jnp.concatenate(
                [own[slot, pl.ds(row, tile), :], late[slot, pl.ds(row, tile), :]], axis=1
            )
            total[...] += dot(stacked, both, 0, 0)
            tap_zero[slot, pl.ds(row, tile), :] = dot(both, kernel[:LANES, :], 1, 1)
            return carry

        lax.fori_loop(0, own.shape[1] // tile, step, 0)
    width = LANES // 2
    for tap in range(2):
        for g in range(2):
            top = tap * LANES + g * width
            left = total[top : top + width, :LANES]
            right = total[top : top + width, LANES:]
            if g == 0:
                right = pltpu.roll(right, width, 1)
            else:
                left = pltpu.roll(left, width, 1)
            grad_kernel[tap, g * width : (g + 1) * width, :] = select_lanes(left, right)


def mixed_body(hops, tile, pair, meta, amounts, tap_zero, *rest):
    sources, (own, partner, series) = rest[: hops + 1], rest[hops + 1 :]
    half = tap_zero.shape[1]
    core = meta[2]
    early_a, early_b = amounts[2 * pair], amounts[2 * pair + 1]
    for n in range(hops + 1):
        for h in range(2):
            series[(2 * n + h) * half : (2 * n + h + 1) * half, :] = sources[n][h ^ core].astype(
                F32
            )
    for slot, target in ((0, own), (1, partner)):

        def step(i, carry, slot=slot, target=target):
            row = pl.multiple_of(i * tile, tile)
            start = (slot ^ core) * half + row
            early = select_lanes(
                series[pl.ds(start + early_a, tile), :], series[pl.ds(start + early_b, tile), :]
            )
            target[pl.ds(row, tile), :] = (tap_zero[slot, pl.ds(row, tile), :] + early).astype(BF)
            return carry

        lax.fori_loop(0, half // tile, step, 0)


def outer_body(chunks, parts, tile, split, taps, meta, *rest):
    count = chunks * (2 if split else 1)
    lefts, rest = rest[:count], rest[count:]
    rights, rest = rest[:2], rest[2:]
    kernels, outs, total = rest[: -1 - parts - split], rest[-1 - parts - split : -1], rest[-1]
    total[...] = jnp.zeros_like(total)
    for slot in range(2):

        def step(i, carry, slot=slot):
            at = pl.multiple_of(i * tile, tile)
            if split:
                left = [lefts[2 * j + slot][pl.ds(at, tile), :] for j in range(chunks)]
            else:
                left = [lefts[j][slot, pl.ds(at, tile), :] for j in range(chunks)]
            left = jnp.concatenate(left, axis=1)
            if split and slot == 1:
                outs[parts][pl.ds(at, tile), :] = left
            total[...] += dot(left, rights[slot][pl.ds(at, tile), :], 0, 0)
            return carry

        lax.fori_loop(0, rights[slot].shape[0] // tile, step, 0)
    columns = outs[0].shape[1]
    for k in range(parts):
        if split:
            start = pl.multiple_of((meta[0] ^ k) * columns, columns)
            outs[k][...] = total[:, pl.ds(start, columns)].astype(outs[k].dtype)
            continue
        rows = total.shape[0] // parts
        start = pl.multiple_of((meta[0] ^ k) * rows, rows)
        outs[k][:rows, :] = total[pl.ds(start, rows), :].astype(outs[k].dtype)
        few = taps // parts
        spot = 0
        for kernel in kernels:
            for low in range(0, LANES, taps):
                for tap in range(2):
                    start = pl.multiple_of(low + (meta[0] ^ k) * few, 8)
                    top, left = rows + spot // columns * few, spot % columns
                    outs[k][top : top + few, left : left + LANES] = kernel[
                        tap, pl.ds(start, few), :
                    ].astype(outs[k].dtype)
                    spot += LANES


def signal_body(tile, base, *rest):
    target, lanes = rest[-1], rest[-2].shape[1] // 2
    low = 0 if target.dtype == F32 else lanes
    side, side_far = (x[:, low : low + lanes] for x in rest[-3:-1])
    mixes, other = rest[:-4], rest[-4]

    def step(i, carry):
        at = pl.multiple_of(i * tile, tile)
        mix = jnp.concatenate([x[pl.ds(at, tile), :] for x in mixes], axis=1)
        acc = base[pl.ds(at, tile), :].astype(F32) + dot(mix, side, 1, 1)
        acc = acc + dot(other[pl.ds(at, tile), :], side_far, 1, 1)
        target[pl.ds(at, tile), :] = acc.astype(target.dtype)
        return carry

    lax.fori_loop(0, base.shape[0] // tile, step, 0)


def tree(values):
    while len(values) > 1:
        values = [values[i] + values[i + 1] for i in range(0, len(values), 2)]
    return values[0]


def split_body(count, parts, meta, *rest):
    ins, outs, total = rest[:count], rest[count:-1], rest[-1]
    total[...] = tree([x[...].astype(F32) for x in ins])
    rows = outs[0].shape[0]
    for k in range(parts):
        at = pl.multiple_of((meta[1] ^ k) * rows, rows)
        outs[k][...] = total[pl.ds(at, rows), :].astype(outs[k].dtype)


def gather_body(count, chips, few, meta, *rest):
    first, second = rest[:count], rest[count : 2 * count]
    outs, (sum_one, sum_two) = rest[2 * count : -2], rest[-2:]
    sum_one[...] = tree([x[...].astype(F32) for x in first])
    sum_two[...] = tree([x[...].astype(F32) for x in second])
    width, wide = sum_one.shape[1], sum_two.shape[1]
    one = sum_one.shape[0] // chips
    flat = sum_two.shape[0] - 2 * LANES * chips * few // wide
    two = flat // chips
    for k in range(chips):
        at, kind = meta[1] ^ k, outs[k].dtype
        outs[k][:one, :] = sum_one[pl.ds(pl.multiple_of(at * one, 8), one), :].astype(kind)
        block = sum_two[pl.ds(pl.multiple_of(at * two, 8), two), :].astype(kind)
        top = one
        for n in range(wide // width):
            outs[k][top : top + two, :] = block[:, n * width : (n + 1) * width]
            top += two
        each = wide // (2 * LANES)
        row = pl.multiple_of(flat + at // each * few, 8)
        lane = pl.multiple_of(at % each * (2 * LANES), 2 * LANES)
        block = sum_two[pl.ds(row, few), pl.ds(lane, 2 * LANES)].astype(kind)
        for n in range(2 * LANES // width):
            outs[k][top : top + few, :] = block[:, n * width : (n + 1) * width]
            top += few


def divide_body(count, *rest):
    got = tree([x[...].astype(F32) for x in rest[:count]]).astype(BF)
    rows = rest[count].shape[0]
    rest[count][...] = got[:rows, :]
    rest[count + 1][...] = got[rows:, :]


def sum_body(count, factor, *rest):
    got = tree([x[...].astype(F32) for x in rest[:count]])
    rest[count][...] = (got if factor is None else got * factor).astype(rest[count].dtype)


def pack_body(count, meta, *rest):
    out = rest[-1]
    rows = rest[0].shape[0]
    for k in range(count):
        out[meta[1] ^ k, :rows, :] = rest[k][...]
        out[meta[1] ^ k, rows:, :] = rest[count + k][...]


def share_body(parts, skip, meta, whole, out):
    piece = whole.shape[1] // (2 * parts)
    got = []
    for f in range(skip // piece, parts):
        both = whole[:, 2 * f * piece : 2 * (f + 1) * piece]
        got.append(jnp.where(meta[2] == 0, both[:, :piece], both[:, piece:]))
    out[...] = jnp.concatenate(got, axis=1)


def taps_body(chips, groups, meta, *rest):
    blocks, amounts, outs = rest[:chips], rest[chips], rest[chips + 1 :]
    rows = blocks[0].shape[0] - NOTE
    width = LANES // 2
    for out in outs:
        out[...] = jnp.zeros_like(out)
    for k in range(chips):
        at = meta[1] ^ k
        notes = blocks[k][rows:, :].astype(F32)
        for n in range(groups):
            group = at * groups + n
            both = notes[2 * n : 2 * n + 1, :] * 64.0 + notes[2 * n + 1 : 2 * n + 2, :]
            amounts[group] = jnp.max(both).astype(jnp.int32)
            for spot in range(2 * len(outs)):

                @pl.when(group == spot)
                def _(k=k, n=n, spot=spot):
                    out, g = outs[spot // 2], spot % 2
                    for tap in range(2):
                        top = tap * LANES + g * width
                        low = tap * rows // 2 + n * width
                        block = blocks[k][low : low + width, :].astype(F32)
                        lane = lax.broadcasted_iota(jnp.int32, block.shape, 1)
                        here = (lane < width) == (g == 0)
                        other = pltpu.roll(block, width, 1)
                        left, right = (block, other) if g == 0 else (other, block)
                        zero = jnp.zeros_like(block)
                        out[top : top + width, :LANES] = jnp.where(here, left, zero).astype(BF)
                        out[top : top + width, LANES:] = jnp.where(here, right, zero).astype(BF)


def local_step(signal, cotangent, w_in, w_conv, w_out, dilation, lengths):
    record, upstream = signal[0], cotangent[0]
    samples, channels = record.shape
    seq_size, fsdp_size = lax.axis_size("seq"), lax.axis_size("fsdp")
    chips = seq_size // 2
    seq_at, fsdp_at = lax.axis_index("seq"), lax.axis_index("fsdp")
    core, chip = seq_at % 2, seq_at // 2
    factor = 1.0 / math.sqrt(samples * seq_size * fsdp_size)
    block = 2 * samples
    hops = -(-MAX_DILATION // block)
    share = channels // 2
    piece = share // fsdp_size
    conv_chans = w_conv.shape[1]
    local_groups = dilation.shape[0]
    width = conv_chans // local_groups
    assert 2 * width == LANES and chips == fsdp_size and piece == conv_chans
    chunks = share // LANES

    def to_partner(x):
        return lax.ppermute(x, "seq", [(i, i ^ 1) for i in range(seq_size)])

    def from_fsdp(blocks):
        got = [blocks[0]]
        for k in range(1, fsdp_size):
            pairs = [(i, i ^ k) for i in range(fsdp_size)]
            got.append(lax.ppermute(blocks[k], "fsdp", pairs))
        return got

    def from_chips(blocks):
        got = [blocks[0]]
        for k in range(1, chips):
            pairs = [(i, i ^ (2 * k)) for i in range(seq_size)]
            got.append(lax.ppermute(blocks[k], "seq", pairs))
        return got

    def up(x, hop):
        return lax.ppermute(x, "seq", [(i, i + 2) for i in range(2 * (hop - 1), seq_size - 2)])

    def down(x, hop):
        return lax.ppermute(x, "seq", [(i + 2, i) for i in range(seq_size - 2 * hop)])

    where = jnp.stack([fsdp_at, chip, core, lengths[0] - chip * block]).astype(jnp.int32)
    wides = [share // 2, share // 2]
    lead_share = jnp.concatenate(
        [
            lax.dynamic_slice_in_dim(w_in, (2 * f + core) * piece, piece, 1)
            for f in range(LANES // piece)
        ],
        axis=1,
    )
    (rest_share,) = call(
        functools.partial(share_body, fsdp_size, LANES),
        [shape((w_in.shape[0], share - LANES), BF)],
        [where, w_in],
    )
    in_shares = [lead_share, rest_share]
    out_share = lax.dynamic_index_in_dim(
        w_out.reshape(2, piece, channels), core, 0, keepdims=False
    )
    record_far = to_partner(record)
    in_parts = [from_fsdp([x] * fsdp_size) for x in in_shares]
    upstream_far = to_partner(upstream)
    out_parts = from_fsdp([out_share] * fsdp_size)
    noted = jnp.concatenate([dilation // 64, dilation % 64]).reshape(2, -1).T.reshape(-1, 1)
    noted = jnp.pad(jnp.broadcast_to(noted, (2 * local_groups, LANES)), ((0, NOTE - 2 * local_groups), (0, 0)))
    noted = jnp.concatenate([w_conv.reshape(-1, LANES), noted.astype(BF)])
    conv_parts = from_chips([noted] * chips)
    taps = call(
        functools.partial(taps_body, chips, local_groups),
        [shape((2 * chunks,), jnp.int32)] + [shape((2 * LANES, 2 * LANES), BF)] * chunks,
        [where] + conv_parts,
        small=1,
    )
    amounts, kernels = taps[0], taps[1:]

    series = shape((2, samples, LANES), BF)
    tile = min(512, samples)
    first, lead = call(
        functools.partial(first_body, fsdp_size, tile),
        [series, shape((channels, LANES), BF)],
        [where, pltpu.with_memory_space_constraint(record, pltpu.HBM), record_far] + in_parts[0],
        scratch=[pltpu.VMEM((samples, channels), BF), pltpu.SemaphoreType.DMA],
        flops=2 * block * channels * LANES,
        stay=(1,),
    )
    got = call(
        functools.partial(product_body, fsdp_size, tile, False, LANES),
        [series] * (chunks - 1) + [shape((channels, share), BF)],
        [where, record, record_far] + in_parts[1] + [lead],
        flops=2 * block * channels * (share - LANES),
    )
    projected, panel = (first,) + got[:-1], got[-1]
    grad_gated = call(
        functools.partial(product_body, fsdp_size, tile, True, 0),
        [series] * chunks,
        [where, upstream, upstream_far] + out_parts,
        scratch=[pltpu.VMEM((share, channels), BF)],
        flops=2 * block * channels * share,
    )
    panel_far = to_partner(panel)

    tile = min(256, samples)
    gated, own_mixed, far_mixed, kernel_grads = [], [], [], []
    long = pltpu.VMEM((2 * (hops + 1) * samples, LANES), F32)
    for j in range(chunks):
        chain = [projected[j]]
        for hop in range(1, hops + 1):
            chain.append(up(chain[-1], hop))
        out, acts, late, tap_one = call(
            functools.partial(conv_body, hops, tile, j),
            [series, shape((2, samples, 2 * LANES), BF), series, series],
            [where, amounts] + chain + [grad_gated[j], kernels[j]],
            scratch=[long],
            flops=4 * block * 4 * LANES * LANES,
            scalars=2,
        )
        tap_zero, grad_kernel = call(
            functools.partial(taps_grad_body, 512 if samples % 512 == 0 else samples),
            [shape((2, samples, LANES), F32), shape((2, LANES, LANES), F32)],
            [projected[j], late, acts, kernels[j]],
            scratch=[pltpu.VMEM((2 * LANES, 2 * LANES), F32)],
            flops=4 * block * 4 * LANES * LANES,
            scalars=0,
        )
        gated.append(out)
        kernel_grads.append(grad_kernel)
        back = [tap_one]
        for hop in range(1, hops + 1):
            back.append(down(back[-1], hop))
        own, other = call(
            functools.partial(mixed_body, hops, tile, j),
            [shape((samples, LANES), BF)] * 2,
            [where, amounts, tap_zero] + back,
            scratch=[long],
            scalars=2,
        )
        own_mixed.append(own)
        far_mixed.append(other)

    tile = min(512, samples)

    few = conv_chans // fsdp_size

    def outer(lefts, rights, split):
        count = len(lefts) // 2 if split else len(lefts)
        rows, columns = LANES * count, channels
        more = [] if split else kernel_grads
        tall = piece + 2 * LANES * chips * few // channels
        one = (rows, columns // fsdp_size) if split else (tall, columns)
        return call(
            functools.partial(outer_body, count, fsdp_size, tile, split, conv_chans),
            [shape(one, F32)]
            + [shape(one, BF)] * (fsdp_size - 1)
            + ([shape((samples, rows), BF)] if split else []),
            [where] + list(lefts) + list(rights) + more,
            scratch=[pltpu.VMEM((rows, columns), F32)],
            flops=2 * block * rows * columns,
        )

    mixed_in, flats = [], []
    for pick in (range(chunks // 2), range(chunks // 2, chunks)):
        sides = []
        for j in pick:
            sides += [own_mixed[j], far_mixed[j]]
        got = outer(sides, (record, record_far), True)
        mixed_in.append(to_partner(got[-1]))
        flats.append(from_fsdp(got[:fsdp_size]))
    got = outer(gated, (upstream, upstream_far), False)
    flat_out = from_fsdp(got)

    own_rows = channels // fsdp_size
    in_part, out_part = wides[0] // chips, piece // chips
    panel_rows = in_part + out_part * (channels // own_rows)
    kernel_rows = 2 * LANES * few // own_rows
    whole = (panel_rows + kernel_rows, own_rows)
    cut = call(
        functools.partial(gather_body, fsdp_size, chips, few),
        [shape(whole, F32)] + [shape(whole, BF)] * (chips - 1),
        [where] + flats[0] + flat_out,
        scratch=[pltpu.VMEM((wides[0], own_rows), F32), pltpu.VMEM(flat_out[0].shape, F32)],
    )
    mine, mine_kernel = call(
        functools.partial(divide_body, chips),
        [shape((panel_rows, own_rows), BF), shape((kernel_rows, own_rows), BF)],
        from_chips(cut),
        scalars=0,
    )
    kernel_parts = from_fsdp([mine_kernel] * fsdp_size)
    gathered = from_chips([mine] * chips)

    last = (wides[1] // chips, own_rows)
    cut = call(
        functools.partial(split_body, fsdp_size, chips),
        [shape(last, F32)] + [shape(last, BF)] * (chips - 1),
        [where] + flats[1],
        scratch=[pltpu.VMEM((wides[1], own_rows), F32)],
    )
    (mine,) = call(
        functools.partial(sum_body, chips, None), [shape(last, BF)], from_chips(cut), scalars=0
    )
    gathered += from_chips([mine] * chips)
    (packed,) = call(
        functools.partial(pack_body, chips),
        [shape((chips, panel_rows + last[0], own_rows), BF)],
        [where] + gathered,
    )
    finals = [packed, to_partner(packed)]

    tile = min(256, samples)

    total = upstream
    for n in range(2):
        (total,) = call(
            functools.partial(signal_body, tile),
            [shape((samples, channels), BF if n else F32)],
            [total] + own_mixed[n * chunks // 2 :][: chunks // 2] + [mixed_in[n], panel, panel_far],
            scalars=0,
            flops=samples * channels * channels,
        )
    grad_signal = total

    def finish_body(meta, *rest):
        packs, parts = rest[:2], rest[2 : 2 + fsdp_size]
        grad_in, grad_out, grad_conv, turned = rest[2 + fsdp_size :]
        core_at = meta[2]
        for side in range(2):
            first = packs[side][...].astype(F32) * factor
            for p in range(chips):
                at = pl.multiple_of((side ^ core_at) * piece + p * out_part, 8)
                for n in range(channels // own_rows):
                    top = in_part + n * out_part
                    grad_out[pl.ds(at, out_part), n * own_rows : (n + 1) * own_rows] = first[
                        p, top : top + out_part, :
                    ]
                at = p * in_part
                turned[side ^ core_at, at : at + in_part, :] = first[p, :in_part, :]
                at, rows = wides[0] + p * last[0], last[0]
                turned[side ^ core_at, at : at + rows, :] = first[p, panel_rows:, :]
        for f in range(fsdp_size):
            pair = [turned[c, f * piece : (f + 1) * piece, :] for c in range(2)]
            grad_in[:, 2 * f * piece : 2 * (f + 1) * piece] = jnp.concatenate(pair, axis=0).T
        for k, x in enumerate(parts):
            total = x[...].astype(F32) * factor
            at = pl.multiple_of((meta[0] ^ k) * few, 8)
            for tap in range(2):
                left, top = (tap * LANES) % own_rows, (tap * LANES) // own_rows * few
                grad_conv[tap, pl.ds(at, few), :] = total[top : top + few, left : left + LANES]

    grad_in, grad_out, grad_conv = call(
        finish_body,
        [shape((own_rows, channels), F32)] * 2 + [shape((2, conv_chans, LANES), F32)],
        [where] + finals + kernel_parts,
        scratch=[pltpu.VMEM((2, share, own_rows), F32)],
    )
    return (grad_signal[None], grad_in, grad_out, grad_conv)


def solution(mesh):
    placed = (
        P("fsdp", "seq", None),
        P("fsdp", "seq", None),
        P("fsdp", None),
        P(None, "seq", None),
        P("fsdp", None),
        P("seq"),
        P("fsdp"),
    )
    return jax.shard_map(
        local_step,
        mesh=mesh,
        in_specs=placed,
        out_specs=(P("fsdp", "seq", None), P("fsdp", None), P("fsdp", None), P(None, "seq", None)),
        check_vma=False,
    )
```
